512 devices in a mesh: blk: 8 (over z_lo, core), owner: 64 (over z_hi, x, y).
Axes of the slice: x: 4, y: 8, z: 8 (z_hi: 2, z_lo: 4; z = z_hi * 4 + z_lo), core: 2. Of those that a mesh axis runs over, the one named last changes fastest.
Arguments:
- tokens: bfloat16 [2048, 32, 1024], P(('owner', 'blk')), may hold values from -6 to 6
- w_qkv: bfloat16 [1024, 3, 1024], P(None, None, 'blk'), may hold values from -0.1875 to 0.1875
- w_out: bfloat16 [1024, 1024], P('blk'), may hold values from -0.5625 to 0.5625
- b_out: bfloat16 [1024], replicated, may hold values from -3 to 3
- gain1: bfloat16 [1024], replicated, may hold values from 0.5 to 1.5
- shift1: bfloat16 [1024], replicated, may hold values from -2 to 2
- w_up: bfloat16 [1024, 4096], P(None, 'blk'), may hold values from -0.1875 to 0.1875
- b_up: bfloat16 [4096], P('blk'), may hold values from -3 to 3
- w_down: bfloat16 [4096, 1024], P('blk'), may hold values from -0.09375 to 0.09375
- b_down: bfloat16 [1024], replicated, may hold values from -3 to 3
- gain2: bfloat16 [1024], replicated, may hold values from 0.5 to 1.5
- shift2: bfloat16 [1024], replicated, may hold values from -2 to 2
- root_cache: bfloat16 [2, 4, 1024, 1024], P(None, None, 'owner', 'blk'), may hold values from -90 to 90
- node_cache: bfloat16 [2, 128, 384, 1024], P(None, 'owner', None, 'blk'), may hold values from -90 to 90
- root_len: int32 [4], replicated, may hold values from 128 to 1024
- node_len: int32 [128], replicated, may hold values from 48 to 384
- node_parent: int32 [128], replicated, may hold values from 0 to 31, as said below
- node_place: int32 [128], replicated, may hold values from 0 to 127, as said below
- req_leaf: int32 [2048], P('owner'), may hold values from 32 to 127, as said below
Outputs:
- result: bfloat16 [2048, 32, 1024], P(('owner', 'blk'))
- new_caches: bfloat16 [2, 2048, 32, 1024], P(None, 'owner', None, 'blk')
The draws below stay inside these ranges and needn't reach their ends.
Inputs may be any that keep to these rules, and one draw needn't show every extreme that they name: `node_parent`: entries below 32 are branch nodes and name their tenant; each other entry is a leaf and names its branch node; every branch node has exactly three leaves. `node_place`: a permutation of the pool slots; slot s lies on owner s // 2. `req_leaf`: always a leaf; the requests of one owner index lie below different branch nodes.
All inputs are finite; a program needn't handle non-finite values.
Results may differ from the reference program's by a relative error of at most 0.02.
Values may be sent and summed in bfloat16 or wider, within the bound.
No kernel may reach another device: no remote copies, remote signals or barrier semaphores. Data moves between devices by JAX's collectives and lax.ppermute only.
A program may use at most 128 MiB of HBM per device.

```python
import jax
import jax.numpy as jnp
from jax import lax

D = 1024
HEADS = 16
HD = 64
FF = 4096
SUF = 32
NODE_MAX = 384
ROOT_MAX = 1024
TENANTS = 4
NODES = 128
REQS = 2048
N_BLK = 8
N_OWNER = 64


def tree_layout(key):
    branches = NODES // 4
    leaf_count = NODES - branches
    branch_tenant = jax.random.randint(jax.random.fold_in(key, 101), (branches,), 0, TENANTS)
    order = jax.random.permutation(jax.random.fold_in(key, 102), leaf_count)
    leaf_parent = order % branches
    parent = jnp.concatenate([branch_tenant, leaf_parent]).astype(jnp.int32)
    place = jax.random.permutation(jax.random.fold_in(key, 103), NODES).astype(jnp.int32)
    inverse = jnp.argsort(order)
    group_size = REQS // N_OWNER
    group_keys = jax.random.split(jax.random.fold_in(key, 104), N_OWNER)

    def pick_branches(group_key):
        return jax.random.permutation(group_key, branches)[:group_size]
    chosen = jax.vmap(pick_branches)(group_keys)
    child = jax.random.randint(jax.random.fold_in(key, 105), (N_OWNER, group_size), 0, 3)
    leaves = branches + inverse[chosen + branches * child]
    return (parent, place, leaves.reshape(REQS).astype(jnp.int32))


def draw_node_parent(key, part):
    return tree_layout(key)[0]


def draw_node_place(key, part):
    return tree_layout(key)[1]


def draw_req_leaf(key, part):
    return tree_layout(key)[2]


def draw_node_len(key, part):
    base = jax.random.randint(jax.random.fold_in(key, 201), (NODES,), NODE_MAX // 8, NODE_MAX + 1)
    chosen = jax.random.randint(jax.random.fold_in(key, 202), (), 0, NODES)
    return jnp.where(jnp.arange(NODES) == chosen, NODE_MAX, base).astype(jnp.int32)


def draw_root_len(key, part):
    base = jax.random.randint(jax.random.fold_in(key, 301), (TENANTS,), ROOT_MAX // 8, ROOT_MAX + 1)
    chosen = jax.random.randint(jax.random.fold_in(key, 302), (), 0, TENANTS)
    return jnp.where(jnp.arange(TENANTS) == chosen, ROOT_MAX, base).astype(jnp.int32)


def cache_values(key, lead, rows):
    shape = (2, lead, rows, D)
    return jax.random.normal(jax.random.fold_in(key, 403), shape, jnp.float32)


def draw_node_cache(key, part):
    return cache_values(key, NODES, NODE_MAX).astype(jnp.bfloat16)


def draw_root_cache(key, part):
    return cache_values(key, TENANTS, ROOT_MAX).astype(jnp.bfloat16)


def raised(values, own_key, source, target, shards_of, factor):
    def block_of(dim):
        return (jnp.arange(values.shape[dim]) // (values.shape[dim] // shards_of)).reshape((-1,) + (1,) * (values.ndim - 1 - dim))

    first = jax.random.permutation(own_key, shards_of)[block_of(target)]
    second = (block_of(target) + shards_of // 2) % shards_of
    return jnp.where((block_of(source) == first) | (block_of(source) == second), factor * values, values)


def block_scale(own_key, extent, cuts, smallest, largest):
    level, own = 1.0, jax.random.fold_in(own_key, 6)
    for dim, parts in cuts:
        steps = jnp.exp(jax.random.uniform(jax.random.fold_in(own, dim), (parts,), jnp.float32, smallest / len(cuts), largest / len(cuts)))
        level = level * jnp.repeat(steps, extent[dim] // parts).reshape([-1 if axis == dim else 1 for axis in range(len(extent))])
    return level


def noise(own_key, dims, scale, most, shards=(), kind=jnp.bfloat16):
    loudness = block_scale(own_key, dims, shards, -0.22, 0.18) if shards else 1.0
    entries = jax.random.normal(own_key, dims, jnp.float32) * scale * loudness
    return jnp.minimum(jnp.maximum(entries, -most), most).astype(kind)


def noise_with(own_key, extent, scale, reach, cuts, heavy, kind=jnp.bfloat16):
    values = scale * jax.random.normal(own_key, extent, jnp.float32)
    if cuts:
        values = values * block_scale(own_key, extent, cuts, -0.22, 0.18)
    return jnp.clip(raised(values, jax.random.fold_in(own_key, 3), *heavy), -reach, reach).astype(kind)


def setup_inputs(seed: int = 0) -> dict:
    streams_of = jax.random.split(jax.random.key(seed), 20)
    tokens = noise(streams_of[0], (REQS, SUF, D), 1.0, 6.0, ((0, 512),))
    w_qkv = noise(streams_of[1], (D, 3, D), D ** -0.5, 0.1875, ((2, 8),))
    w_out = noise_with(streams_of[2], (D, D), (3.0 / D ** 0.5), 0.5625, ((0, 8),), (0, 1, 8, 2.0))
    b_out = noise(streams_of[3], (D,), 0.5, 3.0)
    gain1 = jnp.clip(1.0 + 0.1 * jax.random.normal(streams_of[4], (D,), jnp.float32), 0.5, 1.5).astype(jnp.bfloat16)
    shift1 = noise(streams_of[5], (D,), 0.3, 2.0)
    w_up = noise(streams_of[6], (D, FF), D ** -0.5, 0.1875, ((1, 8),))
    b_up = noise(streams_of[7], (FF,), 0.5, 3.0, ((0, 8),))
    w_down = noise(streams_of[8], (FF, D), FF ** -0.5, 0.09375, ((0, 8),))
    b_down = noise(streams_of[9], (D,), 0.5, 3.0)
    gain2 = jnp.clip(1.0 + 0.1 * jax.random.normal(streams_of[10], (D,), jnp.float32), 0.5, 1.5).astype(jnp.bfloat16)
    shift2 = noise(streams_of[11], (D,), 0.3, 2.0)
    root_cache = draw_root_cache(jax.random.fold_in(streams_of[19], 71), 0)
    node_cache = draw_node_cache(jax.random.fold_in(streams_of[19], 71), 0)
    root_len = draw_root_len(jax.random.fold_in(streams_of[19], 71), 0)
    node_len = draw_node_len(jax.random.fold_in(streams_of[19], 71), 0)
    node_parent = draw_node_parent(jax.random.fold_in(streams_of[19], 71), 0)
    node_place = draw_node_place(jax.random.fold_in(streams_of[19], 71), 0)
    req_leaf = draw_req_leaf(jax.random.fold_in(streams_of[19], 71), 0)
    return {"tokens": tokens, "w_qkv": w_qkv, "w_out": w_out, "b_out": b_out, "gain1": gain1, "shift1": shift1, "w_up": w_up, "b_up": b_up, "w_down": w_down, "b_down": b_down, "gain2": gain2, "shift2": shift2, "root_cache": root_cache, "node_cache": node_cache, "root_len": root_len, "node_len": node_len, "node_parent": node_parent, "node_place": node_place, "req_leaf": req_leaf}


norm_eps = 1e-05
masked_score = -1e+30

def layer_norm(values, gain, shift):
    center = values - lax.optimization_barrier(jnp.mean(values, axis=-1, keepdims=True))
    spread = lax.optimization_barrier(jnp.mean(center * center, axis=-1, keepdims=True))
    return center * lax.rsqrt(spread + norm_eps) * gain.astype(jnp.float32) + shift.astype(jnp.float32)

def attend_set(queries, key_rows, value_rows, in_range):
    scores = jnp.einsum('rshe,rnhe->rshn', queries.astype(jnp.float32), key_rows.astype(jnp.float32)) * HD ** (-0.5)
    keep = in_range[:, None, None, :]
    scores = jnp.where(keep, scores, masked_score)
    peak = lax.optimization_barrier(jnp.max(scores, axis=-1))
    weights = jnp.where(keep, jnp.exp(scores - peak[..., None]), 0.0)
    weight_sum = lax.optimization_barrier(jnp.sum(weights, axis=-1))
    rounded = lax.optimization_barrier(weights.astype(jnp.bfloat16)).astype(jnp.float32)
    mixed = jnp.einsum('rshn,rnhe->rshe', rounded, value_rows.astype(jnp.float32)) / weight_sum[..., None]
    return (mixed, peak + jnp.log(weight_sum))

def reference(tokens, w_qkv, w_out, b_out, gain1, shift1, w_up, b_up, w_down, b_down, gain2, shift2, root_cache, node_cache, root_len, node_len, node_parent, node_place, req_leaf):
    block_cols = D // N_BLK
    block_units = FF // N_BLK
    group_size = REQS // N_OWNER
    tok_count = group_size * SUF
    flat_qkv = w_qkv.reshape(D, 3 * D)
    out_blocks = w_out.astype(jnp.float32).reshape(N_BLK, block_cols, D)
    down_blocks = w_down.astype(jnp.float32).reshape(N_BLK, block_units, D)

    def one_group(group_index):
        first = group_index * group_size
        rows_in = lax.dynamic_slice_in_dim(tokens, first, group_size, 0)
        leaves = lax.dynamic_slice_in_dim(req_leaf, first, group_size, 0)
        branch = node_parent[leaves]
        tenant = node_parent[branch]
        projected = jnp.dot(rows_in.reshape(tok_count, D), flat_qkv, preferred_element_type=jnp.float32)
        projected = projected.astype(jnp.bfloat16).reshape(group_size, SUF, 3, HEADS, HD)
        queries = projected[:, :, 0]
        new_keys = projected[:, :, 1]
        new_values = projected[:, :, 2]
        root_keys = root_cache[0][tenant].reshape(group_size, ROOT_MAX, HEADS, HD)
        root_values = root_cache[1][tenant].reshape(group_size, ROOT_MAX, HEADS, HD)
        root_range = jnp.arange(ROOT_MAX, dtype=jnp.int32)[None, :] < root_len[tenant][:, None]
        node_rows = jnp.arange(NODE_MAX, dtype=jnp.int32)[None, :]
        branch_slot = node_place[branch]
        leaf_slot = node_place[leaves]
        branch_keys = node_cache[0][branch_slot].reshape(group_size, NODE_MAX, HEADS, HD)
        branch_values = node_cache[1][branch_slot].reshape(group_size, NODE_MAX, HEADS, HD)
        leaf_keys = node_cache[0][leaf_slot].reshape(group_size, NODE_MAX, HEADS, HD)
        leaf_values = node_cache[1][leaf_slot].reshape(group_size, NODE_MAX, HEADS, HD)
        set_parts = [attend_set(queries, root_keys, root_values, root_range), attend_set(queries, branch_keys, branch_values, node_rows < node_len[branch][:, None]), attend_set(queries, leaf_keys, leaf_values, node_rows < node_len[leaves][:, None]), attend_set(queries, new_keys, new_values, jnp.ones((group_size, SUF), dtype=bool))]
        masses = jnp.stack([part[1] for part in set_parts])
        total = jax.nn.logsumexp(masses, axis=0)
        attn = set_parts[0][0] * jnp.exp(set_parts[0][1] - total)[..., None]
        for part in set_parts[1:]:
            attn = attn + part[0] * jnp.exp(part[1] - total)[..., None]
        attn = attn.astype(jnp.bfloat16).reshape(tok_count, D)
        head_parts = jnp.einsum('tbc,bcd->tbd', attn.reshape(tok_count, N_BLK, block_cols).astype(jnp.float32), out_blocks)
        head_parts = lax.optimization_barrier(head_parts.astype(jnp.bfloat16)).astype(jnp.float32)
        head_sum = lax.optimization_barrier(jnp.sum(head_parts, axis=1))
        first_norm = layer_norm(rows_in.reshape(tok_count, D).astype(jnp.float32) + head_sum + b_out.astype(jnp.float32), gain1, shift1).astype(jnp.bfloat16)
        hidden = jax.nn.gelu(jnp.dot(first_norm, w_up, preferred_element_type=jnp.float32) + b_up.astype(jnp.float32), approximate=False).astype(jnp.bfloat16)
        down_parts = jnp.einsum('tbf,bfd->tbd', hidden.reshape(tok_count, N_BLK, block_units).astype(jnp.float32), down_blocks)
        down_parts = lax.optimization_barrier(down_parts.astype(jnp.bfloat16)).astype(jnp.float32)
        down_sum = lax.optimization_barrier(jnp.sum(down_parts, axis=1))
        result = layer_norm(first_norm.astype(jnp.float32) + down_sum + b_down.astype(jnp.float32), gain2, shift2).astype(jnp.bfloat16)
        caches = jnp.stack([new_keys, new_values]).reshape(2, group_size, SUF, D)
        return (result.reshape(group_size, SUF, D), caches)
    results, caches = lax.map(one_group, jnp.arange(N_OWNER, dtype=jnp.int32))
    return (results.reshape(REQS, SUF, D), jnp.moveaxis(caches, 1, 0).reshape(2, REQS, SUF, D))
```

```python
import functools

import jax
import jax.numpy as jnp
from jax import lax
from jax.experimental import pallas as pl
from jax.experimental.pallas import tpu as pltpu
from jax.sharding import PartitionSpec as P

F32 = jnp.float32
BF16 = jnp.bfloat16
I32 = jnp.int32

HD = 64
LANES = 128
N_BLK = 8
NX, NY, NZ = 4, 8, 2
PEERS = NZ * NY
SLOTS = 2 * NX
CHUNK = 4
NEG = -1e30
EPS = 1e-05


def layer_norm(values, gain, shift):
    center = values - jnp.mean(values, axis=-1, keepdims=True)
    spread = jnp.mean(center * center, axis=-1, keepdims=True)
    return center * lax.rsqrt(spread + EPS) * gain.astype(F32) + shift.astype(F32)


def xor_pairs(count, bits):
    return [(i, i ^ bits) for i in range(count)]


def dot_nt(a, b):
    return lax.dot_general(a, b, (((1,), (1,)), ((), ())), preferred_element_type=F32)


def dot_nn(a, b):
    return lax.dot_general(a, b, (((1,), (0,)), ((), ())), preferred_element_type=F32)


def both_heads(q):
    lane = lax.broadcasted_iota(I32, q.shape, 1)
    zero = jnp.zeros_like(q)
    return jnp.concatenate([jnp.where(lane < HD, q, zero), jnp.where(lane < HD, zero, q)], axis=0)


def by_head(stacked):
    rows = stacked.shape[0] // 2
    lane = lax.broadcasted_iota(I32, (rows, LANES), 1)
    first = jnp.broadcast_to(stacked[:rows], (rows, LANES))
    second = jnp.broadcast_to(stacked[rows:], (rows, LANES))
    return jnp.where(lane < HD, first, second)


def route_kernel(pos, dst_b, dst_l, q_ref, out_ref):
    out_ref[...] = jnp.zeros_like(out_ref)

    def body(r, _):
        tile = q_ref[pos[r]]
        out_ref[dst_b[r]] = tile
        out_ref[dst_l[r]] = tile
        return 0

    lax.fori_loop(0, pos.shape[0], body, 0)


def route(pos, dst_b, dst_l, q):
    reqs, suf, _ = q.shape
    return pl.pallas_call(
        route_kernel,
        out_shape=jax.ShapeDtypeStruct((PEERS * SLOTS, suf, LANES), BF16),
        in_specs=[pl.BlockSpec(memory_space=pltpu.SMEM)] * 3
        + [pl.BlockSpec(memory_space=pltpu.VMEM)],
        out_specs=pl.BlockSpec(memory_space=pltpu.VMEM),
        cost_estimate=pl.CostEstimate(flops=0, bytes_accessed=3 << 20, transcendentals=0),
    )(pos, dst_b, dst_l, q)


def node_kernel(lens, q_ref, k_ref, v_ref, out_ref):
    slot = pl.program_id(0)
    peers, _, suf, _ = q_ref.shape
    group = 4
    rows = group * suf
    node_max = k_ref.shape[2]
    keys = k_ref[0, 0]
    values = v_ref[0, 0]
    keep = lax.broadcasted_iota(I32, (1, node_max), 1) < lens[slot]
    bias = jnp.where(keep, 0.0, NEG)
    lane = lax.broadcasted_iota(I32, (rows, LANES), 1) % HD

    @pl.when(slot == 0)
    def _():
        out_ref[:, SLOTS] = jnp.zeros((peers, suf, LANES), BF16)

    for g in range(peers // group):
        part = slice(g * group, (g + 1) * group)
        q = q_ref[part, slot].reshape(rows, LANES)
        scores = jnp.where(keep, dot_nt(both_heads(q), keys), NEG)
        peak = jnp.max(scores, axis=1, keepdims=True)
        weights = jnp.exp(scores - peak)
        total = jnp.sum(weights, axis=1, keepdims=True)
        mixed = by_head(dot_nn(weights.astype(BF16), values))
        out = mixed / by_head(total)
        out_ref[part, slot] = out.astype(BF16).reshape(group, suf, LANES)
        mass = by_head(peak + jnp.log(total))
        high = mass.astype(BF16)
        rest = mass - high.astype(F32)
        mid = rest.astype(BF16)
        low = (rest - mid.astype(F32)).astype(BF16)
        held = out_ref[part, SLOTS].reshape(rows, LANES)
        held = jnp.where(lane == 3 * slot, high, held)
        held = jnp.where(lane == 3 * slot + 1, mid, held)
        held = jnp.where(lane == 3 * slot + 2, low, held)
        out_ref[part, SLOTS] = held.reshape(group, suf, LANES)


def node_attention(lens, queries, caches):
    peers, slots, suf, _ = queries.shape
    node_max = caches.shape[3]
    return pl.pallas_call(
        node_kernel,
        out_shape=jax.ShapeDtypeStruct((peers, slots + 1, suf, LANES), BF16),
        grid_spec=pltpu.PrefetchScalarGridSpec(
            num_scalar_prefetch=1,
            grid=(slots,),
            in_specs=[
                pl.BlockSpec((peers, slots, suf, LANES), lambda s, n: (0, 0, 0, 0)),
                pl.BlockSpec(
                    (1, 1, pl.Squeezed(), node_max, LANES), lambda s, n: (s // 2, 0, s % 2, 0, 0)
                ),
                pl.BlockSpec(
                    (1, 1, pl.Squeezed(), node_max, LANES), lambda s, n: (s // 2, 1, s % 2, 0, 0)
                ),
            ],
            out_specs=pl.BlockSpec((peers, slots + 1, suf, LANES), lambda s, n: (0, 0, 0, 0)),
        ),
        compiler_params=pltpu.CompilerParams(vmem_limit_bytes=40 << 20),
        cost_estimate=pl.CostEstimate(
            flops=2 << 30, bytes_accessed=4 << 20, transcendentals=4 << 20
        ),
    )(lens, queries, caches, caches)


def root_kernel(
    used, members, valid, chunk_tenant, root_len, coords, q_ref, k_ref, v_ref, root_ref, out_ref, mass_ref
):
    suf = q_ref.shape[1]
    rows = CHUNK * suf
    root_rows = NY * NZ * NX * root_ref.shape[5]
    per = root_ref.shape[5]

    def body(c, _):
        tenant = chunk_tenant[c]
        where_ = [members[c * CHUNK + j] for j in range(CHUNK)]
        q = both_heads(jnp.concatenate([q_ref[w] for w in where_], axis=0))
        own_k = jnp.concatenate([k_ref[w] for w in where_], axis=0)
        own_v = jnp.concatenate([v_ref[w] for w in where_], axis=0)
        keys = root_ref[:, :, :, 0, tenant].reshape(root_rows, LANES)
        values = root_ref[:, :, :, 1, tenant].reshape(root_rows, LANES)
        n = lax.broadcasted_iota(I32, (1, root_rows), 1)
        row = n % per
        x = (n // per) % NX
        z = (n // (per * NX)) % NZ
        y = n // (per * NX * NZ)
        place = (((z ^ coords[0]) * NX + (x ^ coords[1])) * NY + y) * per + row
        scores = jnp.where(place < root_len[tenant], dot_nt(q, keys), NEG)
        own_row = (lax.broadcasted_iota(I32, (2 * rows, rows), 0) % rows) // suf
        own_col = lax.broadcasted_iota(I32, (2 * rows, rows), 1) // suf
        own = jnp.where(own_row == own_col, dot_nt(q, own_k), NEG)
        peak = jnp.maximum(
            jnp.max(scores, axis=1, keepdims=True), jnp.max(own, axis=1, keepdims=True)
        )
        weights = jnp.exp(scores - peak)
        own_weights = jnp.exp(own - peak)
        total = jnp.sum(weights, axis=1, keepdims=True) + jnp.sum(
            own_weights, axis=1, keepdims=True
        )
        mixed = dot_nn(weights.astype(BF16), values) + dot_nn(own_weights.astype(BF16), own_v)
        out = by_head(mixed) / by_head(total)
        mass = by_head(peak + jnp.log(total))
        for j in range(CHUNK):

            @pl.when(valid[c * CHUNK + j] > 0)
            def _(j=j):
                out_ref[where_[j]] = out[j * suf : (j + 1) * suf]
                mass_ref[where_[j]] = mass[j * suf : (j + 1) * suf]

        return 0

    lax.fori_loop(0, used[0], body, 0)


def root_attention(used, members, valid, chunk_tenant, root_len, coords, q, k, v, roots):
    reqs, suf, _ = q.shape
    shape = jax.ShapeDtypeStruct((reqs, suf, LANES), F32)
    vmem = pl.BlockSpec(memory_space=pltpu.VMEM)
    return pl.pallas_call(
        root_kernel,
        out_shape=(shape, shape),
        in_specs=[pl.BlockSpec(memory_space=pltpu.SMEM)] * 6 + [vmem] * 4,
        out_specs=(vmem, vmem),
        compiler_params=pltpu.CompilerParams(vmem_limit_bytes=40 << 20),
        cost_estimate=pl.CostEstimate(
            flops=4 << 30, bytes_accessed=4 << 20, transcendentals=4 << 20
        ),
    )(used, members, valid, chunk_tenant, root_len, coords, q, k, v, roots)


def merge_kernel(pos, dst_b, dst_l, back_ref, out_ref, mass_ref, send_ref, pick_ref):
    suf = out_ref.shape[1]
    reqs = out_ref.shape[0]
    per_block = reqs // N_BLK
    src = lax.broadcasted_iota(I32, (LANES, LANES), 0)
    dst = lax.broadcasted_iota(I32, (LANES, LANES), 1)
    for s in range(SLOTS):
        hit = (src // HD == dst // HD) & ((src % HD) // 3 == s)
        pick_ref[s] = jnp.where(hit, 1.0, 0.0).astype(BF16)

    def body(r, _):
        here = pos[r]
        outs = [out_ref[here]]
        masses = [mass_ref[here]]
        for table in (dst_b, dst_l):
            peer = table[r] // SLOTS
            slot = table[r] % SLOTS
            outs.append(back_ref[peer, slot].astype(F32))
            masses.append(dot_nn(back_ref[peer, SLOTS], pick_ref[slot]))
        top = jnp.maximum(jnp.maximum(masses[0], masses[1]), masses[2])
        parts = [jnp.exp(m - top) for m in masses]
        total = parts[0] + parts[1] + parts[2]
        attn = (parts[0] * outs[0] + parts[1] * outs[1] + parts[2] * outs[2]) / total
        attn = attn.astype(BF16)
        block = r // per_block
        core = block % 2
        for z in range(N_BLK // 2):
            send_ref[2 * z + core, block // 2, r % per_block] = attn
        return 0

    lax.fori_loop(0, reqs, body, 0)


def merge(pos, dst_b, dst_l, back, out, mass):
    reqs, suf, _ = out.shape
    vmem = pl.BlockSpec(memory_space=pltpu.VMEM)
    return pl.pallas_call(
        merge_kernel,
        out_shape=jax.ShapeDtypeStruct(
            (N_BLK, N_BLK // 2, reqs // N_BLK, suf, LANES), BF16
        ),
        in_specs=[pl.BlockSpec(memory_space=pltpu.SMEM)] * 3 + [vmem] * 3,
        out_specs=vmem,
        scratch_shapes=[pltpu.VMEM((SLOTS, LANES, LANES), BF16)],
        compiler_params=pltpu.CompilerParams(vmem_limit_bytes=30 << 20),
        cost_estimate=pl.CostEstimate(
            flops=1 << 27, bytes_accessed=4 << 20, transcendentals=1 << 20
        ),
    )(pos, dst_b, dst_l, back, out, mass)


def on_device(
    tokens,
    w_qkv,
    w_out,
    b_out,
    gain1,
    shift1,
    w_up,
    b_up,
    w_down,
    b_down,
    gain2,
    shift2,
    root_cache,
    node_cache,
    root_len,
    node_len,
    node_parent,
    node_place,
    req_leaf,
):
    req_dev, suf, width = tokens.shape
    cols = w_qkv.shape[2]
    own_rows = req_dev * suf
    reqs = req_leaf.shape[0]
    nodes = node_place.shape[0]
    node_max = node_cache.shape[2]
    tenants = root_cache.shape[1]
    root_per = root_cache.shape[2]
    blk = lax.axis_index("blk")
    owner = lax.axis_index("owner")
    my_z = owner // (NX * NY)
    my_x = (owner // NY) % NX
    my_y = owner % NY
    chip = blk // 2
    swap = xor_pairs(N_BLK, 1)
    n_own = N_BLK // 2

    tok = tokens.reshape(own_rows, width)
    half = [tok] + [lax.ppermute(tok, "blk", xor_pairs(N_BLK, 2 * k)) for k in range(1, n_own)]
    half = jnp.stack(half)
    other = lax.ppermute(half, "blk", swap)

    node_rows = node_cache.reshape(-1, LANES)
    root_rows = root_cache.reshape(-1, LANES)
    shard = jnp.concatenate([node_rows, root_rows], axis=0)
    n_owner = NX * NY * NZ
    shards = [shard] + [
        lax.ppermute(shard, "owner", xor_pairs(n_owner, k * NY)) for k in range(1, NX)
    ]
    caches = jnp.stack([s[: node_rows.shape[0]] for s in shards])
    caches = caches.reshape(NX, 2, 2, node_max, LANES)
    roots = jnp.stack([s[node_rows.shape[0] :] for s in shards])
    roots = jnp.stack([roots, lax.ppermute(roots, "owner", xor_pairs(n_owner, NX * NY))])
    y_groups = [[g * NY + y for y in range(NY)] for g in range(NZ * NX)]
    roots = lax.all_gather(roots, "owner", axis=0, tiled=False, axis_index_groups=y_groups)
    roots = roots.reshape(NY, NZ, NX, 2, tenants, root_per, LANES)

    w_out_all = lax.all_gather(w_out, "blk", axis=0, tiled=True)
    w_up_2 = lax.ppermute(w_up, "blk", swap)
    w_down_2 = lax.ppermute(w_down, "blk", swap)
    b_up_2 = lax.ppermute(b_up, "blk", swap)

    branch = node_parent[req_leaf]
    tenant = node_parent[branch]

    def slot_index(place):
        at = place // 2
        z, x, y = at // (NX * NY), (at // NY) % NX, at % NY
        return ((z * NY + y) * SLOTS + (x ^ my_x) * 2 + place % 2).astype(I32)

    dst_b = slot_index(node_place[branch])
    dst_l = slot_index(node_place[req_leaf])
    req_ids = jnp.arange(reqs, dtype=I32)
    rel = (req_ids // req_dev) ^ blk
    pos = ((rel % 2) * n_own + rel // 2) * req_dev + req_ids % req_dev
    local = jnp.arange(SLOTS, dtype=I32)
    local_slot = ((my_z * NX + ((local // 2) ^ my_x)) * NY + my_y) * 2 + local % 2
    lens = jnp.sum(jnp.where(local_slot[:, None] == node_place[None, :], node_len[None, :], 0), axis=1)
    same = tenant[:, None] == tenant[None, :]
    within = jnp.sum(jnp.where(same & (req_ids[None, :] < req_ids[:, None]), 1, 0), axis=1)
    tenant_ids = jnp.arange(tenants, dtype=I32)
    counts = jnp.sum(jnp.where(tenant_ids[:, None] == tenant[None, :], 1, 0), axis=1)
    chunks = (counts + CHUNK - 1) // CHUNK
    ends = jnp.sum(jnp.where(tenant_ids[None, :] <= tenant_ids[:, None], chunks[None, :], 0), axis=1)
    first = ends - chunks
    first_of = jnp.sum(jnp.where(tenant[:, None] == tenant_ids[None, :], first[None, :], 0), axis=1)
    place_in = first_of * CHUNK + within
    max_chunks = reqs // CHUNK + tenants - 1
    seats = jnp.arange(max_chunks * CHUNK, dtype=I32)
    seated = seats[:, None] == place_in[None, :]
    members = jnp.sum(jnp.where(seated, pos[None, :], 0), axis=1).astype(I32)
    valid = jnp.sum(jnp.where(seated, 1, 0), axis=1).astype(I32)
    chunk_ids = jnp.arange(max_chunks, dtype=I32)
    chunk_tenant = jnp.minimum(
        jnp.sum(jnp.where(chunk_ids[:, None] >= ends[None, :], 1, 0), axis=1), tenants - 1
    ).astype(I32)
    used = ends[-1:].astype(I32)
    coords = jnp.stack([my_z, my_x]).astype(I32)

    def project(which):
        w = w_qkv[:, which]
        out = jnp.concatenate(
            [jnp.dot(part.reshape(-1, width), w, preferred_element_type=F32) for part in (half, other)]
        )
        return out.astype(BF16).reshape(reqs, suf, cols)

    q = project(0) * jnp.asarray(HD**-0.5, BF16)
    outgoing = route(pos, dst_b, dst_l, q).reshape(PEERS, SLOTS, suf, cols)
    groups = [
        [(z * NX + x) * NY + y for z in range(NZ) for y in range(NY)] for x in range(NX)
    ]
    incoming = lax.all_to_all(
        outgoing, "owner", split_axis=0, concat_axis=0, axis_index_groups=groups, tiled=True
    )
    k_new = project(1)
    v_new = project(2)
    order = jnp.arange(N_BLK, dtype=I32) ^ blk
    order = (order % 2) * n_own + order // 2
    new_caches = jnp.stack([k_new, v_new]).reshape(2, N_BLK, req_dev, suf, cols)
    new_caches = jnp.take(new_caches, order, axis=1).reshape(2, reqs, suf, cols)

    answers = node_attention(lens, incoming, caches)
    back = lax.all_to_all(
        answers, "owner", split_axis=0, concat_axis=0, axis_index_groups=groups, tiled=True
    )
    out, mass = root_attention(
        used, members, valid, chunk_tenant, root_len, coords, q, k_new, v_new, roots
    )
    send = merge(pos, dst_b, dst_l, back, out, mass)
    half_rows = n_own * own_rows
    attn = lax.all_to_all(
        send.reshape(N_BLK, half_rows, cols), "blk", split_axis=0, concat_axis=0, tiled=True
    )
    attn = jnp.swapaxes(attn, 0, 1).reshape(half_rows, N_BLK * cols)
    residual = jnp.take(half, jnp.arange(n_own, dtype=I32) ^ chip, axis=0).reshape(half_rows, width)
    first_norm = layer_norm(
        residual.astype(F32)
        + jnp.dot(attn, w_out_all, preferred_element_type=F32)
        + b_out.astype(F32),
        gain1,
        shift1,
    ).astype(BF16)

    def feed(up, bias, down):
        inner = jnp.dot(first_norm, up, preferred_element_type=F32) + bias.astype(F32)
        hidden = jax.nn.gelu(inner, approximate=False).astype(BF16)
        return jnp.dot(hidden, down, preferred_element_type=F32)

    down = feed(w_up, b_up, w_down) + feed(w_up_2, b_up_2, w_down_2)
    down = down.astype(BF16).reshape(n_own, own_rows, width)

    def own_part(of_chip):
        return lax.dynamic_index_in_dim(down, of_chip, 0, keepdims=False)

    total = own_part(chip).astype(F32)
    for k in range(1, n_own):
        total = total + lax.ppermute(own_part(chip ^ k), "blk", xor_pairs(N_BLK, 2 * k)).astype(F32)
    own_norm = lax.dynamic_slice_in_dim(first_norm, chip * own_rows, own_rows, 0)
    result = layer_norm(
        own_norm.astype(F32) + total + b_down.astype(F32), gain2, shift2
    ).astype(BF16)
    return (result.reshape(req_dev, suf, width), new_caches)


def solution(mesh):
    in_specs = (
        P(("owner", "blk"), None, None),
        P(None, None, "blk"),
        P("blk", None),
        P(),
        P(),
        P(),
        P(None, "blk"),
        P("blk"),
        P("blk", None),
        P(),
        P(),
        P(),
        P(None, None, "owner", "blk"),
        P(None, "owner", None, "blk"),
        P(),
        P(),
        P(),
        P(),
        P("owner"),
    )
    out_specs = (P(("owner", "blk"), None, None), P(None, "owner", None, "blk"))
    return jax.shard_map(
        on_device, mesh=mesh, in_specs=in_specs, out_specs=out_specs, check_vma=False
    )
```

```python
import functools

import jax
import jax.numpy as jnp
from jax import lax
from jax.experimental import pallas as pl
from jax.experimental.pallas import tpu as pltpu
from jax.sharding import PartitionSpec as P

F32 = jnp.float32
BF16 = jnp.bfloat16
I32 = jnp.int32

HD = 64
LANES = 128
N_BLK = 8
NX, NY, NZ = 4, 8, 2
PEERS = NX * NY
SLOTS = 2 * NZ
HALF = 16
CHUNK = 4
NEG = -1e30
EPS = 1e-05


def layer_norm(values, gain, shift):
    center = values - jnp.mean(values, axis=-1, keepdims=True)
    spread = jnp.mean(center * center, axis=-1, keepdims=True)
    return center * lax.rsqrt(spread + EPS) * gain.astype(F32) + shift.astype(F32)


def xor_pairs(count, bits):
    return [(i, i ^ bits) for i in range(count)]


def dot_nt(a, b):
    return lax.dot_general(a, b, (((1,), (1,)), ((), ())), preferred_element_type=F32)


def dot_nn(a, b):
    return lax.dot_general(a, b, (((1,), (0,)), ((), ())), preferred_element_type=F32)


def both_heads(q):
    lane = lax.broadcasted_iota(I32, q.shape, 1)
    zero = jnp.zeros_like(q)
    return jnp.concatenate([jnp.where(lane < HD, q, zero), jnp.where(lane < HD, zero, q)], axis=0)


def by_head(stacked):
    rows = stacked.shape[0] // 2
    lane = lax.broadcasted_iota(I32, (rows, LANES), 1)
    first = jnp.broadcast_to(stacked[:rows], (rows, LANES))
    second = jnp.broadcast_to(stacked[rows:], (rows, LANES))
    return jnp.where(lane < HD, first, second)


def route_kernel(pos, dst_b, dst_l, q_ref, out_ref):
    out_ref[...] = jnp.zeros_like(out_ref)

    def body(r, _):
        tile = q_ref[pos[r]]
        out_ref[dst_b[r]] = tile
        out_ref[dst_l[r]] = tile
        return 0

    lax.fori_loop(0, pos.shape[0], body, 0)


def route(pos, dst_b, dst_l, q):
    reqs, suf, _ = q.shape
    return pl.pallas_call(
        route_kernel,
        out_shape=jax.ShapeDtypeStruct((PEERS * SLOTS, suf, LANES), BF16),
        in_specs=[pl.BlockSpec(memory_space=pltpu.SMEM)] * 3
        + [pl.BlockSpec(memory_space=pltpu.VMEM)],
        out_specs=pl.BlockSpec(memory_space=pltpu.VMEM),
        cost_estimate=pl.CostEstimate(flops=0, bytes_accessed=3 << 20, transcendentals=0),
    )(pos, dst_b, dst_l, q)


def node_kernel(lens, q_ref, k_ref, v_ref, out_ref):
    slot = pl.program_id(0)
    peers, _, suf, _ = q_ref.shape
    group = 8
    rows = group * suf
    node_max = k_ref.shape[2]
    keys = both_heads(k_ref[0, 0])
    values = both_heads(v_ref[0, 0])
    keep = lax.broadcasted_iota(I32, (1, node_max), 1) < lens[slot]
    lane = lax.broadcasted_iota(I32, (group, HALF, LANES), 2)
    piece = lane % (HD // 2) - 3 * slot

    @pl.when(slot == 0)
    def _():
        out_ref[:, 2 * SLOTS] = jnp.zeros((peers, HALF, LANES), BF16)

    for g in range(peers // group):
        part = slice(g * group, (g + 1) * group)
        q = q_ref[part, slot].reshape(rows, LANES)
        scores = dot_nt(q, keys)
        weights, totals, masses = [], [], []
        for h in range(2):
            own = jnp.where(keep, scores[:, h * node_max : (h + 1) * node_max], NEG)
            peak = jnp.max(own, axis=1, keepdims=True)
            weight = jnp.exp(own - peak)
            total = jnp.sum(weight, axis=1, keepdims=True)
            weights.append(weight.astype(BF16))
            totals.append(total)
            masses.append(peak + jnp.log(total))
        mixed = dot_nn(jnp.concatenate(weights, axis=1), values)
        total = by_head(jnp.concatenate(totals, axis=0))
        mass = by_head(jnp.concatenate(masses, axis=0))
        out = (mixed / total).astype(BF16).reshape(group, 2, HALF, LANES)
        out_ref[part, 2 * slot] = out[:, 0]
        out_ref[part, 2 * slot + 1] = out[:, 1]
        mass = mass.reshape(group, 2, HALF, LANES)
        mass = jnp.where(lane % HD < HD // 2, mass[:, 0], mass[:, 1])
        high = mass.astype(BF16).astype(F32)
        rest = mass - high
        mid = rest.astype(BF16).astype(F32)
        sent = jnp.where(piece == 0, high, jnp.where(piece == 1, mid, rest - mid))
        held = out_ref[part, 2 * SLOTS].astype(F32)
        held = jnp.where((piece >= 0) & (piece < 3), sent, held)
        out_ref[part, 2 * SLOTS] = held.astype(BF16)


def node_attention(lens, queries, caches):
    peers, slots, suf, _ = queries.shape
    node_max = caches.shape[3]

    def cache_spec(which):
        return pl.BlockSpec(
            (1, 1, pl.Squeezed(), node_max, LANES), lambda s, n: (s // 2, which, s % 2, 0, 0)
        )

    return pl.pallas_call(
        node_kernel,
        out_shape=jax.ShapeDtypeStruct((peers, 2 * slots + 1, HALF, LANES), BF16),
        grid_spec=pltpu.PrefetchScalarGridSpec(
            num_scalar_prefetch=1,
            grid=(slots,),
            in_specs=[
                pl.BlockSpec((peers, slots, suf, LANES), lambda s, n: (0, 0, 0, 0)),
                cache_spec(0),
                cache_spec(1),
            ],
            out_specs=pl.BlockSpec((peers, 2 * slots + 1, HALF, LANES), lambda s, n: (0, 0, 0, 0)),
        ),
        compiler_params=pltpu.CompilerParams(vmem_limit_bytes=40 << 20),
        cost_estimate=pl.CostEstimate(
            flops=2 << 30, bytes_accessed=4 << 20, transcendentals=4 << 20
        ),
    )(lens, queries, caches, caches)


def root_kernel(
    used, members, valid, chunk_tenant, root_len, coords, q_ref, k_ref, v_ref, root_ref, out_ref, mass_ref
):
    suf = q_ref.shape[1]
    rows = CHUNK * suf
    root_rows = NY * NZ * NX * root_ref.shape[5]
    per = root_ref.shape[5]

    def body(c, _):
        tenant = chunk_tenant[c]
        where_ = [members[c * CHUNK + j] for j in range(CHUNK)]
        q = both_heads(jnp.concatenate([q_ref[w] for w in where_], axis=0))
        own_k = jnp.concatenate([k_ref[w] for w in where_], axis=0)
        own_v = jnp.concatenate([v_ref[w] for w in where_], axis=0)
        keys = root_ref[:, :, :, 0, tenant].reshape(root_rows, LANES)
        values = root_ref[:, :, :, 1, tenant].reshape(root_rows, LANES)
        n = lax.broadcasted_iota(I32, (1, root_rows), 1)
        row = n % per
        z = (n // per) % NZ
        x = (n // (per * NZ)) % NX
        y = n // (per * NX * NZ)
        place = (((z ^ coords[0]) * NX + (x ^ coords[1])) * NY + y) * per + row
        scores = jnp.where(place < root_len[tenant], dot_nt(q, keys), NEG)
        own_row = (lax.broadcasted_iota(I32, (2 * rows, rows), 0) % rows) // suf
        own_col = lax.broadcasted_iota(I32, (2 * rows, rows), 1) // suf
        own = jnp.where(own_row == own_col, dot_nt(q, own_k), NEG)
        peak = jnp.maximum(
            jnp.max(scores, axis=1, keepdims=True), jnp.max(own, axis=1, keepdims=True)
        )
        weights = jnp.exp(scores - peak)
        own_weights = jnp.exp(own - peak)
        total = jnp.sum(weights, axis=1, keepdims=True) + jnp.sum(
            own_weights, axis=1, keepdims=True
        )
        mixed = dot_nn(weights.astype(BF16), values) + dot_nn(own_weights.astype(BF16), own_v)
        out = by_head(mixed) / by_head(total)
        mass = by_head(peak + jnp.log(total))
        for j in range(CHUNK):

            @pl.when(valid[c * CHUNK + j] > 0)
            def _(j=j):
                out_ref[where_[j]] = out[j * suf : (j + 1) * suf]
                mass_ref[where_[j]] = mass[j * suf : (j + 1) * suf]

        return 0

    lax.fori_loop(0, used[0], body, 0)


def root_attention(used, members, valid, chunk_tenant, root_len, coords, q, k, v, roots):
    reqs, suf, _ = q.shape
    shape = jax.ShapeDtypeStruct((reqs, suf, LANES), F32)
    vmem = pl.BlockSpec(memory_space=pltpu.VMEM)
    return pl.pallas_call(
        root_kernel,
        out_shape=(shape, shape),
        in_specs=[pl.BlockSpec(memory_space=pltpu.SMEM)] * 6 + [vmem] * 4,
        out_specs=(vmem, vmem),
        compiler_params=pltpu.CompilerParams(vmem_limit_bytes=40 << 20),
        cost_estimate=pl.CostEstimate(
            flops=4 << 30, bytes_accessed=4 << 20, transcendentals=4 << 20
        ),
    )(used, members, valid, chunk_tenant, root_len, coords, q, k, v, roots)


def merge_kernel(pos, dst_b, dst_l, back_ref, out_ref, mass_ref, send_ref, node_mass):
    reqs, suf, _ = out_ref.shape
    per_block = reqs // N_BLK
    src = lax.broadcasted_iota(I32, (LANES, LANES), 0)
    dst = lax.broadcasted_iota(I32, (LANES, LANES), 1)
    packed = back_ref[:, 2 * SLOTS].reshape(PEERS * HALF, LANES)
    for s in range(SLOTS):
        for g in range(2):
            hit = (src // HD == dst // HD) & ((src % HD) // (HD // 2) == g)
            hit = hit & ((src % (HD // 2)) // 3 == s)
            pick = jnp.where(hit, 1.0, 0.0).astype(BF16)
            node_mass[:, s, g] = dot_nn(packed, pick).reshape(PEERS, HALF, LANES)

    def body(r, _):
        here = pos[r]
        outs = [out_ref[here]]
        masses = [mass_ref[here]]
        for table in (dst_b, dst_l):
            peer = table[r] // SLOTS
            slot = table[r] % SLOTS
            outs.append(back_ref[peer, pl.ds(2 * slot, 2)].astype(F32).reshape(suf, LANES))
            masses.append(node_mass[peer, slot].reshape(suf, LANES))
        top = jnp.maximum(jnp.maximum(masses[0], masses[1]), masses[2])
        parts = [jnp.exp(m - top) for m in masses]
        total = parts[0] + parts[1] + parts[2]
        attn = (parts[0] * outs[0] + parts[1] * outs[1] + parts[2] * outs[2]) / total
        attn = attn.astype(BF16)
        block = r // per_block
        send_ref[block, 0, r % per_block] = attn
        send_ref[(block + N_BLK // 2) % N_BLK, 1, r % per_block] = attn
        return 0

    lax.fori_loop(0, reqs, body, 0, unroll=2)


def merge(pos, dst_b, dst_l, back, out, mass):
    reqs, suf, _ = out.shape
    vmem = pl.BlockSpec(memory_space=pltpu.VMEM)
    return pl.pallas_call(
        merge_kernel,
        out_shape=jax.ShapeDtypeStruct((N_BLK, 2, reqs // N_BLK, suf, LANES), BF16),
        in_specs=[pl.BlockSpec(memory_space=pltpu.SMEM)] * 3 + [vmem] * 3,
        out_specs=vmem,
        scratch_shapes=[pltpu.VMEM((PEERS, SLOTS, 2, HALF, LANES), F32)],
        compiler_params=pltpu.CompilerParams(vmem_limit_bytes=30 << 20),
        cost_estimate=pl.CostEstimate(
            flops=1 << 27, bytes_accessed=4 << 20, transcendentals=1 << 20
        ),
    )(pos, dst_b, dst_l, back, out, mass)


def rows_norm(values, gain, shift):
    center = values - jnp.mean(values, axis=1, keepdims=True)
    spread = jnp.mean(center * center, axis=1, keepdims=True)
    return center * lax.rsqrt(spread + EPS) * gain + shift


def feed_kernel(attn_ref, w_out_ref, tok_a, tok_b, vec_ref, w0, w1, w2, w3, norm_ref, own_ref, far_ref):
    rows = tok_a.shape[0]
    width = tok_a.shape[1]
    attn = jnp.concatenate([attn_ref[h] for h in range(N_BLK)], axis=1)
    tok = jnp.concatenate([tok_a[...], tok_b[...]], axis=0).astype(F32)
    vec = vec_ref[...].astype(F32)
    mixed = tok + dot_nn(attn, w_out_ref[...]) + vec[0:1]
    norm = rows_norm(mixed, vec[1:2], vec[2:3]).astype(BF16)
    norm_ref[...] = norm[:rows]
    total = jnp.zeros((2 * rows, width), F32)
    units = w0.shape[1]
    for w in (w0, w1, w2, w3):
        inner = dot_nn(norm, w[:width]) + w[width + 2 * units : width + 2 * units + 16].astype(F32)[0:1]
        hidden = (0.5 * inner * (1.0 + lax.erf(inner * (0.5**0.5)))).astype(BF16)
        down = [
            dot_nn(hidden, w[width + i * units : width + (i + 1) * units]) for i in range(width // units)
        ]
        total = total + jnp.concatenate(down, axis=1)
    own_ref[...] = total[:rows]
    far_ref[...] = total[rows:].astype(BF16)


def feed_forward(attn, w_out, tok_a, tok_b, vectors, packs):
    rows, width = tok_a.shape
    vmem = pl.BlockSpec(memory_space=pltpu.VMEM)
    return pl.pallas_call(
        feed_kernel,
        out_shape=(
            jax.ShapeDtypeStruct((rows, width), BF16),
            jax.ShapeDtypeStruct((rows, width), F32),
            jax.ShapeDtypeStruct((rows, width), BF16),
        ),
        in_specs=[vmem] * 9,
        out_specs=(vmem, vmem, vmem),
        compiler_params=pltpu.CompilerParams(vmem_limit_bytes=48 << 20),
        cost_estimate=pl.CostEstimate(
            flops=3 << 30, bytes_accessed=12 << 20, transcendentals=1 << 20
        ),
    )(attn, w_out, tok_a, tok_b, vectors, *packs)


def on_device(
    tokens,
    w_qkv,
    w_out,
    b_out,
    gain1,
    shift1,
    w_up,
    b_up,
    w_down,
    b_down,
    gain2,
    shift2,
    root_cache,
    node_cache,
    root_len,
    node_len,
    node_parent,
    node_place,
    req_leaf,
):
    req_dev, suf, width = tokens.shape
    cols = w_qkv.shape[2]
    own_rows = req_dev * suf
    reqs = req_leaf.shape[0]
    nodes = node_place.shape[0]
    node_max = node_cache.shape[2]
    tenants = root_cache.shape[1]
    root_per = root_cache.shape[2]
    blk = lax.axis_index("blk")
    owner = lax.axis_index("owner")
    my_z = owner // (NX * NY)
    my_x = (owner // NY) % NX
    my_y = owner % NY
    swap = xor_pairs(N_BLK, 1)
    n_own = N_BLK // 2

    def zero_after(value):
        flat = value.reshape(-1, value.shape[-1])
        return jnp.minimum(jnp.abs(flat[:1, :1]), 0)

    tok = tokens.reshape(own_rows, width)
    half = [tok] + [lax.ppermute(tok, "blk", xor_pairs(N_BLK, 2 * k)) for k in range(1, n_own)]
    tok_far = half[2]
    first_come, last_come = half[1], half[3]
    half = jnp.stack(half)
    other = lax.ppermute(half, "blk", swap)

    n_owner = NX * NY * NZ
    roots = root_cache.reshape(-1, LANES) + zero_after(first_come)
    roots = jnp.stack([roots, lax.ppermute(roots, "owner", xor_pairs(n_owner, NX * NY))])
    roots = jnp.stack(
        [roots] + [lax.ppermute(roots, "owner", xor_pairs(n_owner, k * NY)) for k in range(1, NX)]
    )
    y_groups = [[g * NY + y for y in range(NY)] for g in range(NZ * NX)]
    roots = lax.all_gather(roots, "owner", axis=0, tiled=False, axis_index_groups=y_groups)
    roots = roots.reshape(NY, NX, NZ, 2, tenants, root_per, LANES)

    node_rows = node_cache.reshape(-1, LANES) + zero_after(last_come)
    node_far = lax.ppermute(node_rows, "owner", xor_pairs(n_owner, NX * NY))
    caches = jnp.stack([node_rows, node_far]).reshape(NZ, 2, 2, node_max, LANES)

    w_out_all = lax.all_gather(w_out + zero_after(last_come), "blk", axis=0, tiled=True)
    units = w_up.shape[1]
    pack = jnp.concatenate(
        [w_up]
        + [w_down[:, i * units : (i + 1) * units] for i in range(width // units)]
        + [jnp.broadcast_to(b_up[None, :], (16, units))],
        axis=0,
    )
    pack_side = lax.ppermute(pack, "blk", swap)
    pack_next = lax.ppermute(pack + zero_after(node_far), "blk", xor_pairs(N_BLK, 2))
    pack_last = lax.ppermute(pack_next, "blk", swap)
    packs = [pack, pack_side, pack_next, pack_last]

    branch = node_parent[req_leaf]
    tenant = node_parent[branch]

    def slot_index(place):
        at = place // 2
        z, x, y = at // (NX * NY), (at // NY) % NX, at % NY
        return ((x * NY + y) * SLOTS + (z ^ my_z) * 2 + place % 2).astype(I32)

    dst_b = slot_index(node_place[branch])
    dst_l = slot_index(node_place[req_leaf])
    req_ids = jnp.arange(reqs, dtype=I32)
    rel = (req_ids // req_dev) ^ blk
    pos = ((rel % 2) * n_own + rel // 2) * req_dev + req_ids % req_dev
    local = jnp.arange(SLOTS, dtype=I32)
    local_slot = ((((local // 2) ^ my_z) * NX + my_x) * NY + my_y) * 2 + local % 2
    lens = jnp.sum(jnp.where(local_slot[:, None] == node_place[None, :], node_len[None, :], 0), axis=1)
    same = tenant[:, None] == tenant[None, :]
    within = jnp.sum(jnp.where(same & (req_ids[None, :] < req_ids[:, None]), 1, 0), axis=1)
    tenant_ids = jnp.arange(tenants, dtype=I32)
    counts = jnp.sum(jnp.where(tenant_ids[:, None] == tenant[None, :], 1, 0), axis=1)
    chunks = (counts + CHUNK - 1) // CHUNK
    ends = jnp.sum(jnp.where(tenant_ids[None, :] <= tenant_ids[:, None], chunks[None, :], 0), axis=1)
    first = ends - chunks
    first_of = jnp.sum(jnp.where(tenant[:, None] == tenant_ids[None, :], first[None, :], 0), axis=1)
    place_in = first_of * CHUNK + within
    max_chunks = reqs // CHUNK + tenants - 1
    seats = jnp.arange(max_chunks * CHUNK, dtype=I32)
    seated = seats[:, None] == place_in[None, :]
    members = jnp.sum(jnp.where(seated, pos[None, :], 0), axis=1).astype(I32)
    valid = jnp.sum(jnp.where(seated, 1, 0), axis=1).astype(I32)
    chunk_ids = jnp.arange(max_chunks, dtype=I32)
    chunk_tenant = jnp.minimum(
        jnp.sum(jnp.where(chunk_ids[:, None] >= ends[None, :], 1, 0), axis=1), tenants - 1
    ).astype(I32)
    used = ends[-1:].astype(I32)
    coords = jnp.stack([my_z, my_x]).astype(I32)

    def project(which):
        w = w_qkv[:, which]
        out = jnp.concatenate(
            [jnp.dot(part.reshape(-1, width), w, preferred_element_type=F32) for part in (half, other)]
        )
        return out.astype(BF16).reshape(reqs, suf, cols)

    q = project(0) * jnp.asarray(HD**-0.5, BF16)
    outgoing = route(pos, dst_b, dst_l, q).reshape(PEERS, SLOTS, suf, cols)
    groups = [[z * PEERS + p for p in range(PEERS)] for z in range(NZ)]
    incoming = lax.all_to_all(
        outgoing, "owner", split_axis=0, concat_axis=0, axis_index_groups=groups, tiled=True
    )
    k_new = project(1)
    v_new = project(2)
    order = jnp.arange(N_BLK, dtype=I32) ^ blk
    order = (order % 2) * n_own + order // 2
    new_caches = jnp.stack([k_new, v_new]).reshape(2, N_BLK, req_dev, suf, cols)
    new_caches = jnp.take(new_caches, order, axis=1).reshape(2, reqs, suf, cols)

    answers = node_attention(lens, incoming, caches)
    back = lax.all_to_all(
        answers, "owner", split_axis=0, concat_axis=0, axis_index_groups=groups, tiled=True
    )
    out, mass = root_attention(
        used, members, valid, chunk_tenant, root_len, coords, q, k_new, v_new, roots
    )
    send = merge(pos, dst_b, dst_l, back, out, mass)
    attn = lax.all_to_all(
        send.reshape(N_BLK, 2 * own_rows, cols), "blk", split_axis=0, concat_axis=0, tiled=True
    )
    vectors = jnp.stack([b_out, gain1, shift1])
    own_norm, down, down_far = feed_forward(attn, w_out_all, tok, tok_far, vectors, packs)
    total = down + lax.ppermute(down_far, "blk", xor_pairs(N_BLK, N_BLK // 2)).astype(F32)
    result = layer_norm(
        own_norm.astype(F32) + total + b_down.astype(F32), gain2, shift2
    ).astype(BF16)
    return (result.reshape(req_dev, suf, width), new_caches)


def solution(mesh):
    in_specs = (
        P(("owner", "blk"), None, None),
        P(None, None, "blk"),
        P("blk", None),
        P(),
        P(),
        P(),
        P(None, "blk"),
        P("blk"),
        P("blk", None),
        P(),
        P(),
        P(),
        P(None, None, "owner", "blk"),
        P(None, "owner", None, "blk"),
        P(),
        P(),
        P(),
        P(),
        P("owner"),
    )
    out_specs = (P(("owner", "blk"), None, None), P(None, "owner", None, "blk"))
    return jax.shard_map(
        on_device, mesh=mesh, in_specs=in_specs, out_specs=out_specs, check_vma=False
    )
```

```python
import functools

import jax
import jax.numpy as jnp
from jax import lax
from jax.experimental import pallas as pl
from jax.experimental.pallas import tpu as pltpu
from jax.sharding import PartitionSpec as P

F32 = jnp.float32
BF16 = jnp.bfloat16
I32 = jnp.int32

HD = 64
LANES = 128
N_BLK = 8
NX, NY, NZ = 4, 8, 2
PEERS = NX * NY
SLOTS = 2 * NZ
HALF = 16
CHUNK = 4
NEG = -1e30
EPS = 1e-05


def layer_norm(values, gain, shift):
    center = values - jnp.mean(values, axis=-1, keepdims=True)
    spread = jnp.mean(center * center, axis=-1, keepdims=True)
    return center * lax.rsqrt(spread + EPS) * gain.astype(F32) + shift.astype(F32)


def xor_pairs(count, bits):
    return [(i, i ^ bits) for i in range(count)]


def dot_nt(a, b):
    return lax.dot_general(a, b, (((1,), (1,)), ((), ())), preferred_element_type=F32)


def dot_nn(a, b):
    return lax.dot_general(a, b, (((1,), (0,)), ((), ())), preferred_element_type=F32)


def both_heads(q):
    lane = lax.broadcasted_iota(I32, q.shape, 1)
    zero = jnp.zeros_like(q)
    return jnp.concatenate([jnp.where(lane < HD, q, zero), jnp.where(lane < HD, zero, q)], axis=0)


def by_head(stacked):
    rows = stacked.shape[0] // 2
    lane = lax.broadcasted_iota(I32, (rows, LANES), 1)
    first = jnp.broadcast_to(stacked[:rows], (rows, LANES))
    second = jnp.broadcast_to(stacked[rows:], (rows, LANES))
    return jnp.where(lane < HD, first, second)


def query_kernel(pos, dst_b, dst_l, half_ref, near_ref, other_ref, w_ref, after_ref, q_ref, out_ref):
    del after_ref
    reqs, suf, cols = q_ref.shape
    out_ref[...] = jnp.zeros_like(out_ref)
    weights = w_ref[...]
    at = 0
    for ref in (half_ref, near_ref, other_ref):
        rows = ref[...].reshape(-1, ref.shape[-1])
        q = dot_nn(rows, weights).astype(BF16).astype(F32) * HD**-0.5
        count = rows.shape[0] // suf
        q_ref[at : at + count] = q.astype(BF16).reshape(count, suf, cols)
        at += count

    def body(r, _):
        tile = q_ref[pos[r]]
        out_ref[dst_b[r]] = tile
        out_ref[dst_l[r]] = tile
        return 0

    lax.fori_loop(0, reqs, body, 0, unroll=2)


def query_and_route(pos, dst_b, dst_l, half, near, other, w, suf, after):
    reqs = pos.shape[0]
    vmem = pl.BlockSpec(memory_space=pltpu.VMEM)
    return pl.pallas_call(
        query_kernel,
        out_shape=(
            jax.ShapeDtypeStruct((reqs, suf, LANES), BF16),
            jax.ShapeDtypeStruct((PEERS * SLOTS, suf, LANES), BF16),
        ),
        in_specs=[pl.BlockSpec(memory_space=pltpu.SMEM)] * 3
        + [vmem] * 4
        + [pl.BlockSpec(memory_space=pl.ANY)],
        out_specs=(vmem, vmem),
        compiler_params=pltpu.CompilerParams(vmem_limit_bytes=24 << 20),
        cost_estimate=pl.CostEstimate(flops=1 << 28, bytes_accessed=4 << 20, transcendentals=0),
    )(pos, dst_b, dst_l, half, near, other, w, after)


def pack_kernel(up_ref, down_ref, bias_ref, after_ref, out_ref):
    del after_ref
    width = up_ref.shape[0]
    units = out_ref.shape[2]
    for j in range(2):
        own = slice(j * units, (j + 1) * units)
        out_ref[j, :width] = up_ref[:, own]
        for i in range(width // units):
            out_ref[j, width + i * units : width + (i + 1) * units] = down_ref[
                own, i * units : (i + 1) * units
            ]
        bias = jnp.broadcast_to(bias_ref[:, own].astype(F32), (16, units))
        out_ref[j, 2 * width :] = bias.astype(BF16)


def pack_weights(up, down, bias, after):
    width, units = up.shape
    vmem = pl.BlockSpec(memory_space=pltpu.VMEM)
    return pl.pallas_call(
        pack_kernel,
        out_shape=jax.ShapeDtypeStruct((2, 2 * width + 16, units // 2), BF16),
        in_specs=[vmem] * 3 + [pl.BlockSpec(memory_space=pl.ANY)],
        out_specs=vmem,
        compiler_params=pltpu.CompilerParams(vmem_limit_bytes=16 << 20),
        cost_estimate=pl.CostEstimate(flops=0, bytes_accessed=4 << 20, transcendentals=0),
    )(up, down, bias.reshape(1, units), after)


def node_kernel(lens, q_ref, k_ref, v_ref, after_ref, out_ref):
    del after_ref
    slot = pl.program_id(0)
    peers, _, suf, _ = q_ref.shape
    group = 8
    rows = group * suf
    node_max = k_ref.shape[2]
    keys = both_heads(k_ref[0, 0])
    values = both_heads(v_ref[0, 0])
    keep = lax.broadcasted_iota(I32, (1, node_max), 1) < lens[slot]
    lane = lax.broadcasted_iota(I32, (group, HALF, LANES), 2)
    piece = lane % (HD // 2) - 3 * slot

    @pl.when(slot == 0)
    def _():
        out_ref[:, 2 * SLOTS] = jnp.zeros((peers, HALF, LANES), BF16)

    for g in range(peers // group):
        part = slice(g * group, (g + 1) * group)
        q = q_ref[part, slot].reshape(rows, LANES)
        scores = dot_nt(q, keys)
        weights, totals, masses = [], [], []
        for h in range(2):
            own = jnp.where(keep, scores[:, h * node_max : (h + 1) * node_max], NEG)
            peak = jnp.max(own, axis=1, keepdims=True)
            weight = jnp.exp(own - peak)
            total = jnp.sum(weight, axis=1, keepdims=True)
            weights.append(weight.astype(BF16))
            totals.append(total)
            masses.append(peak + jnp.log(total))
        mixed = dot_nn(jnp.concatenate(weights, axis=1), values)
        total = by_head(jnp.concatenate(totals, axis=0))
        mass = by_head(jnp.concatenate(masses, axis=0))
        out = (mixed / total).astype(BF16).reshape(group, 2, HALF, LANES)
        out_ref[part, 2 * slot] = out[:, 0]
        out_ref[part, 2 * slot + 1] = out[:, 1]
        mass = mass.reshape(group, 2, HALF, LANES)
        mass = jnp.where(lane % HD < HD // 2, mass[:, 0], mass[:, 1])
        high = mass.astype(BF16).astype(F32)
        rest = mass - high
        mid = rest.astype(BF16).astype(F32)
        sent = jnp.where(piece == 0, high, jnp.where(piece == 1, mid, rest - mid))
        held = out_ref[part, 2 * SLOTS].astype(F32)
        held = jnp.where((piece >= 0) & (piece < 3), sent, held)
        out_ref[part, 2 * SLOTS] = held.astype(BF16)


def node_attention(lens, queries, caches, after):
    peers, slots, suf, _ = queries.shape
    node_max = caches.shape[3]

    def cache_spec(which):
        return pl.BlockSpec(
            (1, 1, pl.Squeezed(), node_max, LANES), lambda s, n: (s // 2, which, s % 2, 0, 0)
        )

    return pl.pallas_call(
        node_kernel,
        out_shape=jax.ShapeDtypeStruct((peers, 2 * slots + 1, HALF, LANES), BF16),
        grid_spec=pltpu.PrefetchScalarGridSpec(
            num_scalar_prefetch=1,
            grid=(slots,),
            in_specs=[
                pl.BlockSpec((peers, slots, suf, LANES), lambda s, n: (0, 0, 0, 0)),
                cache_spec(0),
                cache_spec(1),
                pl.BlockSpec(memory_space=pl.ANY),
            ],
            out_specs=pl.BlockSpec((peers, 2 * slots + 1, HALF, LANES), lambda s, n: (0, 0, 0, 0)),
        ),
        compiler_params=pltpu.CompilerParams(vmem_limit_bytes=40 << 20),
        cost_estimate=pl.CostEstimate(
            flops=2 << 30, bytes_accessed=4 << 20, transcendentals=4 << 20
        ),
    )(lens, queries, caches, caches, after)


def root_kernel(
    used, members, valid, chunk_tenant, root_len, coords, q_ref, k_ref, v_ref, root_ref, out_ref, mass_ref
):
    suf = q_ref.shape[1]
    rows = CHUNK * suf
    root_rows = NY * NZ * NX * root_ref.shape[5]
    per = root_ref.shape[5]

    def body(c, _):
        tenant = chunk_tenant[c]
        where_ = [members[c * CHUNK + j] for j in range(CHUNK)]
        q = both_heads(jnp.concatenate([q_ref[w] for w in where_], axis=0))
        own_k = jnp.concatenate([k_ref[w] for w in where_], axis=0)
        own_v = jnp.concatenate([v_ref[w] for w in where_], axis=0)
        keys = root_ref[:, :, :, 0, tenant].reshape(root_rows, LANES)
        values = root_ref[:, :, :, 1, tenant].reshape(root_rows, LANES)
        n = lax.broadcasted_iota(I32, (1, root_rows), 1)
        row = n % per
        z = (n // per) % NZ
        y = (n // (per * NZ)) % NY
        x = n // (per * NY * NZ)
        place = (((z ^ coords[0]) * NX + (x ^ coords[1])) * NY + y) * per + row
        scores = jnp.where(place < root_len[tenant], dot_nt(q, keys), NEG)
        own_row = (lax.broadcasted_iota(I32, (2 * rows, rows), 0) % rows) // suf
        own_col = lax.broadcasted_iota(I32, (2 * rows, rows), 1) // suf
        own = jnp.where(own_row == own_col, dot_nt(q, own_k), NEG)
        peak = jnp.maximum(
            jnp.max(scores, axis=1, keepdims=True), jnp.max(own, axis=1, keepdims=True)
        )
        weights = jnp.exp(scores - peak)
        own_weights = jnp.exp(own - peak)
        total = jnp.sum(weights, axis=1, keepdims=True) + jnp.sum(
            own_weights, axis=1, keepdims=True
        )
        mixed = dot_nn(weights.astype(BF16), values) + dot_nn(own_weights.astype(BF16), own_v)
        out = by_head(mixed) / by_head(total)
        mass = by_head(peak + jnp.log(total))
        for j in range(CHUNK):

            @pl.when(valid[c * CHUNK + j] > 0)
            def _(j=j):
                out_ref[where_[j]] = out[j * suf : (j + 1) * suf]
                mass_ref[where_[j]] = mass[j * suf : (j + 1) * suf]

        return 0

    lax.fori_loop(0, used[0], body, 0)


def root_attention(used, members, valid, chunk_tenant, root_len, coords, q, k, v, roots):
    reqs, suf, _ = q.shape
    shape = jax.ShapeDtypeStruct((reqs, suf, LANES), F32)
    vmem = pl.BlockSpec(memory_space=pltpu.VMEM)
    return pl.pallas_call(
        root_kernel,
        out_shape=(shape, shape),
        in_specs=[pl.BlockSpec(memory_space=pltpu.SMEM)] * 6 + [vmem] * 4,
        out_specs=(vmem, vmem),
        compiler_params=pltpu.CompilerParams(vmem_limit_bytes=40 << 20),
        cost_estimate=pl.CostEstimate(
            flops=4 << 30, bytes_accessed=4 << 20, transcendentals=4 << 20
        ),
    )(used, members, valid, chunk_tenant, root_len, coords, q, k, v, roots)


def merge_kernel(pos, dst_b, dst_l, back_ref, out_ref, mass_ref, send_ref, node_mass):
    reqs, suf, _ = out_ref.shape
    per_block = reqs // N_BLK
    src = lax.broadcasted_iota(I32, (LANES, LANES), 0)
    dst = lax.broadcasted_iota(I32, (LANES, LANES), 1)
    packed = back_ref[:, 2 * SLOTS].reshape(PEERS * HALF, LANES)
    for s in range(SLOTS):
        for g in range(2):
            hit = (src // HD == dst // HD) & ((src % HD) // (HD // 2) == g)
            hit = hit & ((src % (HD // 2)) // 3 == s)
            pick = jnp.where(hit, 1.0, 0.0).astype(BF16)
            node_mass[:, s, g] = dot_nn(packed, pick).reshape(PEERS, HALF, LANES)

    def body(r, _):
        here = pos[r]
        outs = [out_ref[here]]
        masses = [mass_ref[here]]
        for table in (dst_b, dst_l):
            peer = table[r] // SLOTS
            slot = table[r] % SLOTS
            outs.append(back_ref[peer, pl.ds(2 * slot, 2)].astype(F32).reshape(suf, LANES))
            masses.append(node_mass[peer, slot].reshape(suf, LANES))
        top = jnp.maximum(jnp.maximum(masses[0], masses[1]), masses[2])
        parts = [jnp.exp(m - top) for m in masses]
        total = parts[0] + parts[1] + parts[2]
        attn = (parts[0] * outs[0] + parts[1] * outs[1] + parts[2] * outs[2]) / total
        attn = attn.astype(BF16)
        block = r // per_block
        send_ref[block, 0, r % per_block] = attn
        send_ref[(block + N_BLK // 2) % N_BLK, 1, r % per_block] = attn
        return 0

    lax.fori_loop(0, reqs, body, 0, unroll=2)


def merge(pos, dst_b, dst_l, back, out, mass):
    reqs, suf, _ = out.shape
    vmem = pl.BlockSpec(memory_space=pltpu.VMEM)
    return pl.pallas_call(
        merge_kernel,
        out_shape=jax.ShapeDtypeStruct((N_BLK, 2, reqs // N_BLK, suf, LANES), BF16),
        in_specs=[pl.BlockSpec(memory_space=pltpu.SMEM)] * 3 + [vmem] * 3,
        out_specs=vmem,
        scratch_shapes=[pltpu.VMEM((PEERS, SLOTS, 2, HALF, LANES), F32)],
        compiler_params=pltpu.CompilerParams(vmem_limit_bytes=30 << 20),
        cost_estimate=pl.CostEstimate(
            flops=1 << 27, bytes_accessed=4 << 20, transcendentals=1 << 20
        ),
    )(pos, dst_b, dst_l, back, out, mass)


def rows_norm(values, gain, shift):
    center = values - jnp.mean(values, axis=1, keepdims=True)
    spread = jnp.mean(center * center, axis=1, keepdims=True)
    return center * lax.rsqrt(spread + EPS) * gain + shift


def feed_kernel(attn_ref, w_out_ref, tok_a, tok_b, vec_ref, w0, w1, w2, w3, norm_ref, own_ref, far_ref):
    rows = tok_a.shape[0]
    width = tok_a.shape[1]
    attn = jnp.concatenate([attn_ref[h] for h in range(N_BLK)], axis=1)
    tok = jnp.concatenate([tok_a[...], tok_b[...]], axis=0).astype(F32)
    vec = vec_ref[...].astype(F32)
    mixed = tok + dot_nn(attn, w_out_ref[...]) + vec[0:1]
    norm = rows_norm(mixed, vec[1:2], vec[2:3]).astype(BF16)
    norm_ref[...] = norm[:rows]
    total = jnp.zeros((2 * rows, width), F32)
    units = w0.shape[-1]
    for w in [ref.at[i] for ref in (w0, w1, w2, w3) for i in range(2)]:
        bias = w[width + units * (width // units) :].astype(F32)[0:1]
        inner = dot_nn(norm, w[:width]) + bias
        hidden = (0.5 * inner * (1.0 + lax.erf(inner * (0.5**0.5)))).astype(BF16)
        down = [
            dot_nn(hidden, w[width + i * units : width + (i + 1) * units])
            for i in range(width // units)
        ]
        total = total + jnp.concatenate(down, axis=1)
    own_ref[...] = total[:rows]
    far_ref[...] = total[rows:].astype(BF16)


def feed_forward(attn, w_out, tok_a, tok_b, vectors, packs):
    rows, width = tok_a.shape
    vmem = pl.BlockSpec(memory_space=pltpu.VMEM)
    return pl.pallas_call(
        feed_kernel,
        out_shape=(
            jax.ShapeDtypeStruct((rows, width), BF16),
            jax.ShapeDtypeStruct((rows, width), F32),
            jax.ShapeDtypeStruct((rows, width), BF16),
        ),
        in_specs=[vmem] * (5 + len(packs)),
        out_specs=(vmem, vmem, vmem),
        compiler_params=pltpu.CompilerParams(vmem_limit_bytes=48 << 20),
        cost_estimate=pl.CostEstimate(
            flops=3 << 30, bytes_accessed=12 << 20, transcendentals=1 << 20
        ),
    )(attn, w_out, tok_a, tok_b, vectors, *packs)


def on_device(
    tokens,
    w_qkv,
    w_out,
    b_out,
    gain1,
    shift1,
    w_up,
    b_up,
    w_down,
    b_down,
    gain2,
    shift2,
    root_cache,
    node_cache,
    root_len,
    node_len,
    node_parent,
    node_place,
    req_leaf,
):
    req_dev, suf, width = tokens.shape
    cols = w_qkv.shape[2]
    own_rows = req_dev * suf
    reqs = req_leaf.shape[0]
    nodes = node_place.shape[0]
    node_max = node_cache.shape[2]
    tenants = root_cache.shape[1]
    root_per = root_cache.shape[2]
    blk = lax.axis_index("blk")
    owner = lax.axis_index("owner")
    my_z = owner // (NX * NY)
    my_x = (owner // NY) % NX
    my_y = owner % NY
    swap = xor_pairs(N_BLK, 1)
    n_own = N_BLK // 2

    def zero_after(value):
        flat = value.reshape(-1, value.shape[-1])
        return jnp.minimum(jnp.abs(flat[:1, :1]), 0)

    tok = tokens.reshape(own_rows, width)
    near = lax.ppermute(tok, "blk", swap)
    half = [lax.ppermute(tok, "blk", xor_pairs(N_BLK, 2 * k)) for k in range(1, n_own)]
    tok_far, last_come = half[1], half[2]

    n_owner = NX * NY * NZ
    roots = root_cache.reshape(-1, LANES) + zero_after(near)
    roots = jnp.stack([roots, lax.ppermute(roots, "owner", xor_pairs(n_owner, NX * NY))])
    y_groups = [[g * NY + y for y in range(NY)] for g in range(NZ * NX)]
    roots_y = lax.all_gather(roots, "owner", axis=0, tiled=False, axis_index_groups=y_groups)
    other = lax.ppermute(jnp.stack(half) + zero_after(roots_y), "blk", swap)
    half = jnp.stack([tok] + half)
    roots = jnp.stack(
        [roots_y]
        + [lax.ppermute(roots_y, "owner", xor_pairs(n_owner, k * NY)) for k in range(1, NX)]
    )
    roots = roots.reshape(NX, NY, NZ, 2, tenants, root_per, LANES)

    node_rows = node_cache.reshape(-1, LANES) + zero_after(last_come)
    node_far = lax.ppermute(node_rows, "owner", xor_pairs(n_owner, NX * NY))
    caches = jnp.stack([node_rows, node_far]).reshape(NZ, 2, 2, node_max, LANES)

    w_out_all = lax.all_gather(w_out + zero_after(last_come), "blk", axis=0, tiled=True)
    packs = pack_weights(w_up, w_down, b_up, last_come)
    pack_side = lax.ppermute(packs, "blk", swap)
    z_chips = NZ * n_own

    def to_neighbour(step):
        pairs = []
        for dev in range(n_owner * N_BLK):
            b, own = dev // n_owner, dev % n_owner
            z = (own // PEERS * n_own + b // 2 + step) % z_chips
            pairs.append((dev, (z % n_own * 2 + b % 2) * n_owner + z // n_own * PEERS + own % PEERS))
        part = ((blk // 2 + step + n_own) % n_own) // (n_own // 2)
        sent = lax.dynamic_index_in_dim(packs, part, 0, keepdims=False) + zero_after(node_far)
        return lax.ppermute(sent, ("blk", "owner"), pairs)

    pack_next = jnp.stack([to_neighbour(1), to_neighbour(-1)])
    pack_last = lax.ppermute(pack_next, "blk", swap)
    packs = [packs, pack_side, pack_next, pack_last]

    branch = node_parent[req_leaf]
    tenant = node_parent[branch]

    def slot_index(place):
        at = place // 2
        z, x, y = at // (NX * NY), (at // NY) % NX, at % NY
        return ((x * NY + y) * SLOTS + (z ^ my_z) * 2 + place % 2).astype(I32)

    dst_b = slot_index(node_place[branch])
    dst_l = slot_index(node_place[req_leaf])
    req_ids = jnp.arange(reqs, dtype=I32)
    rel = (req_ids // req_dev) ^ blk
    pos = ((rel % 2) * n_own + rel // 2) * req_dev + req_ids % req_dev
    local = jnp.arange(SLOTS, dtype=I32)
    local_slot = ((((local // 2) ^ my_z) * NX + my_x) * NY + my_y) * 2 + local % 2
    lens = jnp.sum(jnp.where(local_slot[:, None] == node_place[None, :], node_len[None, :], 0), axis=1)
    same = tenant[:, None] == tenant[None, :]
    within = jnp.sum(jnp.where(same & (req_ids[None, :] < req_ids[:, None]), 1, 0), axis=1)
    tenant_ids = jnp.arange(tenants, dtype=I32)
    counts = jnp.sum(jnp.where(tenant_ids[:, None] == tenant[None, :], 1, 0), axis=1)
    chunks = (counts + CHUNK - 1) // CHUNK
    ends = jnp.sum(jnp.where(tenant_ids[None, :] <= tenant_ids[:, None], chunks[None, :], 0), axis=1)
    first = ends - chunks
    first_of = jnp.sum(jnp.where(tenant[:, None] == tenant_ids[None, :], first[None, :], 0), axis=1)
    place_in = first_of * CHUNK + within
    max_chunks = reqs // CHUNK + tenants - 1
    seats = jnp.arange(max_chunks * CHUNK, dtype=I32)
    seated = seats[:, None] == place_in[None, :]
    members = jnp.sum(jnp.where(seated, pos[None, :], 0), axis=1).astype(I32)
    valid = jnp.sum(jnp.where(seated, 1, 0), axis=1).astype(I32)
    chunk_ids = jnp.arange(max_chunks, dtype=I32)
    chunk_tenant = jnp.minimum(
        jnp.sum(jnp.where(chunk_ids[:, None] >= ends[None, :], 1, 0), axis=1), tenants - 1
    ).astype(I32)
    used = ends[-1:].astype(I32)
    coords = jnp.stack([my_z, my_x]).astype(I32)

    q, outgoing = query_and_route(pos, dst_b, dst_l, half, near, other, w_qkv[:, 0], suf, roots_y)
    outgoing = outgoing.reshape(PEERS, SLOTS, suf, cols)

    def project(which):
        w = w_qkv[:, which]
        out = jnp.concatenate(
            [
                jnp.dot(part.reshape(-1, width), w, preferred_element_type=F32)
                for part in (half, near, other)
            ]
        )
        return out.astype(BF16).reshape(reqs, suf, cols)

    groups = [[z * PEERS + p for p in range(PEERS)] for z in range(NZ)]
    incoming = lax.all_to_all(
        outgoing, "owner", split_axis=0, concat_axis=0, axis_index_groups=groups, tiled=True
    )
    k_new = project(1)
    v_new = project(2)
    order = jnp.arange(N_BLK, dtype=I32) ^ blk
    order = (order % 2) * n_own + order // 2
    new_caches = jnp.stack([k_new, v_new]).reshape(2, N_BLK, req_dev, suf, cols)
    new_caches = jnp.take(new_caches, order, axis=1).reshape(2, reqs, suf, cols)

    answers = node_attention(lens, incoming, caches, roots)
    back = lax.all_to_all(
        answers, "owner", split_axis=0, concat_axis=0, axis_index_groups=groups, tiled=True
    )
    out, mass = root_attention(
        used, members, valid, chunk_tenant, root_len, coords, q, k_new, v_new, roots
    )
    send = merge(pos, dst_b, dst_l, back, out, mass)
    attn = lax.all_to_all(
        send.reshape(N_BLK, 2 * own_rows, cols), "blk", split_axis=0, concat_axis=0, tiled=True
    )
    vectors = jnp.stack([b_out, gain1, shift1])
    own_norm, down, down_far = feed_forward(attn, w_out_all, tok, tok_far, vectors, packs)
    total = down + lax.ppermute(down_far, "blk", xor_pairs(N_BLK, N_BLK // 2)).astype(F32)
    result = layer_norm(
        own_norm.astype(F32) + total + b_down.astype(F32), gain2, shift2
    ).astype(BF16)
    return (result.reshape(req_dev, suf, width), new_caches)


def solution(mesh):
    in_specs = (
        P(("owner", "blk"), None, None),
        P(None, None, "blk"),
        P("blk", None),
        P(),
        P(),
        P(),
        P(None, "blk"),
        P("blk"),
        P("blk", None),
        P(),
        P(),
        P(),
        P(None, None, "owner", "blk"),
        P(None, "owner", None, "blk"),
        P(),
        P(),
        P(),
        P(),
        P("owner"),
    )
    out_specs = (P(("owner", "blk"), None, None), P(None, "owner", None, "blk"))
    return jax.shard_map(
        on_device, mesh=mesh, in_specs=in_specs, out_specs=out_specs, check_vma=False
    )
```

```python
import functools

import jax
import jax.numpy as jnp
from jax import lax
from jax.experimental import pallas as pl
from jax.experimental.pallas import tpu as pltpu
from jax.sharding import PartitionSpec as P

F32 = jnp.float32
BF16 = jnp.bfloat16
I32 = jnp.int32

HD = 64
LANES = 128
N_BLK = 8
NX, NY, NZ = 4, 8, 2
PEERS = NX * NY
SLOTS = 2 * NZ
HALF = 16
CHUNK = 4
NEG = -1e30
EPS = 1e-05


def layer_norm(values, gain, shift):
    center = values - jnp.mean(values, axis=-1, keepdims=True)
    spread = jnp.mean(center * center, axis=-1, keepdims=True)
    return center * lax.rsqrt(spread + EPS) * gain.astype(F32) + shift.astype(F32)


def xor_pairs(count, bits):
    return [(i, i ^ bits) for i in range(count)]


def dot_nt(a, b):
    return lax.dot_general(a, b, (((1,), (1,)), ((), ())), preferred_element_type=F32)


def dot_nn(a, b):
    return lax.dot_general(a, b, (((1,), (0,)), ((), ())), preferred_element_type=F32)


def both_heads(q):
    lane = lax.broadcasted_iota(I32, q.shape, 1)
    zero = jnp.zeros_like(q)
    return jnp.concatenate([jnp.where(lane < HD, q, zero), jnp.where(lane < HD, zero, q)], axis=0)


def by_head(stacked):
    rows = stacked.shape[0] // 2
    lane = lax.broadcasted_iota(I32, (rows, LANES), 1)
    first = jnp.broadcast_to(stacked[:rows], (rows, LANES))
    second = jnp.broadcast_to(stacked[rows:], (rows, LANES))
    return jnp.where(lane < HD, first, second)


def table_kernel(
    coords, leaf_of, parent, place, length, dst_b, dst_l, pos, lens, members, valid, chunk_tenant, used, tenant_of, count
):
    my_z, my_x, my_y, blk = (coords[i] for i in range(4))
    reqs = leaf_of.shape[0]
    req_dev = reqs // N_BLK
    tenants = count.shape[0]

    def slot_index(slot):
        owner = slot // 2
        return (owner % PEERS) * SLOTS + ((owner // PEERS) ^ my_z) * 2 + slot % 2

    for t in range(tenants):
        count[t] = 0

    def first_pass(r, _):
        leaf = leaf_of[r]
        branch = parent[leaf]
        tenant = parent[branch]
        dst_b[r] = slot_index(place[branch])
        dst_l[r] = slot_index(place[leaf])
        rel = (r // req_dev) ^ blk
        pos[r] = ((rel % 2) * (N_BLK // 2) + rel // 2) * req_dev + r % req_dev
        tenant_of[r] = tenant
        count[tenant] = count[tenant] + 1
        return 0

    lax.fori_loop(0, reqs, first_pass, 0)

    def clear(i, _):
        members[i] = 0
        valid[i] = 0
        return 0

    lax.fori_loop(0, members.shape[0], clear, 0)
    end = 0
    for t in range(tenants):
        chunks = (count[t] + CHUNK - 1) // CHUNK

        def name(c, _, t=t):
            chunk_tenant[c] = t
            return 0

        lax.fori_loop(end, end + chunks, name, 0)
        count[t] = end * CHUNK
        end = end + chunks
    used[0] = end

    def second_pass(r, _):
        tenant = tenant_of[r]
        seat = count[tenant]
        count[tenant] = seat + 1
        members[seat] = pos[r]
        valid[seat] = 1
        return 0

    lax.fori_loop(0, reqs, second_pass, 0)

    def node(n, _):
        slot = place[n]
        owner = slot // 2

        @pl.when(owner % PEERS == my_x * NY + my_y)
        def _():
            lens[((owner // PEERS) ^ my_z) * 2 + slot % 2] = length[n]

        return 0

    lax.fori_loop(0, place.shape[0], node, 0)


def make_tables(coords, leaf_of, parent, place, length, tenants):
    reqs = leaf_of.shape[0]
    max_chunks = reqs // CHUNK + tenants - 1
    smem = pl.BlockSpec(memory_space=pltpu.SMEM)
    sizes = (reqs, reqs, reqs, SLOTS, max_chunks * CHUNK, max_chunks * CHUNK, max_chunks, 1)
    return pl.pallas_call(
        table_kernel,
        out_shape=tuple(jax.ShapeDtypeStruct((n,), I32) for n in sizes),
        in_specs=[smem] * 5,
        out_specs=(smem,) * len(sizes),
        scratch_shapes=[pltpu.SMEM((reqs,), I32), pltpu.SMEM((tenants,), I32)],
        cost_estimate=pl.CostEstimate(flops=1 << 20, bytes_accessed=1 << 12, transcendentals=0),
    )(coords, leaf_of, parent, place, length)


def query_kernel(pos, dst_b, dst_l, half_ref, near_ref, other_ref, w_ref, after_ref, q_ref, out_ref):
    del after_ref
    reqs, suf, cols = q_ref.shape
    out_ref[...] = jnp.zeros_like(out_ref)
    weights = w_ref[...]
    at = 0
    for ref in (half_ref, near_ref, other_ref):
        rows = ref[...].reshape(-1, ref.shape[-1])
        q = dot_nn(rows, weights).astype(BF16).astype(F32) * HD**-0.5
        count = rows.shape[0] // suf
        q_ref[at : at + count] = q.astype(BF16).reshape(count, suf, cols)
        at += count

    def body(r, _):
        tile = q_ref[pos[r]]
        out_ref[dst_b[r]] = tile
        out_ref[dst_l[r]] = tile
        return 0

    lax.fori_loop(0, reqs, body, 0, unroll=2)


def query_and_route(pos, dst_b, dst_l, half, near, other, w, suf, after):
    reqs = pos.shape[0]
    vmem = pl.BlockSpec(memory_space=pltpu.VMEM)
    return pl.pallas_call(
        query_kernel,
        out_shape=(
            jax.ShapeDtypeStruct((reqs, suf, LANES), BF16),
            jax.ShapeDtypeStruct((PEERS * SLOTS, suf, LANES), BF16),
        ),
        in_specs=[pl.BlockSpec(memory_space=pltpu.SMEM)] * 3
        + [vmem] * 4
        + [pl.BlockSpec(memory_space=pl.ANY)],
        out_specs=(vmem, vmem),
        compiler_params=pltpu.CompilerParams(vmem_limit_bytes=24 << 20),
        cost_estimate=pl.CostEstimate(flops=1 << 28, bytes_accessed=4 << 20, transcendentals=0),
    )(pos, dst_b, dst_l, half, near, other, w, after)


def pack_kernel(up_ref, down_ref, bias_ref, after_ref, out_ref):
    del after_ref
    width = up_ref.shape[0]
    units = out_ref.shape[2]
    for j in range(2):
        own = slice(j * units, (j + 1) * units)
        out_ref[j, :width] = up_ref[:, own]
        for i in range(width // units):
            out_ref[j, width + i * units : width + (i + 1) * units] = down_ref[
                own, i * units : (i + 1) * units
            ]
        bias = jnp.broadcast_to(bias_ref[:, own].astype(F32), (16, units))
        out_ref[j, 2 * width :] = bias.astype(BF16)


def pack_weights(up, down, bias, after):
    width, units = up.shape
    vmem = pl.BlockSpec(memory_space=pltpu.VMEM)
    return pl.pallas_call(
        pack_kernel,
        out_shape=jax.ShapeDtypeStruct((2, 2 * width + 16, units // 2), BF16),
        in_specs=[vmem] * 3 + [pl.BlockSpec(memory_space=pl.ANY)],
        out_specs=vmem,
        compiler_params=pltpu.CompilerParams(vmem_limit_bytes=16 << 20),
        cost_estimate=pl.CostEstimate(flops=0, bytes_accessed=4 << 20, transcendentals=0),
    )(up, down, bias.reshape(1, units), after)


def node_kernel(lens, q_ref, k_ref, v_ref, after_ref, out_ref):
    del after_ref
    slot = pl.program_id(0)
    peers, _, suf, _ = q_ref.shape
    group = 8
    rows = group * suf
    node_max = k_ref.shape[2]
    keys = both_heads(k_ref[0, 0])
    values = both_heads(v_ref[0, 0])
    keep = lax.broadcasted_iota(I32, (1, node_max), 1) < lens[slot]
    lane = lax.broadcasted_iota(I32, (group, HALF, LANES), 2)
    piece = lane % (HD // 2) - 3 * slot

    @pl.when(slot == 0)
    def _():
        out_ref[:, 2 * SLOTS] = jnp.zeros((peers, HALF, LANES), BF16)

    for g in range(peers // group):
        part = slice(g * group, (g + 1) * group)
        q = q_ref[part, slot].reshape(rows, LANES)
        scores = dot_nt(q, keys)
        weights, totals, masses = [], [], []
        for h in range(2):
            own = jnp.where(keep, scores[:, h * node_max : (h + 1) * node_max], NEG)
            peak = jnp.max(own, axis=1, keepdims=True)
            weight = jnp.exp(own - peak)
            total = jnp.sum(weight, axis=1, keepdims=True)
            weights.append(weight.astype(BF16))
            totals.append(total)
            masses.append(peak + jnp.log(total))
        mixed = dot_nn(jnp.concatenate(weights, axis=1), values)
        total = by_head(jnp.concatenate(totals, axis=0))
        mass = by_head(jnp.concatenate(masses, axis=0))
        out = (mixed / total).astype(BF16).reshape(group, 2, HALF, LANES)
        out_ref[part, 2 * slot] = out[:, 0]
        out_ref[part, 2 * slot + 1] = out[:, 1]
        mass = mass.reshape(group, 2, HALF, LANES)
        mass = jnp.where(lane % HD < HD // 2, mass[:, 0], mass[:, 1])
        high = mass.astype(BF16).astype(F32)
        rest = mass - high
        mid = rest.astype(BF16).astype(F32)
        sent = jnp.where(piece == 0, high, jnp.where(piece == 1, mid, rest - mid))
        held = out_ref[part, 2 * SLOTS].astype(F32)
        held = jnp.where((piece >= 0) & (piece < 3), sent, held)
        out_ref[part, 2 * SLOTS] = held.astype(BF16)


def node_attention(lens, queries, caches, after):
    peers, slots, suf, _ = queries.shape
    node_max = caches.shape[3]

    def cache_spec(which):
        return pl.BlockSpec(
            (1, 1, pl.Squeezed(), node_max, LANES), lambda s, n: (s // 2, which, s % 2, 0, 0)
        )

    return pl.pallas_call(
        node_kernel,
        out_shape=jax.ShapeDtypeStruct((peers, 2 * slots + 1, HALF, LANES), BF16),
        grid_spec=pltpu.PrefetchScalarGridSpec(
            num_scalar_prefetch=1,
            grid=(slots,),
            in_specs=[
                pl.BlockSpec((peers, slots, suf, LANES), lambda s, n: (0, 0, 0, 0)),
                cache_spec(0),
                cache_spec(1),
                pl.BlockSpec(memory_space=pl.ANY),
            ],
            out_specs=pl.BlockSpec((peers, 2 * slots + 1, HALF, LANES), lambda s, n: (0, 0, 0, 0)),
        ),
        compiler_params=pltpu.CompilerParams(vmem_limit_bytes=40 << 20),
        cost_estimate=pl.CostEstimate(
            flops=2 << 30, bytes_accessed=4 << 20, transcendentals=4 << 20
        ),
    )(lens, queries, caches, caches, after)


def root_kernel(
    used, members, valid, chunk_tenant, root_len, coords, q_ref, k_ref, v_ref, root_ref, out_ref, mass_ref
):
    suf = q_ref.shape[1]
    rows = CHUNK * suf
    root_rows = NY * NZ * NX * root_ref.shape[5]
    per = root_ref.shape[5]

    def body(c, _):
        tenant = chunk_tenant[c]
        where_ = [members[c * CHUNK + j] for j in range(CHUNK)]
        q = both_heads(jnp.concatenate([q_ref[w] for w in where_], axis=0))
        own_k = jnp.concatenate([k_ref[w] for w in where_], axis=0)
        own_v = jnp.concatenate([v_ref[w] for w in where_], axis=0)
        keys = root_ref[:, :, :, 0, tenant].reshape(root_rows, LANES)
        values = root_ref[:, :, :, 1, tenant].reshape(root_rows, LANES)
        n = lax.broadcasted_iota(I32, (1, root_rows), 1)
        row = n % per
        z = (n // per) % NZ
        y = (n // (per * NZ)) % NY
        x = n // (per * NY * NZ)
        place = (((z ^ coords[0]) * NX + x) * NY + y) * per + row
        scores = jnp.where(place < root_len[tenant], dot_nt(q, keys), NEG)
        own_row = (lax.broadcasted_iota(I32, (2 * rows, rows), 0) % rows) // suf
        own_col = lax.broadcasted_iota(I32, (2 * rows, rows), 1) // suf
        own = jnp.where(own_row == own_col, dot_nt(q, own_k), NEG)
        peak = jnp.maximum(
            jnp.max(scores, axis=1, keepdims=True), jnp.max(own, axis=1, keepdims=True)
        )
        weights = jnp.exp(scores - peak)
        own_weights = jnp.exp(own - peak)
        total = jnp.sum(weights, axis=1, keepdims=True) + jnp.sum(
            own_weights, axis=1, keepdims=True
        )
        mixed = dot_nn(weights.astype(BF16), values) + dot_nn(own_weights.astype(BF16), own_v)
        out = by_head(mixed) / by_head(total)
        mass = by_head(peak + jnp.log(total))
        for j in range(CHUNK):

            @pl.when(valid[c * CHUNK + j] > 0)
            def _(j=j):
                out_ref[where_[j]] = out[j * suf : (j + 1) * suf]
                mass_ref[where_[j]] = mass[j * suf : (j + 1) * suf]

        return 0

    lax.fori_loop(0, used[0], body, 0)


def root_attention(used, members, valid, chunk_tenant, root_len, coords, q, k, v, roots):
    reqs, suf, _ = q.shape
    shape = jax.ShapeDtypeStruct((reqs, suf, LANES), F32)
    vmem = pl.BlockSpec(memory_space=pltpu.VMEM)
    return pl.pallas_call(
        root_kernel,
        out_shape=(shape, shape),
        in_specs=[pl.BlockSpec(memory_space=pltpu.SMEM)] * 6 + [vmem] * 4,
        out_specs=(vmem, vmem),
        compiler_params=pltpu.CompilerParams(vmem_limit_bytes=40 << 20),
        cost_estimate=pl.CostEstimate(
            flops=4 << 30, bytes_accessed=4 << 20, transcendentals=4 << 20
        ),
    )(used, members, valid, chunk_tenant, root_len, coords, q, k, v, roots)


def merge_kernel(pos, dst_b, dst_l, back_ref, out_ref, mass_ref, send_ref, node_mass):
    reqs, suf, _ = out_ref.shape
    per_block = reqs // N_BLK
    src = lax.broadcasted_iota(I32, (LANES, LANES), 0)
    dst = lax.broadcasted_iota(I32, (LANES, LANES), 1)
    packed = back_ref[:, 2 * SLOTS].reshape(PEERS * HALF, LANES)
    for s in range(SLOTS):
        for g in range(2):
            hit = (src // HD == dst // HD) & ((src % HD) // (HD // 2) == g)
            hit = hit & ((src % (HD // 2)) // 3 == s)
            pick = jnp.where(hit, 1.0, 0.0).astype(BF16)
            node_mass[:, s, g] = dot_nn(packed, pick).reshape(PEERS, HALF, LANES)

    def body(r, _):
        here = pos[r]
        outs = [out_ref[here]]
        masses = [mass_ref[here]]
        for table in (dst_b, dst_l):
            peer = table[r] // SLOTS
            slot = table[r] % SLOTS
            outs.append(back_ref[peer, pl.ds(2 * slot, 2)].astype(F32).reshape(suf, LANES))
            masses.append(node_mass[peer, slot].reshape(suf, LANES))
        top = jnp.maximum(jnp.maximum(masses[0], masses[1]), masses[2])
        parts = [jnp.exp(m - top) for m in masses]
        total = parts[0] + parts[1] + parts[2]
        attn = (parts[0] * outs[0] + parts[1] * outs[1] + parts[2] * outs[2]) / total
        attn = attn.astype(BF16)
        block = r // per_block
        send_ref[block, 0, r % per_block] = attn
        send_ref[(block + N_BLK // 2) % N_BLK, 1, r % per_block] = attn
        return 0

    lax.fori_loop(0, reqs, body, 0, unroll=2)


def merge(pos, dst_b, dst_l, back, out, mass):
    reqs, suf, _ = out.shape
    vmem = pl.BlockSpec(memory_space=pltpu.VMEM)
    return pl.pallas_call(
        merge_kernel,
        out_shape=jax.ShapeDtypeStruct((N_BLK, 2, reqs // N_BLK, suf, LANES), BF16),
        in_specs=[pl.BlockSpec(memory_space=pltpu.SMEM)] * 3 + [vmem] * 3,
        out_specs=vmem,
        scratch_shapes=[pltpu.VMEM((PEERS, SLOTS, 2, HALF, LANES), F32)],
        compiler_params=pltpu.CompilerParams(vmem_limit_bytes=30 << 20),
        cost_estimate=pl.CostEstimate(
            flops=1 << 27, bytes_accessed=4 << 20, transcendentals=1 << 20
        ),
    )(pos, dst_b, dst_l, back, out, mass)


def rows_norm(values, gain, shift):
    center = values - jnp.mean(values, axis=1, keepdims=True)
    spread = jnp.mean(center * center, axis=1, keepdims=True)
    return center * lax.rsqrt(spread + EPS) * gain + shift


def feed_kernel(attn_ref, w_out_ref, tok_a, tok_b, vec_ref, w0, w1, w2, w3, w4, w5, norm_ref, own_ref, far_ref):
    rows = tok_a.shape[0]
    width = tok_a.shape[1]
    attn = jnp.concatenate([attn_ref[h] for h in range(N_BLK)], axis=1)
    tok = jnp.concatenate([tok_a[...], tok_b[...]], axis=0).astype(F32)
    vec = vec_ref[...].astype(F32)
    mixed = tok + dot_nn(attn, w_out_ref[...]) + vec[0:1]
    norm = rows_norm(mixed, vec[1:2], vec[2:3]).astype(BF16)
    norm_ref[...] = norm[:rows]
    total = jnp.zeros((2 * rows, width), F32)
    units = w0.shape[-1]
    for w in [ref.at[i] for ref in (w0, w1) for i in range(2)] + [w2, w3, w4, w5]:
        bias = w[width + units * (width // units) :].astype(F32)[0:1]
        inner = dot_nn(norm, w[:width]) + bias
        hidden = (0.5 * inner * (1.0 + lax.erf(inner * (0.5**0.5)))).astype(BF16)
        down = [
            dot_nn(hidden, w[width + i * units : width + (i + 1) * units])
            for i in range(width // units)
        ]
        total = total + jnp.concatenate(down, axis=1)
    own_ref[...] = total[:rows]
    far_ref[...] = total[rows:].astype(BF16)


def feed_forward(attn, w_out, tok_a, tok_b, vectors, packs):
    rows, width = tok_a.shape
    vmem = pl.BlockSpec(memory_space=pltpu.VMEM)
    return pl.pallas_call(
        feed_kernel,
        out_shape=(
            jax.ShapeDtypeStruct((rows, width), BF16),
            jax.ShapeDtypeStruct((rows, width), F32),
            jax.ShapeDtypeStruct((rows, width), BF16),
        ),
        in_specs=[vmem] * (5 + len(packs)),
        out_specs=(vmem, vmem, vmem),
        compiler_params=pltpu.CompilerParams(vmem_limit_bytes=48 << 20),
        cost_estimate=pl.CostEstimate(
            flops=3 << 30, bytes_accessed=12 << 20, transcendentals=1 << 20
        ),
    )(attn, w_out, tok_a, tok_b, vectors, *packs)


def on_device(
    tokens,
    w_qkv,
    w_out,
    b_out,
    gain1,
    shift1,
    w_up,
    b_up,
    w_down,
    b_down,
    gain2,
    shift2,
    root_cache,
    node_cache,
    root_len,
    node_len,
    node_parent,
    node_place,
    req_leaf,
):
    req_dev, suf, width = tokens.shape
    cols = w_qkv.shape[2]
    own_rows = req_dev * suf
    reqs = req_leaf.shape[0]
    node_max = node_cache.shape[2]
    tenants = root_cache.shape[1]
    root_per = root_cache.shape[2]
    blk = lax.axis_index("blk")
    owner = lax.axis_index("owner")
    my_z = owner // (NX * NY)
    my_x = (owner // NY) % NX
    my_y = owner % NY
    swap = xor_pairs(N_BLK, 1)
    n_own = N_BLK // 2

    def zero_after(value):
        flat = value.reshape(-1, value.shape[-1])
        return jnp.minimum(jnp.abs(flat[:1, :1]), 0)

    coords = jnp.stack([my_z, my_x, my_y, blk]).astype(I32)
    dst_b, dst_l, pos, lens, members, valid, chunk_tenant, used = make_tables(
        coords, req_leaf, node_parent, node_place, node_len, tenants
    )

    tok = tokens.reshape(own_rows, width)
    near = lax.ppermute(tok, "blk", swap)
    half = [lax.ppermute(tok, "blk", xor_pairs(N_BLK, 2 * k)) for k in range(1, n_own)]
    tok_far, last_come = half[1], half[2]

    n_owner = NX * NY * NZ
    roots = root_cache.reshape(-1, LANES)
    roots = jnp.stack([roots, lax.ppermute(roots, "owner", xor_pairs(n_owner, NX * NY))])
    for came in half + [near, jnp.broadcast_to(pos[None, :1], (1, 1)).astype(BF16)]:
        roots = roots + zero_after(came)
    groups = [[z * PEERS + p for p in range(PEERS)] for z in range(NZ)]
    roots = lax.all_gather(roots, "owner", axis=0, tiled=False, axis_index_groups=groups)
    other = lax.ppermute(jnp.stack(half), "blk", swap)
    half = jnp.stack([tok] + half)
    roots = roots.reshape(NX, NY, NZ, 2, tenants, root_per, LANES)

    node_rows = node_cache.reshape(-1, LANES) + zero_after(last_come)
    node_far = lax.ppermute(node_rows, "owner", xor_pairs(n_owner, NX * NY))
    caches = jnp.stack([node_rows, node_far]).reshape(NZ, 2, 2, node_max, LANES)

    w_out_all = lax.all_gather(w_out + zero_after(last_come), "blk", axis=0, tiled=True)
    packs = pack_weights(w_up, w_down, b_up, last_come)
    pack_side = lax.ppermute(packs, "blk", swap)

    q, outgoing = query_and_route(pos, dst_b, dst_l, half, near, other, w_qkv[:, 0], suf, last_come)
    outgoing = outgoing.reshape(PEERS, SLOTS, suf, cols)

    def project(which):
        w = w_qkv[:, which]
        out = jnp.concatenate(
            [
                jnp.dot(part.reshape(-1, width), w, preferred_element_type=F32)
                for part in (half, near, other)
            ]
        )
        return out.astype(BF16).reshape(reqs, suf, cols)

    incoming = lax.all_to_all(
        outgoing, "owner", split_axis=0, concat_axis=0, axis_index_groups=groups, tiled=True
    )
    k_new = project(1)
    v_new = project(2)
    order = jnp.arange(N_BLK, dtype=I32) ^ blk
    order = (order % 2) * n_own + order // 2
    new_caches = jnp.stack([k_new, v_new]).reshape(2, N_BLK, req_dev, suf, cols)
    new_caches = jnp.take(new_caches, order, axis=1).reshape(2, reqs, suf, cols)

    answers = node_attention(lens, incoming, caches, packs)
    z_chips = NZ * n_own

    def to_neighbour(step):
        pairs = []
        for dev in range(n_owner * N_BLK):
            b, own = dev // n_owner, dev % n_owner
            z = (own // PEERS * n_own + b // 2 + step) % z_chips
            pairs.append((dev, (z % n_own * 2 + b % 2) * n_owner + z // n_own * PEERS + own % PEERS))
        part = ((blk // 2 + step + n_own) % n_own) // (n_own // 2)
        sent = lax.dynamic_index_in_dim(packs, part, 0, keepdims=False) + zero_after(answers)
        return lax.ppermute(sent, ("blk", "owner"), pairs)

    pack_next = [to_neighbour(1), to_neighbour(-1)]
    pack_last = [lax.ppermute(part, "blk", swap) for part in pack_next]
    parts = [packs, pack_side] + pack_next + pack_last
    back = lax.all_to_all(
        answers, "owner", split_axis=0, concat_axis=0, axis_index_groups=groups, tiled=True
    )
    out, mass = root_attention(
        used, members, valid, chunk_tenant, root_len, coords, q, k_new, v_new, roots
    )
    send = merge(pos, dst_b, dst_l, back, out, mass)
    attn = lax.all_to_all(
        send.reshape(N_BLK, 2 * own_rows, cols), "blk", split_axis=0, concat_axis=0, tiled=True
    )
    vectors = jnp.stack([b_out, gain1, shift1])
    own_norm, down, down_far = feed_forward(attn, w_out_all, tok, tok_far, vectors, parts)
    total = down + lax.ppermute(down_far, "blk", xor_pairs(N_BLK, N_BLK // 2)).astype(F32)
    result = layer_norm(
        own_norm.astype(F32) + total + b_down.astype(F32), gain2, shift2
    ).astype(BF16)
    return (result.reshape(req_dev, suf, width), new_caches)


def solution(mesh):
    in_specs = (
        P(("owner", "blk"), None, None),
        P(None, None, "blk"),
        P("blk", None),
        P(),
        P(),
        P(),
        P(None, "blk"),
        P("blk"),
        P("blk", None),
        P(),
        P(),
        P(),
        P(None, None, "owner", "blk"),
        P(None, "owner", None, "blk"),
        P(),
        P(),
        P(),
        P(),
        P("owner"),
    )
    out_specs = (P(("owner", "blk"), None, None), P(None, "owner", None, "blk"))
    return jax.shard_map(
        on_device, mesh=mesh, in_specs=in_specs, out_specs=out_specs, check_vma=False
    )
```

```python
import functools

import jax
import jax.numpy as jnp
from jax import lax
from jax.experimental import pallas as pl
from jax.experimental.pallas import tpu as pltpu
from jax.sharding import PartitionSpec as P

F32 = jnp.float32
BF16 = jnp.bfloat16
I32 = jnp.int32

HD = 64
LANES = 128
N_BLK = 8
NX, NY, NZ = 4, 8, 2
PEERS = NX * NY
SLOTS = 2 * NZ
HALF = 16
CHUNK = 4
NEG = -1e30
EPS = 1e-05


def layer_norm(values, gain, shift):
    center = values - jnp.mean(values, axis=-1, keepdims=True)
    spread = jnp.mean(center * center, axis=-1, keepdims=True)
    return center * lax.rsqrt(spread + EPS) * gain.astype(F32) + shift.astype(F32)


def xor_pairs(count, bits):
    return [(i, i ^ bits) for i in range(count)]


def dot_nt(a, b):
    return lax.dot_general(a, b, (((1,), (1,)), ((), ())), preferred_element_type=F32)


def dot_nn(a, b):
    return lax.dot_general(a, b, (((1,), (0,)), ((), ())), preferred_element_type=F32)


def both_heads(q):
    lane = lax.broadcasted_iota(I32, q.shape, 1)
    zero = jnp.zeros_like(q)
    return jnp.concatenate([jnp.where(lane < HD, q, zero), jnp.where(lane < HD, zero, q)], axis=0)


def by_head(stacked):
    rows = stacked.shape[0] // 2
    lane = lax.broadcasted_iota(I32, (rows, LANES), 1)
    first = jnp.broadcast_to(stacked[:rows], (rows, LANES))
    second = jnp.broadcast_to(stacked[rows:], (rows, LANES))
    return jnp.where(lane < HD, first, second)


def table_kernel(
    coords, leaf_of, parent, place, length, dst_b, dst_l, pos, lens, members, valid, chunk_tenant, used, tenant_of, count
):
    my_z, my_x, my_y, blk = (coords[i] for i in range(4))
    reqs = leaf_of.shape[0]
    req_dev = reqs // N_BLK
    tenants = count.shape[0]

    def slot_index(slot):
        owner = slot // 2
        return (owner % PEERS) * SLOTS + ((owner // PEERS) ^ my_z) * 2 + slot % 2

    for t in range(tenants):
        count[t] = 0

    def first_pass(r, _):
        leaf = leaf_of[r]
        branch = parent[leaf]
        tenant = parent[branch]
        dst_b[r] = slot_index(place[branch])
        dst_l[r] = slot_index(place[leaf])
        rel = (r // req_dev) ^ blk
        pos[r] = ((rel % 2) * (N_BLK // 2) + rel // 2) * req_dev + r % req_dev
        tenant_of[r] = tenant
        count[tenant] = count[tenant] + 1
        return 0

    lax.fori_loop(0, reqs, first_pass, 0)

    def clear(i, _):
        members[i] = 0
        valid[i] = 0
        return 0

    lax.fori_loop(0, members.shape[0], clear, 0)
    end = 0
    for t in range(tenants):
        chunks = (count[t] + CHUNK - 1) // CHUNK

        def name(c, _, t=t):
            chunk_tenant[c] = t
            return 0

        lax.fori_loop(end, end + chunks, name, 0)
        count[t] = end * CHUNK
        end = end + chunks
    used[0] = end

    def second_pass(r, _):
        tenant = tenant_of[r]
        seat = count[tenant]
        count[tenant] = seat + 1
        members[seat] = pos[r]
        valid[seat] = 1
        return 0

    lax.fori_loop(0, reqs, second_pass, 0)

    def node(n, _):
        slot = place[n]
        owner = slot // 2

        @pl.when(owner % PEERS == my_x * NY + my_y)
        def _():
            lens[((owner // PEERS) ^ my_z) * 2 + slot % 2] = length[n]

        return 0

    lax.fori_loop(0, place.shape[0], node, 0)


def make_tables(coords, leaf_of, parent, place, length, tenants):
    reqs = leaf_of.shape[0]
    max_chunks = reqs // CHUNK + tenants - 1
    smem = pl.BlockSpec(memory_space=pltpu.SMEM)
    sizes = (reqs, reqs, reqs, SLOTS, max_chunks * CHUNK, max_chunks * CHUNK, max_chunks, 1)
    return pl.pallas_call(
        table_kernel,
        out_shape=tuple(jax.ShapeDtypeStruct((n,), I32) for n in sizes),
        in_specs=[smem] * 5,
        out_specs=(smem,) * len(sizes),
        scratch_shapes=[pltpu.SMEM((reqs,), I32), pltpu.SMEM((tenants,), I32)],
        cost_estimate=pl.CostEstimate(flops=1 << 20, bytes_accessed=1 << 12, transcendentals=0),
    )(coords, leaf_of, parent, place, length)


def query_kernel(pos, dst_b, dst_l, half_ref, near_ref, other_ref, w_ref, after_ref, q_ref, out_ref):
    del after_ref
    reqs, suf, cols = q_ref.shape
    out_ref[...] = jnp.zeros_like(out_ref)
    weights = w_ref[...]
    at = 0
    for ref in (half_ref, near_ref, other_ref):
        rows = ref[...].reshape(-1, ref.shape[-1])
        q = dot_nn(rows, weights).astype(BF16).astype(F32) * HD**-0.5
        count = rows.shape[0] // suf
        q_ref[at : at + count] = q.astype(BF16).reshape(count, suf, cols)
        at += count

    def body(r, _):
        tile = q_ref[pos[r]]
        out_ref[dst_b[r]] = tile
        out_ref[dst_l[r]] = tile
        return 0

    lax.fori_loop(0, reqs, body, 0, unroll=2)


def query_and_route(pos, dst_b, dst_l, half, near, other, w, suf, after):
    reqs = pos.shape[0]
    vmem = pl.BlockSpec(memory_space=pltpu.VMEM)
    return pl.pallas_call(
        query_kernel,
        out_shape=(
            jax.ShapeDtypeStruct((reqs, suf, LANES), BF16),
            jax.ShapeDtypeStruct((PEERS * SLOTS, suf, LANES), BF16),
        ),
        in_specs=[pl.BlockSpec(memory_space=pltpu.SMEM)] * 3
        + [vmem] * 4
        + [pl.BlockSpec(memory_space=pl.ANY)],
        out_specs=(vmem, vmem),
        compiler_params=pltpu.CompilerParams(vmem_limit_bytes=24 << 20),
        cost_estimate=pl.CostEstimate(flops=1 << 28, bytes_accessed=4 << 20, transcendentals=0),
    )(pos, dst_b, dst_l, half, near, other, w, after)


def pack_kernel(up_ref, down_ref, bias_ref, after_ref, out_ref):
    del after_ref
    width = up_ref.shape[0]
    units = out_ref.shape[2]
    for j in range(2):
        own = slice(j * units, (j + 1) * units)
        out_ref[j, :width] = up_ref[:, own]
        for i in range(width // units):
            out_ref[j, width + i * units : width + (i + 1) * units] = down_ref[
                own, i * units : (i + 1) * units
            ]
        bias = jnp.broadcast_to(bias_ref[:, own].astype(F32), (16, units))
        out_ref[j, 2 * width :] = bias.astype(BF16)


def pack_weights(up, down, bias, after):
    width, units = up.shape
    vmem = pl.BlockSpec(memory_space=pltpu.VMEM)
    return pl.pallas_call(
        pack_kernel,
        out_shape=jax.ShapeDtypeStruct((2, 2 * width + 16, units // 2), BF16),
        in_specs=[vmem] * 3 + [pl.BlockSpec(memory_space=pl.ANY)],
        out_specs=vmem,
        compiler_params=pltpu.CompilerParams(vmem_limit_bytes=16 << 20),
        cost_estimate=pl.CostEstimate(flops=0, bytes_accessed=4 << 20, transcendentals=0),
    )(up, down, bias.reshape(1, units), after)


def node_kernel(lens, q_ref, cache_ref, after_ref, out_ref):
    del after_ref
    peers, slots, suf, _ = q_ref.shape
    group = 4
    rows = group * suf
    node_max = cache_ref.shape[3]
    out_ref[:, 2 * SLOTS] = jnp.zeros((peers, HALF, LANES), BF16)

    def one_slot(slot, _):
        keys = both_heads(cache_ref[slot // 2, 0, slot % 2])
        values = cache_ref[slot // 2, 1, slot % 2]
        values = jnp.concatenate([both_heads(values), both_heads(jnp.ones_like(values))], axis=1)
        keep = lax.broadcasted_iota(I32, (1, node_max), 1) < lens[slot]
        lane = lax.broadcasted_iota(I32, (group, HALF, LANES), 2)
        piece = lane % (HD // 2) - 3 * slot
        for g in range(peers // group):
            part = slice(g * group, (g + 1) * group)
            q = q_ref[part, slot].reshape(rows, LANES)
            scores = dot_nt(q, keys)
            weights, peaks = [], []
            for h in range(2):
                own = jnp.where(keep, scores[:, h * node_max : (h + 1) * node_max], NEG)
                peak = jnp.max(own, axis=1, keepdims=True)
                weights.append(jnp.exp(own - peak).astype(BF16))
                peaks.append(peak)
            mixed = dot_nn(jnp.concatenate(weights, axis=1), values)
            total = mixed[:, LANES:]
            mass = by_head(jnp.concatenate(peaks, axis=0)) + jnp.log(total)
            out = (mixed[:, :LANES] / total).astype(BF16).reshape(group, 2, HALF, LANES)
            out_ref[part, 2 * slot] = out[:, 0]
            out_ref[part, 2 * slot + 1] = out[:, 1]
            mass = mass.reshape(group, 2, HALF, LANES)
            mass = jnp.where(lane % HD < HD // 2, mass[:, 0], mass[:, 1])
            high = mass.astype(BF16).astype(F32)
            rest = mass - high
            mid = rest.astype(BF16).astype(F32)
            sent = jnp.where(piece == 0, high, jnp.where(piece == 1, mid, rest - mid))
            held = out_ref[part, 2 * SLOTS].astype(F32)
            held = jnp.where((piece >= 0) & (piece < 3), sent, held)
            out_ref[part, 2 * SLOTS] = held.astype(BF16)
        return 0

    lax.fori_loop(0, slots, one_slot, 0)


def node_attention(lens, queries, caches, after):
    peers, slots, suf, _ = queries.shape
    vmem = pl.BlockSpec(memory_space=pltpu.VMEM)
    return pl.pallas_call(
        node_kernel,
        out_shape=jax.ShapeDtypeStruct((peers, 2 * slots + 1, HALF, LANES), BF16),
        in_specs=[
            pl.BlockSpec(memory_space=pltpu.SMEM),
            vmem,
            vmem,
            pl.BlockSpec(memory_space=pl.ANY),
        ],
        out_specs=vmem,
        compiler_params=pltpu.CompilerParams(vmem_limit_bytes=24 << 20),
        cost_estimate=pl.CostEstimate(
            flops=2 << 30, bytes_accessed=4 << 20, transcendentals=4 << 20
        ),
    )(lens, queries, caches, after)


def root_kernel(
    used, members, valid, chunk_tenant, root_len, coords, q_ref, k_ref, v_ref, root_ref, out_ref, mass_ref
):
    suf = q_ref.shape[1]
    rows = CHUNK * suf
    root_rows = NY * NZ * NX * root_ref.shape[5]
    per = root_ref.shape[5]

    def body(c, _):
        tenant = chunk_tenant[c]
        where_ = [members[c * CHUNK + j] for j in range(CHUNK)]
        q = both_heads(jnp.concatenate([q_ref[w] for w in where_], axis=0))
        own_k = jnp.concatenate([k_ref[w] for w in where_], axis=0)
        own_v = jnp.concatenate([v_ref[w] for w in where_], axis=0)
        keys = root_ref[:, :, :, 0, tenant].reshape(root_rows, LANES)
        values = root_ref[:, :, :, 1, tenant].reshape(root_rows, LANES)
        n = lax.broadcasted_iota(I32, (1, root_rows), 1)
        row = n % per
        z = ((n // per) % NZ) ^ coords[0]
        x_side = (n // (per * NZ)) % 2
        y = (n // (per * NZ * 2)) % NY
        x = (n // (per * NZ * 2 * NY) * 2 + coords[1]) ^ x_side
        place = ((z * NX + x) * NY + y) * per + row
        scores = jnp.where(place < root_len[tenant], dot_nt(q, keys), NEG)
        own_row = (lax.broadcasted_iota(I32, (2 * rows, rows), 0) % rows) // suf
        own_col = lax.broadcasted_iota(I32, (2 * rows, rows), 1) // suf
        own = jnp.where(own_row == own_col, dot_nt(q, own_k), NEG)
        peak = jnp.maximum(
            jnp.max(scores, axis=1, keepdims=True), jnp.max(own, axis=1, keepdims=True)
        )
        weights = jnp.exp(scores - peak)
        own_weights = jnp.exp(own - peak)
        total = jnp.sum(weights, axis=1, keepdims=True) + jnp.sum(
            own_weights, axis=1, keepdims=True
        )
        mixed = dot_nn(weights.astype(BF16), values) + dot_nn(own_weights.astype(BF16), own_v)
        out = by_head(mixed) / by_head(total)
        mass = by_head(peak + jnp.log(total))
        for j in range(CHUNK):

            @pl.when(valid[c * CHUNK + j] > 0)
            def _(j=j):
                out_ref[where_[j]] = out[j * suf : (j + 1) * suf]
                mass_ref[where_[j]] = mass[j * suf : (j + 1) * suf]

        return 0

    lax.fori_loop(0, used[0], body, 0)


def root_attention(used, members, valid, chunk_tenant, root_len, coords, q, k, v, roots):
    reqs, suf, _ = q.shape
    shape = jax.ShapeDtypeStruct((reqs, suf, LANES), F32)
    vmem = pl.BlockSpec(memory_space=pltpu.VMEM)
    return pl.pallas_call(
        root_kernel,
        out_shape=(shape, shape),
        in_specs=[pl.BlockSpec(memory_space=pltpu.SMEM)] * 6 + [vmem] * 4,
        out_specs=(vmem, vmem),
        compiler_params=pltpu.CompilerParams(vmem_limit_bytes=40 << 20),
        cost_estimate=pl.CostEstimate(
            flops=4 << 30, bytes_accessed=4 << 20, transcendentals=4 << 20
        ),
    )(used, members, valid, chunk_tenant, root_len, coords, q, k, v, roots)


def merge_kernel(pos, dst_b, dst_l, back_ref, out_ref, mass_ref, send_ref, node_mass):
    reqs, suf, _ = out_ref.shape
    per_block = reqs // N_BLK
    src = lax.broadcasted_iota(I32, (LANES, LANES), 0)
    dst = lax.broadcasted_iota(I32, (LANES, LANES), 1)
    packed = back_ref[:, 2 * SLOTS].reshape(PEERS * HALF, LANES)
    for s in range(SLOTS):
        for g in range(2):
            hit = (src // HD == dst // HD) & ((src % HD) // (HD // 2) == g)
            hit = hit & ((src % (HD // 2)) // 3 == s)
            pick = jnp.where(hit, 1.0, 0.0).astype(BF16)
            node_mass[:, s, g] = dot_nn(packed, pick).reshape(PEERS, HALF, LANES)

    def body(r, _):
        here = pos[r]
        outs = [out_ref[here]]
        masses = [mass_ref[here]]
        for table in (dst_b, dst_l):
            peer = table[r] // SLOTS
            slot = table[r] % SLOTS
            outs.append(back_ref[peer, pl.ds(2 * slot, 2)].astype(F32).reshape(suf, LANES))
            masses.append(node_mass[peer, slot].reshape(suf, LANES))
        top = jnp.maximum(jnp.maximum(masses[0], masses[1]), masses[2])
        parts = [jnp.exp(m - top) for m in masses]
        total = parts[0] + parts[1] + parts[2]
        attn = (parts[0] * outs[0] + parts[1] * outs[1] + parts[2] * outs[2]) / total
        attn = attn.astype(BF16)
        block = r // per_block
        send_ref[block, 0, r % per_block] = attn
        send_ref[(block + N_BLK // 2) % N_BLK, 1, r % per_block] = attn
        return 0

    lax.fori_loop(0, reqs, body, 0, unroll=2)


def merge(pos, dst_b, dst_l, back, out, mass):
    reqs, suf, _ = out.shape
    vmem = pl.BlockSpec(memory_space=pltpu.VMEM)
    return pl.pallas_call(
        merge_kernel,
        out_shape=jax.ShapeDtypeStruct((N_BLK, 2, reqs // N_BLK, suf, LANES), BF16),
        in_specs=[pl.BlockSpec(memory_space=pltpu.SMEM)] * 3 + [vmem] * 3,
        out_specs=vmem,
        scratch_shapes=[pltpu.VMEM((PEERS, SLOTS, 2, HALF, LANES), F32)],
        compiler_params=pltpu.CompilerParams(vmem_limit_bytes=30 << 20),
        cost_estimate=pl.CostEstimate(
            flops=1 << 27, bytes_accessed=4 << 20, transcendentals=1 << 20
        ),
    )(pos, dst_b, dst_l, back, out, mass)


def rows_norm(values, gain, shift):
    center = values - jnp.mean(values, axis=1, keepdims=True)
    spread = jnp.mean(center * center, axis=1, keepdims=True)
    return center * lax.rsqrt(spread + EPS) * gain + shift


def feed_kernel(attn_ref, w_out_ref, tok_a, tok_b, vec_ref, w0, w1, w2, w3, w4, w5, norm_ref, own_ref, far_ref):
    rows = tok_a.shape[0]
    width = tok_a.shape[1]
    attn = jnp.concatenate([attn_ref[h] for h in range(N_BLK)], axis=1)
    tok = jnp.concatenate([tok_a[...], tok_b[...]], axis=0).astype(F32)
    vec = vec_ref[...].astype(F32)
    mixed = tok + dot_nn(attn, w_out_ref[...]) + vec[0:1]
    norm = rows_norm(mixed, vec[1:2], vec[2:3]).astype(BF16)
    norm_ref[...] = norm[:rows]
    total = jnp.zeros((2 * rows, width), F32)
    units = w0.shape[-1]
    for w in [ref.at[i] for ref in (w0, w1) for i in range(2)] + [w2, w3, w4, w5]:
        bias = w[width + units * (width // units) :].astype(F32)[0:1]
        inner = dot_nn(norm, w[:width]) + bias
        hidden = (0.5 * inner * (1.0 + lax.erf(inner * (0.5**0.5)))).astype(BF16)
        down = [
            dot_nn(hidden, w[width + i * units : width + (i + 1) * units])
            for i in range(width // units)
        ]
        total = total + jnp.concatenate(down, axis=1)
    own_ref[...] = total[:rows]
    far_ref[...] = total[rows:].astype(BF16)


def feed_forward(attn, w_out, tok_a, tok_b, vectors, packs):
    rows, width = tok_a.shape
    vmem = pl.BlockSpec(memory_space=pltpu.VMEM)
    return pl.pallas_call(
        feed_kernel,
        out_shape=(
            jax.ShapeDtypeStruct((rows, width), BF16),
            jax.ShapeDtypeStruct((rows, width), F32),
            jax.ShapeDtypeStruct((rows, width), BF16),
        ),
        in_specs=[vmem] * (5 + len(packs)),
        out_specs=(vmem, vmem, vmem),
        compiler_params=pltpu.CompilerParams(vmem_limit_bytes=48 << 20),
        cost_estimate=pl.CostEstimate(
            flops=3 << 30, bytes_accessed=12 << 20, transcendentals=1 << 20
        ),
    )(attn, w_out, tok_a, tok_b, vectors, *packs)


def on_device(
    tokens,
    w_qkv,
    w_out,
    b_out,
    gain1,
    shift1,
    w_up,
    b_up,
    w_down,
    b_down,
    gain2,
    shift2,
    root_cache,
    node_cache,
    root_len,
    node_len,
    node_parent,
    node_place,
    req_leaf,
):
    req_dev, suf, width = tokens.shape
    cols = w_qkv.shape[2]
    own_rows = req_dev * suf
    reqs = req_leaf.shape[0]
    node_max = node_cache.shape[2]
    tenants = root_cache.shape[1]
    root_per = root_cache.shape[2]
    blk = lax.axis_index("blk")
    owner = lax.axis_index("owner")
    my_z = owner // (NX * NY)
    my_x = (owner // NY) % NX
    my_y = owner % NY
    swap = xor_pairs(N_BLK, 1)
    n_own = N_BLK // 2

    def zero_after(value):
        flat = value.reshape(-1, value.shape[-1])
        return jnp.minimum(jnp.abs(flat[:1, :1]), 0)

    coords = jnp.stack([my_z, my_x, my_y, blk]).astype(I32)
    dst_b, dst_l, pos, lens, members, valid, chunk_tenant, used = make_tables(
        coords, req_leaf, node_parent, node_place, node_len, tenants
    )

    tok = tokens.reshape(own_rows, width)
    near = lax.ppermute(tok, "blk", swap)
    half = [lax.ppermute(tok, "blk", xor_pairs(N_BLK, 2 * k)) for k in range(1, n_own)]
    tok_far, last_come = half[1], half[2]

    n_owner = NX * NY * NZ
    roots = root_cache.reshape(-1, LANES)
    roots = jnp.stack([roots, lax.ppermute(roots, "owner", xor_pairs(n_owner, NX * NY))])
    roots = jnp.stack([roots, lax.ppermute(roots, "owner", xor_pairs(n_owner, NY))])
    roots = roots + zero_after(last_come)
    groups = [
        [(z * NX + parity + 2 * i) * NY + y for i in range(NX // 2) for y in range(NY)]
        for z in range(NZ)
        for parity in range(2)
    ]
    roots = lax.all_gather(roots, "owner", axis=0, tiled=False, axis_index_groups=groups)
    planned = zero_after(jnp.broadcast_to(pos[None, :1], (1, 1)).astype(BF16))
    other = lax.ppermute(jnp.stack(half) + planned, "blk", swap)
    half = jnp.stack([tok] + half)
    roots = roots.reshape(NX // 2 * NY, 2, NZ, 2, tenants, root_per, LANES)

    node_rows = node_cache.reshape(-1, LANES) + zero_after(last_come)
    node_far = lax.ppermute(node_rows, "owner", xor_pairs(n_owner, NX * NY))
    caches = jnp.stack([node_rows, node_far]).reshape(NZ, 2, 2, node_max, LANES)

    w_out_all = lax.all_gather(w_out + zero_after(last_come), "blk", axis=0, tiled=True)
    packs = pack_weights(w_up, w_down, b_up, last_come)
    pack_side = lax.ppermute(packs, "blk", swap)

    q, outgoing = query_and_route(pos, dst_b, dst_l, half, near, other, w_qkv[:, 0], suf, last_come)
    outgoing = outgoing.reshape(PEERS, SLOTS, suf, cols)

    def project(which):
        w = w_qkv[:, which]
        out = jnp.concatenate(
            [
                jnp.dot(part.reshape(-1, width), w, preferred_element_type=F32)
                for part in (half, near, other)
            ]
        )
        return out.astype(BF16).reshape(reqs, suf, cols)

    groups = [[z * PEERS + p for p in range(PEERS)] for z in range(NZ)]
    incoming = lax.all_to_all(
        outgoing, "owner", split_axis=0, concat_axis=0, axis_index_groups=groups, tiled=True
    )
    k_new = project(1)
    v_new = project(2)
    order = jnp.arange(N_BLK, dtype=I32) ^ blk
    order = (order % 2) * n_own + order // 2
    new_caches = jnp.stack([k_new, v_new]).reshape(2, N_BLK, req_dev, suf, cols)
    new_caches = jnp.take(new_caches, order, axis=1).reshape(2, reqs, suf, cols)

    answers = node_attention(lens, incoming, caches, packs)
    z_chips = NZ * n_own

    def to_neighbour(step):
        pairs = []
        for dev in range(n_owner * N_BLK):
            b, own = dev // n_owner, dev % n_owner
            z = (own // PEERS * n_own + b // 2 + step) % z_chips
            pairs.append((dev, (z % n_own * 2 + b % 2) * n_owner + z // n_own * PEERS + own % PEERS))
        part = ((blk // 2 + step + n_own) % n_own) // (n_own // 2)
        sent = lax.dynamic_index_in_dim(packs, part, 0, keepdims=False) + zero_after(answers)
        return lax.ppermute(sent, ("blk", "owner"), pairs)

    pack_next = [to_neighbour(1), to_neighbour(-1)]
    pack_last = [lax.ppermute(part, "blk", swap) for part in pack_next]
    parts = [packs, pack_side] + pack_next + pack_last
    back = lax.all_to_all(
        answers, "owner", split_axis=0, concat_axis=0, axis_index_groups=groups, tiled=True
    )
    parity = jnp.stack([my_z, my_x % 2]).astype(I32)
    out, mass = root_attention(
        used, members, valid, chunk_tenant, root_len, parity, q, k_new, v_new, roots
    )
    send = merge(pos, dst_b, dst_l, back, out, mass)
    attn = lax.all_to_all(
        send.reshape(N_BLK, 2 * own_rows, cols), "blk", split_axis=0, concat_axis=0, tiled=True
    )
    vectors = jnp.stack([b_out, gain1, shift1])
    own_norm, down, down_far = feed_forward(attn, w_out_all, tok, tok_far, vectors, parts)
    total = down + lax.ppermute(down_far, "blk", xor_pairs(N_BLK, N_BLK // 2)).astype(F32)
    result = layer_norm(
        own_norm.astype(F32) + total + b_down.astype(F32), gain2, shift2
    ).astype(BF16)
    return (result.reshape(req_dev, suf, width), new_caches)


def solution(mesh):
    in_specs = (
        P(("owner", "blk"), None, None),
        P(None, None, "blk"),
        P("blk", None),
        P(),
        P(),
        P(),
        P(None, "blk"),
        P("blk"),
        P("blk", None),
        P(),
        P(),
        P(),
        P(None, None, "owner", "blk"),
        P(None, "owner", None, "blk"),
        P(),
        P(),
        P(),
        P(),
        P("owner"),
    )
    out_specs = (P(("owner", "blk"), None, None), P(None, "owner", None, "blk"))
    return jax.shard_map(
        on_device, mesh=mesh, in_specs=in_specs, out_specs=out_specs, check_vma=False
    )
```

```python
import functools

import jax
import jax.numpy as jnp
from jax import lax
from jax.experimental import pallas as pl
from jax.experimental.pallas import tpu as pltpu
from jax.sharding import PartitionSpec as P

F32 = jnp.float32
BF16 = jnp.bfloat16
I32 = jnp.int32

HD = 64
LANES = 128
N_BLK = 8
NX, NY, NZ = 4, 8, 2
PEERS = NX * NY
SLOTS = 2 * NZ
HALF = 16
CHUNK = 4
NEG = -1e30
EPS = 1e-05


def layer_norm(values, gain, shift):
    center = values - jnp.mean(values, axis=-1, keepdims=True)
    spread = jnp.mean(center * center, axis=-1, keepdims=True)
    return center * lax.rsqrt(spread + EPS) * gain.astype(F32) + shift.astype(F32)


def xor_pairs(count, bits):
    return [(i, i ^ bits) for i in range(count)]


def dot_nt(a, b):
    return lax.dot_general(a, b, (((1,), (1,)), ((), ())), preferred_element_type=F32)


def dot_nn(a, b):
    return lax.dot_general(a, b, (((1,), (0,)), ((), ())), preferred_element_type=F32)


def both_heads(q):
    lane = lax.broadcasted_iota(I32, q.shape, 1)
    zero = jnp.zeros_like(q)
    return jnp.concatenate([jnp.where(lane < HD, q, zero), jnp.where(lane < HD, zero, q)], axis=0)


def by_head(stacked):
    rows = stacked.shape[0] // 2
    lane = lax.broadcasted_iota(I32, (rows, LANES), 1)
    first = jnp.broadcast_to(stacked[:rows], (rows, LANES))
    second = jnp.broadcast_to(stacked[rows:], (rows, LANES))
    return jnp.where(lane < HD, first, second)


DST_B, DST_L, POS, LENS, USED, ROOT_LEN, PLACE, TENANT, MEMBERS, VALID, COUNT, CHUNK_TENANT, TABLE = (
    0, 32, 64, 96, 100, 104, 112, 128, 160, 208, 256, 264, 288,
)


def table_kernel(coords, leaf_of, parent, place, length, root_len, out):
    my_z, my_x, my_y, blk = (coords[i] for i in range(4))
    reqs = leaf_of.shape[0]
    req_dev = reqs // N_BLK
    tenants = root_len.shape[0]
    seats = (reqs // CHUNK + tenants - 1) * CHUNK

    def slot_index(slot):
        owner = slot >> 1
        return (owner & (PEERS - 1)) * SLOTS + (((owner // PEERS) ^ my_z) << 1) + (slot & 1)

    for t in range(tenants):
        out[COUNT + t] = 0
        out[ROOT_LEN + t] = root_len[t]
    out[PLACE] = my_z
    out[PLACE + 1] = my_x

    def first_pass(r, _):
        leaf = leaf_of[r]
        branch = parent[leaf]
        tenant = parent[branch]
        out[DST_B + r] = slot_index(place[branch])
        out[DST_L + r] = slot_index(place[leaf])
        rel = (r // req_dev) ^ blk
        out[POS + r] = ((rel & 1) * (N_BLK // 2) + (rel >> 1)) * req_dev + (r & (req_dev - 1))
        out[TENANT + r] = tenant
        out[COUNT + tenant] = out[COUNT + tenant] + 1
        return 0

    lax.fori_loop(0, reqs, first_pass, 0, unroll=4)

    def clear(i, _):
        out[MEMBERS + i] = 0
        out[VALID + i] = 0
        return 0

    lax.fori_loop(0, seats, clear, 0, unroll=4)
    end = 0
    for t in range(tenants):
        chunks = (out[COUNT + t] + CHUNK - 1) // CHUNK

        def name(c, _, t=t):
            out[CHUNK_TENANT + c] = t
            return 0

        lax.fori_loop(end, end + chunks, name, 0)
        out[COUNT + t] = end * CHUNK
        end = end + chunks
    out[USED] = end

    def second_pass(r, _):
        tenant = out[TENANT + r]
        seat = out[COUNT + tenant]
        out[COUNT + tenant] = seat + 1
        out[MEMBERS + seat] = out[POS + r]
        out[VALID + seat] = 1
        return 0

    lax.fori_loop(0, reqs, second_pass, 0, unroll=4)

    def node(n, _):
        slot = place[n]
        owner = slot >> 1

        @pl.when((owner & (PEERS - 1)) == my_x * NY + my_y)
        def _():
            out[LENS + (((owner // PEERS) ^ my_z) << 1) + (slot & 1)] = length[n]

        return 0

    lax.fori_loop(0, place.shape[0], node, 0, unroll=4)


def make_tables(coords, leaf_of, parent, place, length, root_len):
    smem = pl.BlockSpec(memory_space=pltpu.SMEM)
    return pl.pallas_call(
        table_kernel,
        out_shape=jax.ShapeDtypeStruct((TABLE,), I32),
        in_specs=[smem] * 6,
        out_specs=smem,
        cost_estimate=pl.CostEstimate(flops=1 << 20, bytes_accessed=1 << 12, transcendentals=0),
    )(coords, leaf_of, parent, place, length, root_len)


def query_kernel(tab, half_ref, near_ref, other_ref, w_ref, after_ref, q_ref, out_ref):
    del after_ref
    reqs, suf, cols = q_ref.shape
    out_ref[...] = jnp.zeros_like(out_ref)
    weights = w_ref[...]
    at = 0
    for ref in (half_ref, near_ref, other_ref):
        rows = ref[...].reshape(-1, ref.shape[-1])
        q = dot_nn(rows, weights).astype(BF16).astype(F32) * HD**-0.5
        count = rows.shape[0] // suf
        q_ref[at : at + count] = q.astype(BF16).reshape(count, suf, cols)
        at += count

    def body(r, _):
        tile = q_ref[tab[POS + r]]
        out_ref[tab[DST_B + r]] = tile
        out_ref[tab[DST_L + r]] = tile
        return 0

    lax.fori_loop(0, reqs, body, 0, unroll=2)


def query_and_route(tab, half, near, other, w, suf, after):
    reqs = (half.size + near.size + other.size) // (suf * half.shape[-1])
    vmem = pl.BlockSpec(memory_space=pltpu.VMEM)
    return pl.pallas_call(
        query_kernel,
        out_shape=(
            jax.ShapeDtypeStruct((reqs, suf, LANES), BF16),
            jax.ShapeDtypeStruct((PEERS * SLOTS, suf, LANES), BF16),
        ),
        in_specs=[pl.BlockSpec(memory_space=pltpu.SMEM)]
        + [vmem] * 4
        + [pl.BlockSpec(memory_space=pl.ANY)],
        out_specs=(vmem, vmem),
        compiler_params=pltpu.CompilerParams(vmem_limit_bytes=24 << 20),
        cost_estimate=pl.CostEstimate(flops=1 << 28, bytes_accessed=4 << 20, transcendentals=0),
    )(tab, half, near, other, w, after)


def pack_kernel(up_ref, down_ref, bias_ref, after_ref, out_ref):
    del after_ref
    width = up_ref.shape[0]
    units = out_ref.shape[2]
    for j in range(2):
        own = slice(j * units, (j + 1) * units)
        out_ref[j, :width] = up_ref[:, own]
        for i in range(width // units):
            out_ref[j, width + i * units : width + (i + 1) * units] = down_ref[
                own, i * units : (i + 1) * units
            ]
        bias = jnp.broadcast_to(bias_ref[:, own].astype(F32), (16, units))
        out_ref[j, 2 * width :] = bias.astype(BF16)


def pack_weights(up, down, bias, after):
    width, units = up.shape
    vmem = pl.BlockSpec(memory_space=pltpu.VMEM)
    return pl.pallas_call(
        pack_kernel,
        out_shape=jax.ShapeDtypeStruct((2, 2 * width + 16, units // 2), BF16),
        in_specs=[vmem] * 3 + [pl.BlockSpec(memory_space=pl.ANY)],
        out_specs=vmem,
        compiler_params=pltpu.CompilerParams(vmem_limit_bytes=16 << 20),
        cost_estimate=pl.CostEstimate(flops=0, bytes_accessed=4 << 20, transcendentals=0),
    )(up, down, bias.reshape(1, units), after)


def node_kernel(tab, q_ref, cache_ref, after_ref, out_ref):
    del after_ref
    peers, slots, suf, _ = q_ref.shape
    group = 4
    rows = group * suf
    node_max = cache_ref.shape[3]
    out_ref[:, 2 * SLOTS] = jnp.zeros((peers, HALF, LANES), BF16)

    def one_slot(slot, _):
        keys = both_heads(cache_ref[slot // 2, 0, slot % 2])
        values = cache_ref[slot // 2, 1, slot % 2]
        values = jnp.concatenate([both_heads(values), both_heads(jnp.ones_like(values))], axis=1)
        keep = lax.broadcasted_iota(I32, (1, node_max), 1) < tab[LENS + slot]
        lane = lax.broadcasted_iota(I32, (group, HALF, LANES), 2)
        piece = lane % (HD // 2) - 3 * slot
        for g in range(peers // group):
            part = slice(g * group, (g + 1) * group)
            q = q_ref[part, slot].reshape(rows, LANES)
            scores = dot_nt(q, keys)
            weights, peaks = [], []
            for h in range(2):
                own = jnp.where(keep, scores[:, h * node_max : (h + 1) * node_max], NEG)
                peak = jnp.max(own, axis=1, keepdims=True)
                weights.append(jnp.exp(own - peak).astype(BF16))
                peaks.append(peak)
            mixed = dot_nn(jnp.concatenate(weights, axis=1), values)
            total = mixed[:, LANES:]
            mass = by_head(jnp.concatenate(peaks, axis=0)) + jnp.log(total)
            out = (mixed[:, :LANES] / total).astype(BF16).reshape(group, 2, HALF, LANES)
            out_ref[part, 2 * slot] = out[:, 0]
            out_ref[part, 2 * slot + 1] = out[:, 1]
            mass = mass.reshape(group, 2, HALF, LANES)
            mass = jnp.where(lane % HD < HD // 2, mass[:, 0], mass[:, 1])
            high = mass.astype(BF16).astype(F32)
            rest = mass - high
            mid = rest.astype(BF16).astype(F32)
            sent = jnp.where(piece == 0, high, jnp.where(piece == 1, mid, rest - mid))
            held = out_ref[part, 2 * SLOTS].astype(F32)
            held = jnp.where((piece >= 0) & (piece < 3), sent, held)
            out_ref[part, 2 * SLOTS] = held.astype(BF16)
        return 0

    lax.fori_loop(0, slots, one_slot, 0)


def node_attention(tab, queries, caches, after):
    peers, slots, suf, _ = queries.shape
    vmem = pl.BlockSpec(memory_space=pltpu.VMEM)
    return pl.pallas_call(
        node_kernel,
        out_shape=jax.ShapeDtypeStruct((peers, 2 * slots + 1, HALF, LANES), BF16),
        in_specs=[
            pl.BlockSpec(memory_space=pltpu.SMEM),
            vmem,
            vmem,
            pl.BlockSpec(memory_space=pl.ANY),
        ],
        out_specs=vmem,
        compiler_params=pltpu.CompilerParams(vmem_limit_bytes=24 << 20),
        cost_estimate=pl.CostEstimate(
            flops=2 << 30, bytes_accessed=4 << 20, transcendentals=4 << 20
        ),
    )(tab, queries, caches, after)


def root_kernel(tab, q_ref, k_ref, v_ref, root_ref, out_ref, mass_ref):
    suf = q_ref.shape[1]
    rows = CHUNK * suf
    per = root_ref.shape[5]
    root_rows = NY * NZ * NX * per

    def body(c, _):
        tenant = tab[CHUNK_TENANT + c]
        where_ = [tab[MEMBERS + c * CHUNK + j] for j in range(CHUNK)]
        q = both_heads(jnp.concatenate([q_ref[w] for w in where_], axis=0))
        own_k = jnp.concatenate([k_ref[w] for w in where_], axis=0)
        own_v = jnp.concatenate([v_ref[w] for w in where_], axis=0)
        keys = root_ref[:, :, :, 0, tenant].reshape(root_rows, LANES)
        values = root_ref[:, :, :, 1, tenant].reshape(root_rows, LANES)
        n = lax.broadcasted_iota(I32, (1, root_rows), 1)
        row = n % per
        z = ((n // per) % NZ) ^ tab[PLACE]
        x = (n // (per * NZ)) % NX
        y = n // (per * NZ * NX)
        place = ((z * NX + x) * NY + y) * per + row
        scores = jnp.where(place < tab[ROOT_LEN + tenant], dot_nt(q, keys), NEG)
        own_row = (lax.broadcasted_iota(I32, (2 * rows, rows), 0) % rows) // suf
        own_col = lax.broadcasted_iota(I32, (2 * rows, rows), 1) // suf
        own = jnp.where(own_row == own_col, dot_nt(q, own_k), NEG)
        peak = jnp.maximum(
            jnp.max(scores, axis=1, keepdims=True), jnp.max(own, axis=1, keepdims=True)
        )
        weights = jnp.exp(scores - peak)
        own_weights = jnp.exp(own - peak)
        total = jnp.sum(weights, axis=1, keepdims=True) + jnp.sum(
            own_weights, axis=1, keepdims=True
        )
        mixed = dot_nn(weights.astype(BF16), values) + dot_nn(own_weights.astype(BF16), own_v)
        out = by_head(mixed) / by_head(total)
        mass = by_head(peak + jnp.log(total))
        for j in range(CHUNK):

            @pl.when(tab[VALID + c * CHUNK + j] > 0)
            def _(j=j):
                out_ref[where_[j]] = out[j * suf : (j + 1) * suf]
                mass_ref[where_[j]] = mass[j * suf : (j + 1) * suf]

        return 0

    lax.fori_loop(0, tab[USED], body, 0)


def root_attention(tab, q, k, v, roots):
    reqs, suf, _ = q.shape
    shape = jax.ShapeDtypeStruct((reqs, suf, LANES), F32)
    vmem = pl.BlockSpec(memory_space=pltpu.VMEM)
    return pl.pallas_call(
        root_kernel,
        out_shape=(shape, shape),
        in_specs=[pl.BlockSpec(memory_space=pltpu.SMEM)] + [vmem] * 4,
        out_specs=(vmem, vmem),
        compiler_params=pltpu.CompilerParams(vmem_limit_bytes=40 << 20),
        cost_estimate=pl.CostEstimate(
            flops=4 << 30, bytes_accessed=4 << 20, transcendentals=4 << 20
        ),
    )(tab, q, k, v, roots)


def merge_kernel(tab, back_ref, out_ref, mass_ref, send_ref, node_mass):
    reqs, suf, _ = out_ref.shape
    per_block = reqs // N_BLK
    src = lax.broadcasted_iota(I32, (LANES, LANES), 0)
    dst = lax.broadcasted_iota(I32, (LANES, LANES), 1)
    packed = back_ref[:, 2 * SLOTS].reshape(PEERS * HALF, LANES)
    for s in range(SLOTS):
        for g in range(2):
            hit = (src // HD == dst // HD) & ((src % HD) // (HD // 2) == g)
            hit = hit & ((src % (HD // 2)) // 3 == s)
            pick = jnp.where(hit, 1.0, 0.0).astype(BF16)
            node_mass[:, s, g] = dot_nn(packed, pick).reshape(PEERS, HALF, LANES)

    def body(r, _):
        here = tab[POS + r]
        outs = [out_ref[here]]
        masses = [mass_ref[here]]
        for first in (DST_B, DST_L):
            peer = tab[first + r] // SLOTS
            slot = tab[first + r] % SLOTS
            outs.append(back_ref[peer, pl.ds(2 * slot, 2)].astype(F32).reshape(suf, LANES))
            masses.append(node_mass[peer, slot].reshape(suf, LANES))
        top = jnp.maximum(jnp.maximum(masses[0], masses[1]), masses[2])
        parts = [jnp.exp(m - top) for m in masses]
        total = parts[0] + parts[1] + parts[2]
        attn = (parts[0] * outs[0] + parts[1] * outs[1] + parts[2] * outs[2]) / total
        attn = attn.astype(BF16)
        block = r // per_block
        send_ref[block, 0, r % per_block] = attn
        send_ref[(block + N_BLK // 2) % N_BLK, 1, r % per_block] = attn
        return 0

    lax.fori_loop(0, reqs, body, 0, unroll=2)


def merge(tab, back, out, mass):
    reqs, suf, _ = out.shape
    vmem = pl.BlockSpec(memory_space=pltpu.VMEM)
    return pl.pallas_call(
        merge_kernel,
        out_shape=jax.ShapeDtypeStruct((N_BLK, 2, reqs // N_BLK, suf, LANES), BF16),
        in_specs=[pl.BlockSpec(memory_space=pltpu.SMEM)] + [vmem] * 3,
        out_specs=vmem,
        scratch_shapes=[pltpu.VMEM((PEERS, SLOTS, 2, HALF, LANES), F32)],
        compiler_params=pltpu.CompilerParams(vmem_limit_bytes=30 << 20),
        cost_estimate=pl.CostEstimate(
            flops=1 << 27, bytes_accessed=4 << 20, transcendentals=1 << 20
        ),
    )(tab, back, out, mass)


def rows_norm(values, gain, shift):
    center = values - jnp.mean(values, axis=1, keepdims=True)
    spread = jnp.mean(center * center, axis=1, keepdims=True)
    return center * lax.rsqrt(spread + EPS) * gain + shift


def feed_kernel(attn_ref, w_out_ref, tok_a, tok_b, vec_ref, w0, w1, w2, w3, w4, w5, norm_ref, own_ref, far_ref):
    rows = tok_a.shape[0]
    width = tok_a.shape[1]
    attn = jnp.concatenate([attn_ref[h] for h in range(N_BLK)], axis=1)
    tok = jnp.concatenate([tok_a[...], tok_b[...]], axis=0).astype(F32)
    vec = vec_ref[...].astype(F32)
    mixed = tok + dot_nn(attn, w_out_ref[...]) + vec[0:1]
    norm = rows_norm(mixed, vec[1:2], vec[2:3]).astype(BF16)
    norm_ref[...] = norm[:rows]
    total = jnp.zeros((2 * rows, width), F32)
    units = w0.shape[-1]
    for w in [ref.at[i] for ref in (w0, w1) for i in range(2)] + [w2, w3, w4, w5]:
        bias = w[width + units * (width // units) :].astype(F32)[0:1]
        inner = dot_nn(norm, w[:width]) + bias
        hidden = (0.5 * inner * (1.0 + lax.erf(inner * (0.5**0.5)))).astype(BF16)
        down = [
            dot_nn(hidden, w[width + i * units : width + (i + 1) * units])
            for i in range(width // units)
        ]
        total = total + jnp.concatenate(down, axis=1)
    own_ref[...] = total[:rows]
    far_ref[...] = total[rows:].astype(BF16)


def feed_forward(attn, w_out, tok_a, tok_b, vectors, packs):
    rows, width = tok_a.shape
    vmem = pl.BlockSpec(memory_space=pltpu.VMEM)
    return pl.pallas_call(
        feed_kernel,
        out_shape=(
            jax.ShapeDtypeStruct((rows, width), BF16),
            jax.ShapeDtypeStruct((rows, width), F32),
            jax.ShapeDtypeStruct((rows, width), BF16),
        ),
        in_specs=[vmem] * (5 + len(packs)),
        out_specs=(vmem, vmem, vmem),
        compiler_params=pltpu.CompilerParams(vmem_limit_bytes=48 << 20),
        cost_estimate=pl.CostEstimate(
            flops=3 << 30, bytes_accessed=12 << 20, transcendentals=1 << 20
        ),
    )(attn, w_out, tok_a, tok_b, vectors, *packs)


def on_device(
    tokens,
    w_qkv,
    w_out,
    b_out,
    gain1,
    shift1,
    w_up,
    b_up,
    w_down,
    b_down,
    gain2,
    shift2,
    root_cache,
    node_cache,
    root_len,
    node_len,
    node_parent,
    node_place,
    req_leaf,
):
    req_dev, suf, width = tokens.shape
    cols = w_qkv.shape[2]
    own_rows = req_dev * suf
    reqs = req_leaf.shape[0]
    node_max = node_cache.shape[2]
    tenants = root_cache.shape[1]
    root_per = root_cache.shape[2]
    blk = lax.axis_index("blk")
    owner = lax.axis_index("owner")
    my_z = owner // (NX * NY)
    my_x = (owner // NY) % NX
    my_y = owner % NY
    swap = xor_pairs(N_BLK, 1)
    n_own = N_BLK // 2

    def zero_after(value):
        flat = value.reshape(-1, value.shape[-1])
        return jnp.minimum(jnp.abs(flat[:1, :1]), 0)

    coords = jnp.stack([my_z, my_x, my_y, blk]).astype(I32)
    tab = make_tables(coords, req_leaf, node_parent, node_place, node_len, root_len)

    tok = tokens.reshape(own_rows, width)
    near = lax.ppermute(tok, "blk", swap)
    half = [lax.ppermute(tok, "blk", xor_pairs(N_BLK, 2 * k)) for k in range(1, n_own)]
    tok_far, last_come = half[1], half[2]

    n_owner = NX * NY * NZ
    roots = root_cache.reshape(-1, LANES)
    roots = jnp.stack([roots, lax.ppermute(roots, "owner", xor_pairs(n_owner, NX * NY))])
    x_groups = [[(z * NX + x) * NY + y for x in range(NX)] for z in range(NZ) for y in range(NY)]
    y_groups = [[g * NY + y for y in range(NY)] for g in range(NZ * NX)]
    roots = lax.all_gather(roots, "owner", axis=0, tiled=False, axis_index_groups=x_groups)
    tables_made = jnp.minimum(jnp.abs(tab[:1]), 0).astype(BF16)
    planned = zero_after(roots)
    roots = roots + tables_made
    for came in half + [near]:
        roots = roots + zero_after(came)
    roots = lax.all_gather(roots, "owner", axis=0, tiled=False, axis_index_groups=y_groups)
    other = lax.ppermute(jnp.stack(half) + planned, "blk", swap)
    half = jnp.stack([tok] + half)
    roots = roots.reshape(NY, NX, NZ, 2, tenants, root_per, LANES)

    node_rows = node_cache.reshape(-1, LANES) + zero_after(last_come)
    node_far = lax.ppermute(node_rows, "owner", xor_pairs(n_owner, NX * NY))
    caches = jnp.stack([node_rows, node_far]).reshape(NZ, 2, 2, node_max, LANES)

    w_out_all = lax.all_gather(w_out + zero_after(last_come), "blk", axis=0, tiled=True)
    packs = pack_weights(w_up, w_down, b_up, last_come)
    pack_side = lax.ppermute(packs, "blk", swap)

    q, outgoing = query_and_route(tab, half, near, other, w_qkv[:, 0], suf, last_come)
    outgoing = outgoing.reshape(PEERS, SLOTS, suf, cols)

    def project(which):
        w = w_qkv[:, which]
        out = jnp.concatenate(
            [
                jnp.dot(part.reshape(-1, width), w, preferred_element_type=F32)
                for part in (half, near, other)
            ]
        )
        return out.astype(BF16).reshape(reqs, suf, cols)

    groups = [[z * PEERS + p for p in range(PEERS)] for z in range(NZ)]
    incoming = lax.all_to_all(
        outgoing, "owner", split_axis=0, concat_axis=0, axis_index_groups=groups, tiled=True
    )
    k_new = project(1)
    v_new = project(2)
    order = jnp.arange(N_BLK, dtype=I32) ^ blk
    order = (order % 2) * n_own + order // 2
    new_caches = jnp.stack([k_new, v_new]).reshape(2, N_BLK, req_dev, suf, cols)
    new_caches = jnp.take(new_caches, order, axis=1).reshape(2, reqs, suf, cols)

    answers = node_attention(tab, incoming, caches, packs)
    z_chips = NZ * n_own

    def to_neighbour(step):
        pairs = []
        for dev in range(n_owner * N_BLK):
            b, own = dev // n_owner, dev % n_owner
            z = (own // PEERS * n_own + b // 2 + step) % z_chips
            pairs.append((dev, (z % n_own * 2 + b % 2) * n_owner + z // n_own * PEERS + own % PEERS))
        part = ((blk // 2 + step + n_own) % n_own) // (n_own // 2)
        sent = lax.dynamic_index_in_dim(packs, part, 0, keepdims=False) + zero_after(answers)
        return lax.ppermute(sent, ("blk", "owner"), pairs)

    pack_next = [to_neighbour(1), to_neighbour(-1)]
    back = lax.all_to_all(
        answers, "owner", split_axis=0, concat_axis=0, axis_index_groups=groups, tiled=True
    )
    out, mass = root_attention(tab, q, k_new, v_new, roots)
    send = merge(tab, back, out, mass)
    pack_last = [lax.ppermute(part + zero_after(mass.reshape(-1, LANES)).astype(BF16), "blk", swap) for part in pack_next]
    parts = [packs, pack_side] + pack_next + pack_last
    attn = lax.all_to_all(
        send.reshape(N_BLK, 2 * own_rows, cols), "blk", split_axis=0, concat_axis=0, tiled=True
    )
    vectors = jnp.stack([b_out, gain1, shift1])
    own_norm, down, down_far = feed_forward(attn, w_out_all, tok, tok_far, vectors, parts)
    total = down + lax.ppermute(down_far, "blk", xor_pairs(N_BLK, N_BLK // 2)).astype(F32)
    result = layer_norm(
        own_norm.astype(F32) + total + b_down.astype(F32), gain2, shift2
    ).astype(BF16)
    return (result.reshape(req_dev, suf, width), new_caches)


def solution(mesh):
    in_specs = (
        P(("owner", "blk"), None, None),
        P(None, None, "blk"),
        P("blk", None),
        P(),
        P(),
        P(),
        P(None, "blk"),
        P("blk"),
        P("blk", None),
        P(),
        P(),
        P(),
        P(None, None, "owner", "blk"),
        P(None, "owner", None, "blk"),
        P(),
        P(),
        P(),
        P(),
        P("owner"),
    )
    out_specs = (P(("owner", "blk"), None, None), P(None, "owner", None, "blk"))
    return jax.shard_map(
        on_device, mesh=mesh, in_specs=in_specs, out_specs=out_specs, check_vma=False
    )
```

```python
import functools

import jax
import jax.numpy as jnp
from jax import lax
from jax.experimental import pallas as pl
from jax.experimental.pallas import tpu as pltpu
from jax.sharding import PartitionSpec as P

F32 = jnp.float32
BF16 = jnp.bfloat16
I32 = jnp.int32

HD = 64
LANES = 128
N_BLK = 8
NX, NY, NZ = 4, 8, 2
PEERS = NX * NY
SLOTS = 2 * NZ
HALF = 16
CHUNK = 4
NEG = -1e30
EPS = 1e-05


def layer_norm(values, gain, shift):
    center = values - jnp.mean(values, axis=-1, keepdims=True)
    spread = jnp.mean(center * center, axis=-1, keepdims=True)
    return center * lax.rsqrt(spread + EPS) * gain.astype(F32) + shift.astype(F32)


def xor_pairs(count, bits):
    return [(i, i ^ bits) for i in range(count)]


def dot_nt(a, b):
    return lax.dot_general(a, b, (((1,), (1,)), ((), ())), preferred_element_type=F32)


def dot_nn(a, b):
    return lax.dot_general(a, b, (((1,), (0,)), ((), ())), preferred_element_type=F32)


def both_heads(q):
    lane = lax.broadcasted_iota(I32, q.shape, 1)
    zero = jnp.zeros_like(q)
    return jnp.concatenate([jnp.where(lane < HD, q, zero), jnp.where(lane < HD, zero, q)], axis=0)


def by_head(stacked):
    rows = stacked.shape[0] // 2
    lane = lax.broadcasted_iota(I32, (rows, LANES), 1)
    first = jnp.broadcast_to(stacked[:rows], (rows, LANES))
    second = jnp.broadcast_to(stacked[rows:], (rows, LANES))
    return jnp.where(lane < HD, first, second)


DST_B, DST_L, POS, LENS, USED, ROOT_LEN, PLACE, TENANT, MEMBERS, VALID, COUNT, CHUNK_TENANT, TABLE = (
    0, 32, 64, 96, 100, 104, 112, 128, 160, 208, 256, 264, 288,
)


def table_kernel(coords, leaf_of, parent, place, length, root_len, out):
    my_z, my_x, my_y, blk = (coords[i] for i in range(4))
    reqs = leaf_of.shape[0]
    req_dev = reqs // N_BLK
    tenants = root_len.shape[0]
    seats = (reqs // CHUNK + tenants - 1) * CHUNK

    def slot_index(slot):
        owner = slot >> 1
        return (owner & (PEERS - 1)) * SLOTS + (((owner // PEERS) ^ my_z) << 1) + (slot & 1)

    for t in range(tenants):
        out[COUNT + t] = 0
        out[ROOT_LEN + t] = root_len[t]
    out[PLACE] = my_z
    out[PLACE + 1] = my_x

    def first_pass(r, _):
        leaf = leaf_of[r]
        branch = parent[leaf]
        tenant = parent[branch]
        out[DST_B + r] = slot_index(place[branch])
        out[DST_L + r] = slot_index(place[leaf])
        rel = (r // req_dev) ^ blk
        out[POS + r] = ((rel & 1) * (N_BLK // 2) + (rel >> 1)) * req_dev + (r & (req_dev - 1))
        out[TENANT + r] = tenant
        out[COUNT + tenant] = out[COUNT + tenant] + 1
        return 0

    lax.fori_loop(0, reqs, first_pass, 0, unroll=4)

    def clear(i, _):
        out[MEMBERS + i] = 0
        out[VALID + i] = 0
        return 0

    lax.fori_loop(0, seats, clear, 0, unroll=4)
    end = 0
    for t in range(tenants):
        chunks = (out[COUNT + t] + CHUNK - 1) // CHUNK

        def name(c, _, t=t):
            out[CHUNK_TENANT + c] = t
            return 0

        lax.fori_loop(end, end + chunks, name, 0)
        out[COUNT + t] = end * CHUNK
        end = end + chunks
    out[USED] = end

    def second_pass(r, _):
        tenant = out[TENANT + r]
        seat = out[COUNT + tenant]
        out[COUNT + tenant] = seat + 1
        out[MEMBERS + seat] = out[POS + r]
        out[VALID + seat] = 1
        return 0

    lax.fori_loop(0, reqs, second_pass, 0, unroll=4)

    def node(n, _):
        slot = place[n]
        owner = slot >> 1

        @pl.when((owner & (PEERS - 1)) == my_x * NY + my_y)
        def _():
            out[LENS + (((owner // PEERS) ^ my_z) << 1) + (slot & 1)] = length[n]

        return 0

    lax.fori_loop(0, place.shape[0], node, 0, unroll=4)


def make_tables(coords, leaf_of, parent, place, length, root_len):
    smem = pl.BlockSpec(memory_space=pltpu.SMEM)
    return pl.pallas_call(
        table_kernel,
        out_shape=jax.ShapeDtypeStruct((TABLE,), I32),
        in_specs=[smem] * 6,
        out_specs=smem,
        cost_estimate=pl.CostEstimate(flops=1 << 20, bytes_accessed=1 << 12, transcendentals=0),
    )(coords, leaf_of, parent, place, length, root_len)


def query_kernel(tab, half_ref, near_ref, other_ref, w_ref, after_ref, q_ref, out_ref):
    del after_ref
    reqs, suf, cols = q_ref.shape
    out_ref[...] = jnp.zeros_like(out_ref)
    weights = w_ref[...]
    at = 0
    for ref in (half_ref, near_ref, other_ref):
        rows = ref[...].reshape(-1, ref.shape[-1])
        q = dot_nn(rows, weights).astype(BF16).astype(F32) * HD**-0.5
        count = rows.shape[0] // suf
        q_ref[at : at + count] = q.astype(BF16).reshape(count, suf, cols)
        at += count

    def body(r, _):
        tile = q_ref[tab[POS + r]]
        out_ref[tab[DST_B + r]] = tile
        out_ref[tab[DST_L + r]] = tile
        return 0

    lax.fori_loop(0, reqs, body, 0, unroll=2)


def query_and_route(tab, half, near, other, w, suf, after):
    reqs = (half.size + near.size + other.size) // (suf * half.shape[-1])
    vmem = pl.BlockSpec(memory_space=pltpu.VMEM)
    return pl.pallas_call(
        query_kernel,
        out_shape=(
            jax.ShapeDtypeStruct((reqs, suf, LANES), BF16),
            jax.ShapeDtypeStruct((PEERS * SLOTS, suf, LANES), BF16),
        ),
        in_specs=[pl.BlockSpec(memory_space=pltpu.SMEM)]
        + [vmem] * 4
        + [pl.BlockSpec(memory_space=pl.ANY)],
        out_specs=(vmem, vmem),
        compiler_params=pltpu.CompilerParams(vmem_limit_bytes=24 << 20),
        cost_estimate=pl.CostEstimate(flops=1 << 28, bytes_accessed=4 << 20, transcendentals=0),
    )(tab, half, near, other, w, after)


def pack_kernel(up_ref, down_ref, bias_ref, after_ref, out_ref):
    del after_ref
    width = up_ref.shape[0]
    units = out_ref.shape[2]
    for j in range(2):
        own = slice(j * units, (j + 1) * units)
        out_ref[j, :width] = up_ref[:, own]
        for i in range(width // units):
            out_ref[j, width + i * units : width + (i + 1) * units] = down_ref[
                own, i * units : (i + 1) * units
            ]
        bias = jnp.broadcast_to(bias_ref[:, own].astype(F32), (16, units))
        out_ref[j, 2 * width :] = bias.astype(BF16)


def pack_weights(up, down, bias, after):
    width, units = up.shape
    vmem = pl.BlockSpec(memory_space=pltpu.VMEM)
    return pl.pallas_call(
        pack_kernel,
        out_shape=jax.ShapeDtypeStruct((2, 2 * width + 16, units // 2), BF16),
        in_specs=[vmem] * 3 + [pl.BlockSpec(memory_space=pl.ANY)],
        out_specs=vmem,
        compiler_params=pltpu.CompilerParams(vmem_limit_bytes=16 << 20),
        cost_estimate=pl.CostEstimate(flops=0, bytes_accessed=4 << 20, transcendentals=0),
    )(up, down, bias.reshape(1, units), after)


def node_kernel(tab, q_ref, cache_ref, after_ref, out_ref):
    del after_ref
    peers, slots, suf, _ = q_ref.shape
    group = 4
    rows = group * suf
    node_max = cache_ref.shape[3]
    out_ref[:, 2 * SLOTS] = jnp.zeros((peers, HALF, LANES), BF16)

    def one_slot(slot, _):
        keys = both_heads(cache_ref[slot // 2, 0, slot % 2])
        values = cache_ref[slot // 2, 1, slot % 2]
        values = jnp.concatenate([both_heads(values), both_heads(jnp.ones_like(values))], axis=1)
        keep = lax.broadcasted_iota(I32, (1, node_max), 1) < tab[LENS + slot]
        lane = lax.broadcasted_iota(I32, (group, HALF, LANES), 2)
        piece = lane % (HD // 2) - 3 * slot
        for g in range(peers // group):
            part = slice(g * group, (g + 1) * group)
            q = q_ref[part, slot].reshape(rows, LANES)
            scores = dot_nt(q, keys)
            weights, peaks = [], []
            for h in range(2):
                own = jnp.where(keep, scores[:, h * node_max : (h + 1) * node_max], NEG)
                peak = jnp.max(own, axis=1, keepdims=True)
                weights.append(jnp.exp(own - peak).astype(BF16))
                peaks.append(peak)
            mixed = dot_nn(jnp.concatenate(weights, axis=1), values)
            total = mixed[:, LANES:]
            mass = by_head(jnp.concatenate(peaks, axis=0)) + jnp.log(total)
            out = (mixed[:, :LANES] / total).astype(BF16).reshape(group, 2, HALF, LANES)
            out_ref[part, 2 * slot] = out[:, 0]
            out_ref[part, 2 * slot + 1] = out[:, 1]
            mass = mass.reshape(group, 2, HALF, LANES)
            mass = jnp.where(lane % HD < HD // 2, mass[:, 0], mass[:, 1])
            high = mass.astype(BF16).astype(F32)
            rest = mass - high
            mid = rest.astype(BF16).astype(F32)
            sent = jnp.where(piece == 0, high, jnp.where(piece == 1, mid, rest - mid))
            held = out_ref[part, 2 * SLOTS].astype(F32)
            held = jnp.where((piece >= 0) & (piece < 3), sent, held)
            out_ref[part, 2 * SLOTS] = held.astype(BF16)
        return 0

    lax.fori_loop(0, slots, one_slot, 0)


def node_attention(tab, queries, caches, after):
    peers, slots, suf, _ = queries.shape
    vmem = pl.BlockSpec(memory_space=pltpu.VMEM)
    return pl.pallas_call(
        node_kernel,
        out_shape=jax.ShapeDtypeStruct((peers, 2 * slots + 1, HALF, LANES), BF16),
        in_specs=[
            pl.BlockSpec(memory_space=pltpu.SMEM),
            vmem,
            vmem,
            pl.BlockSpec(memory_space=pl.ANY),
        ],
        out_specs=vmem,
        compiler_params=pltpu.CompilerParams(vmem_limit_bytes=24 << 20),
        cost_estimate=pl.CostEstimate(
            flops=2 << 30, bytes_accessed=4 << 20, transcendentals=4 << 20
        ),
    )(tab, queries, caches, after)


def root_kernel(tab, q_ref, k_ref, v_ref, root_ref, out_ref, mass_ref):
    suf = q_ref.shape[1]
    rows = CHUNK * suf
    per = root_ref.shape[5]
    root_rows = NY * NZ * NX * per

    def body(c, _):
        tenant = tab[CHUNK_TENANT + c]
        where_ = [tab[MEMBERS + c * CHUNK + j] for j in range(CHUNK)]
        q = both_heads(jnp.concatenate([q_ref[w] for w in where_], axis=0))
        own_k = jnp.concatenate([k_ref[w] for w in where_], axis=0)
        own_v = jnp.concatenate([v_ref[w] for w in where_], axis=0)
        keys = root_ref[:, :, :, 0, tenant].reshape(root_rows, LANES)
        values = root_ref[:, :, :, 1, tenant].reshape(root_rows, LANES)
        n = lax.broadcasted_iota(I32, (1, root_rows), 1)
        row = n % per
        z = ((n // per) % NZ) ^ tab[PLACE]
        y = (n // (per * NZ)) % NY
        x = n // (per * NZ * NY)
        place = ((z * NX + x) * NY + y) * per + row
        scores = jnp.where(place < tab[ROOT_LEN + tenant], dot_nt(q, keys), NEG)
        own_row = (lax.broadcasted_iota(I32, (2 * rows, rows), 0) % rows) // suf
        own_col = lax.broadcasted_iota(I32, (2 * rows, rows), 1) // suf
        own = jnp.where(own_row == own_col, dot_nt(q, own_k), NEG)
        peak = jnp.maximum(
            jnp.max(scores, axis=1, keepdims=True), jnp.max(own, axis=1, keepdims=True)
        )
        weights = jnp.exp(scores - peak)
        own_weights = jnp.exp(own - peak)
        total = jnp.sum(weights, axis=1, keepdims=True) + jnp.sum(
            own_weights, axis=1, keepdims=True
        )
        mixed = dot_nn(weights.astype(BF16), values) + dot_nn(own_weights.astype(BF16), own_v)
        out = by_head(mixed) / by_head(total)
        mass = by_head(peak + jnp.log(total))
        for j in range(CHUNK):

            @pl.when(tab[VALID + c * CHUNK + j] > 0)
            def _(j=j):
                out_ref[where_[j]] = out[j * suf : (j + 1) * suf]
                mass_ref[where_[j]] = mass[j * suf : (j + 1) * suf]

        return 0

    lax.fori_loop(0, tab[USED], body, 0)


def root_attention(tab, q, k, v, roots):
    reqs, suf, _ = q.shape
    shape = jax.ShapeDtypeStruct((reqs, suf, LANES), F32)
    vmem = pl.BlockSpec(memory_space=pltpu.VMEM)
    return pl.pallas_call(
        root_kernel,
        out_shape=(shape, shape),
        in_specs=[pl.BlockSpec(memory_space=pltpu.SMEM)] + [vmem] * 4,
        out_specs=(vmem, vmem),
        compiler_params=pltpu.CompilerParams(vmem_limit_bytes=40 << 20),
        cost_estimate=pl.CostEstimate(
            flops=4 << 30, bytes_accessed=4 << 20, transcendentals=4 << 20
        ),
    )(tab, q, k, v, roots)


def merge_kernel(tab, back_ref, out_ref, mass_ref, send_ref, node_mass):
    reqs, suf, _ = out_ref.shape
    per_block = reqs // N_BLK
    src = lax.broadcasted_iota(I32, (LANES, LANES), 0)
    dst = lax.broadcasted_iota(I32, (LANES, LANES), 1)
    packed = back_ref[:, 2 * SLOTS].reshape(PEERS * HALF, LANES)
    for s in range(SLOTS):
        for g in range(2):
            hit = (src // HD == dst // HD) & ((src % HD) // (HD // 2) == g)
            hit = hit & ((src % (HD // 2)) // 3 == s)
            pick = jnp.where(hit, 1.0, 0.0).astype(BF16)
            node_mass[:, s, g] = dot_nn(packed, pick).reshape(PEERS, HALF, LANES)

    def body(r, _):
        here = tab[POS + r]
        outs = [out_ref[here]]
        masses = [mass_ref[here]]
        for first in (DST_B, DST_L):
            peer = tab[first + r] // SLOTS
            slot = tab[first + r] % SLOTS
            outs.append(back_ref[peer, pl.ds(2 * slot, 2)].astype(F32).reshape(suf, LANES))
            masses.append(node_mass[peer, slot].reshape(suf, LANES))
        top = jnp.maximum(jnp.maximum(masses[0], masses[1]), masses[2])
        parts = [jnp.exp(m - top) for m in masses]
        total = parts[0] + parts[1] + parts[2]
        attn = (parts[0] * outs[0] + parts[1] * outs[1] + parts[2] * outs[2]) / total
        attn = attn.astype(BF16)
        block = r // per_block
        send_ref[block, 0, r % per_block] = attn
        send_ref[(block + N_BLK // 2) % N_BLK, 1, r % per_block] = attn
        return 0

    lax.fori_loop(0, reqs, body, 0, unroll=2)


def merge(tab, back, out, mass):
    reqs, suf, _ = out.shape
    vmem = pl.BlockSpec(memory_space=pltpu.VMEM)
    return pl.pallas_call(
        merge_kernel,
        out_shape=jax.ShapeDtypeStruct((N_BLK, 2, reqs // N_BLK, suf, LANES), BF16),
        in_specs=[pl.BlockSpec(memory_space=pltpu.SMEM)] + [vmem] * 3,
        out_specs=vmem,
        scratch_shapes=[pltpu.VMEM((PEERS, SLOTS, 2, HALF, LANES), F32)],
        compiler_params=pltpu.CompilerParams(vmem_limit_bytes=30 << 20),
        cost_estimate=pl.CostEstimate(
            flops=1 << 27, bytes_accessed=4 << 20, transcendentals=1 << 20
        ),
    )(tab, back, out, mass)


def after_kernel(*refs):
    del refs


def after(arrays, value):
    keep = pl.BlockSpec(memory_space=pl.ANY)
    return list(
        pl.pallas_call(
            after_kernel,
            out_shape=tuple(jax.ShapeDtypeStruct(a.shape, a.dtype) for a in arrays),
            in_specs=[keep] * (len(arrays) + 1),
            out_specs=(keep,) * len(arrays),
            input_output_aliases={i: i for i in range(len(arrays))},
        )(*arrays, value)
    )


def rows_norm(values, gain, shift):
    center = values - jnp.mean(values, axis=1, keepdims=True)
    spread = jnp.mean(center * center, axis=1, keepdims=True)
    return center * lax.rsqrt(spread + EPS) * gain + shift


def feed_kernel(attn_ref, w_out_ref, tok_a, tok_b, vec_ref, w0, w1, w2, w3, w4, w5, norm_ref, own_ref, far_ref):
    rows = tok_a.shape[0]
    width = tok_a.shape[1]
    attn = jnp.concatenate([attn_ref[h] for h in range(N_BLK)], axis=1)
    tok = jnp.concatenate([tok_a[...], tok_b[...]], axis=0).astype(F32)
    vec = vec_ref[...].astype(F32)
    mixed = tok + dot_nn(attn, w_out_ref[...]) + vec[0:1]
    norm = rows_norm(mixed, vec[1:2], vec[2:3]).astype(BF16)
    norm_ref[...] = norm[:rows]
    total = jnp.zeros((2 * rows, width), F32)
    units = w0.shape[-1]
    for w in [ref.at[i] for ref in (w0, w1) for i in range(2)] + [w2, w3, w4, w5]:
        bias = w[width + units * (width // units) :].astype(F32)[0:1]
        inner = dot_nn(norm, w[:width]) + bias
        hidden = (0.5 * inner * (1.0 + lax.erf(inner * (0.5**0.5)))).astype(BF16)
        down = [
            dot_nn(hidden, w[width + i * units : width + (i + 1) * units])
            for i in range(width // units)
        ]
        total = total + jnp.concatenate(down, axis=1)
    own_ref[...] = total[:rows]
    far_ref[...] = total[rows:].astype(BF16)


def feed_forward(attn, w_out, tok_a, tok_b, vectors, packs):
    rows, width = tok_a.shape
    vmem = pl.BlockSpec(memory_space=pltpu.VMEM)
    return pl.pallas_call(
        feed_kernel,
        out_shape=(
            jax.ShapeDtypeStruct((rows, width), BF16),
            jax.ShapeDtypeStruct((rows, width), F32),
            jax.ShapeDtypeStruct((rows, width), BF16),
        ),
        in_specs=[vmem] * (5 + len(packs)),
        out_specs=(vmem, vmem, vmem),
        compiler_params=pltpu.CompilerParams(vmem_limit_bytes=48 << 20),
        cost_estimate=pl.CostEstimate(
            flops=3 << 30, bytes_accessed=12 << 20, transcendentals=1 << 20
        ),
    )(attn, w_out, tok_a, tok_b, vectors, *packs)


def on_device(
    tokens,
    w_qkv,
    w_out,
    b_out,
    gain1,
    shift1,
    w_up,
    b_up,
    w_down,
    b_down,
    gain2,
    shift2,
    root_cache,
    node_cache,
    root_len,
    node_len,
    node_parent,
    node_place,
    req_leaf,
):
    req_dev, suf, width = tokens.shape
    cols = w_qkv.shape[2]
    own_rows = req_dev * suf
    reqs = req_leaf.shape[0]
    node_max = node_cache.shape[2]
    tenants = root_cache.shape[1]
    root_per = root_cache.shape[2]
    blk = lax.axis_index("blk")
    owner = lax.axis_index("owner")
    my_z = owner // (NX * NY)
    my_x = (owner // NY) % NX
    my_y = owner % NY
    swap = xor_pairs(N_BLK, 1)
    n_own = N_BLK // 2

    def zero_after(value):
        flat = value.reshape(-1, value.shape[-1])
        return jnp.minimum(jnp.abs(flat[:1, :1]), 0)

    coords = jnp.stack([my_z, my_x, my_y, blk]).astype(I32)
    tab = make_tables(coords, req_leaf, node_parent, node_place, node_len, root_len)

    tok = tokens.reshape(own_rows, width)
    near = lax.ppermute(tok, "blk", swap)
    half = [lax.ppermute(tok, "blk", xor_pairs(N_BLK, 2 * k)) for k in range(1, n_own)]
    tok_far, last_come = half[1], half[2]

    n_owner = NX * NY * NZ
    roots = root_cache.reshape(-1, LANES)
    roots = jnp.stack([roots, lax.ppermute(roots, "owner", xor_pairs(n_owner, NX * NY))])
    groups = [[z * PEERS + p for p in range(PEERS)] for z in range(NZ)]
    roots = roots + jnp.minimum(jnp.abs(tab[:1]), 0).astype(BF16)
    for came in half + [near]:
        roots = roots + zero_after(came)
    roots = lax.all_gather(roots, "owner", axis=0, tiled=False, axis_index_groups=groups)
    other = lax.ppermute(jnp.stack(half), "blk", swap)
    half = jnp.stack([tok] + half)
    roots = roots.reshape(NX, NY, NZ, 2, tenants, root_per, LANES)

    node_rows = node_cache.reshape(-1, LANES) + zero_after(last_come)
    node_far = lax.ppermute(node_rows, "owner", xor_pairs(n_owner, NX * NY))
    caches = jnp.stack([node_rows, node_far]).reshape(NZ, 2, 2, node_max, LANES)

    w_out_all = lax.all_gather(w_out + zero_after(last_come), "blk", axis=0, tiled=True)
    packs = pack_weights(w_up, w_down, b_up, last_come)
    pack_side = lax.ppermute(packs, "blk", swap)

    q, outgoing = query_and_route(tab, half, near, other, w_qkv[:, 0], suf, last_come)
    outgoing = outgoing.reshape(PEERS, SLOTS, suf, cols)

    def project(which):
        w = w_qkv[:, which]
        out = jnp.concatenate(
            [
                jnp.dot(part.reshape(-1, width), w, preferred_element_type=F32)
                for part in (half, near, other)
            ]
        )
        return out.astype(BF16).reshape(reqs, suf, cols)

    incoming = lax.all_to_all(
        outgoing, "owner", split_axis=0, concat_axis=0, axis_index_groups=groups, tiled=True
    )
    k_new = project(1)
    v_new = project(2)
    order = jnp.arange(N_BLK, dtype=I32) ^ blk
    order = (order % 2) * n_own + order // 2
    new_caches = jnp.stack([k_new, v_new]).reshape(2, N_BLK, req_dev, suf, cols)
    new_caches = jnp.take(new_caches, order, axis=1).reshape(2, reqs, suf, cols)

    answers = node_attention(tab, incoming, caches, packs)
    z_chips = NZ * n_own

    def to_neighbour(step):
        pairs = []
        for dev in range(n_owner * N_BLK):
            b, own = dev // n_owner, dev % n_owner
            z = (own // PEERS * n_own + b // 2 + step) % z_chips
            pairs.append((dev, (z % n_own * 2 + b % 2) * n_owner + z // n_own * PEERS + own % PEERS))
        part = ((blk // 2 + step + n_own) % n_own) // (n_own // 2)
        sent = lax.dynamic_index_in_dim(packs, part, 0, keepdims=False) + zero_after(answers)
        return lax.ppermute(sent, ("blk", "owner"), pairs)

    pack_next = [to_neighbour(1), to_neighbour(-1)]
    back = lax.all_to_all(
        answers, "owner", split_axis=0, concat_axis=0, axis_index_groups=groups, tiled=True
    )
    out, mass = root_attention(tab, q, k_new, v_new, roots)
    send = merge(tab, back, out, mass)
    pack_next = after(pack_next, mass)
    pack_last = [lax.ppermute(part, "blk", swap) for part in pack_next]
    parts = [packs, pack_side] + pack_next + pack_last
    attn = lax.all_to_all(
        send.reshape(N_BLK, 2 * own_rows, cols), "blk", split_axis=0, concat_axis=0, tiled=True
    )
    vectors = jnp.stack([b_out, gain1, shift1])
    own_norm, down, down_far = feed_forward(attn, w_out_all, tok, tok_far, vectors, parts)
    total = down + lax.ppermute(down_far, "blk", xor_pairs(N_BLK, N_BLK // 2)).astype(F32)
    result = layer_norm(
        own_norm.astype(F32) + total + b_down.astype(F32), gain2, shift2
    ).astype(BF16)
    return (result.reshape(req_dev, suf, width), new_caches)


def solution(mesh):
    in_specs = (
        P(("owner", "blk"), None, None),
        P(None, None, "blk"),
        P("blk", None),
        P(),
        P(),
        P(),
        P(None, "blk"),
        P("blk"),
        P("blk", None),
        P(),
        P(),
        P(),
        P(None, None, "owner", "blk"),
        P(None, "owner", None, "blk"),
        P(),
        P(),
        P(),
        P(),
        P("owner"),
    )
    out_specs = (P(("owner", "blk"), None, None), P(None, "owner", None, "blk"))
    return jax.shard_map(
        on_device, mesh=mesh, in_specs=in_specs, out_specs=out_specs, check_vma=False
    )
```

```python
import functools

import jax
import jax.numpy as jnp
from jax import lax
from jax.experimental import pallas as pl
from jax.experimental.pallas import tpu as pltpu
from jax.sharding import PartitionSpec as P

F32 = jnp.float32
BF16 = jnp.bfloat16
I32 = jnp.int32

HD = 64
LANES = 128
N_BLK = 8
NX, NY, NZ = 4, 8, 2
PEERS = NX * NY
SLOTS = 2 * NZ
HALF = 16
CHUNK = 4
NEG = -1e30
EPS = 1e-05


def layer_norm(values, gain, shift):
    center = values - jnp.mean(values, axis=-1, keepdims=True)
    spread = jnp.mean(center * center, axis=-1, keepdims=True)
    return center * lax.rsqrt(spread + EPS) * gain.astype(F32) + shift.astype(F32)


def xor_pairs(count, bits):
    return [(i, i ^ bits) for i in range(count)]


def dot_nt(a, b):
    return lax.dot_general(a, b, (((1,), (1,)), ((), ())), preferred_element_type=F32)


def dot_nn(a, b):
    return lax.dot_general(a, b, (((1,), (0,)), ((), ())), preferred_element_type=F32)


def both_heads(q):
    lane = lax.broadcasted_iota(I32, q.shape, 1)
    zero = jnp.zeros_like(q)
    return jnp.concatenate([jnp.where(lane < HD, q, zero), jnp.where(lane < HD, zero, q)], axis=0)


def by_head(stacked):
    rows = stacked.shape[0] // 2
    lane = lax.broadcasted_iota(I32, (rows, LANES), 1)
    first = jnp.broadcast_to(stacked[:rows], (rows, LANES))
    second = jnp.broadcast_to(stacked[rows:], (rows, LANES))
    return jnp.where(lane < HD, first, second)


DST_B, DST_L, POS, LENS, USED, ROOT_LEN, PLACE, TENANT, MEMBERS, VALID, COUNT, CHUNK_TENANT, TABLE = (
    0, 32, 64, 96, 100, 104, 112, 128, 160, 208, 256, 264, 288,
)


def table_kernel(coords, leaf_of, parent, place, length, root_len, out):
    my_z, my_x, my_y, blk = (coords[i] for i in range(4))
    reqs = leaf_of.shape[0]
    req_dev = reqs // N_BLK
    tenants = root_len.shape[0]
    seats = (reqs // CHUNK + tenants - 1) * CHUNK

    def slot_index(slot):
        owner = slot >> 1
        return (owner & (PEERS - 1)) * SLOTS + (((owner // PEERS) ^ my_z) << 1) + (slot & 1)

    for t in range(tenants):
        out[COUNT + t] = 0
        out[ROOT_LEN + t] = root_len[t]
    out[PLACE] = my_z
    out[PLACE + 1] = my_x

    def first_pass(r, _):
        leaf = leaf_of[r]
        branch = parent[leaf]
        tenant = parent[branch]
        out[DST_B + r] = slot_index(place[branch])
        out[DST_L + r] = slot_index(place[leaf])
        rel = (r // req_dev) ^ blk
        out[POS + r] = ((rel & 1) * (N_BLK // 2) + (rel >> 1)) * req_dev + (r & (req_dev - 1))
        out[TENANT + r] = tenant
        out[COUNT + tenant] = out[COUNT + tenant] + 1
        return 0

    lax.fori_loop(0, reqs, first_pass, 0, unroll=4)

    def clear(i, _):
        out[MEMBERS + i] = 0
        out[VALID + i] = 0
        return 0

    lax.fori_loop(0, seats, clear, 0, unroll=4)
    end = 0
    for t in range(tenants):
        chunks = (out[COUNT + t] + CHUNK - 1) // CHUNK

        def name(c, _, t=t):
            out[CHUNK_TENANT + c] = t
            return 0

        lax.fori_loop(end, end + chunks, name, 0)
        out[COUNT + t] = end * CHUNK
        end = end + chunks
    out[USED] = end

    def second_pass(r, _):
        tenant = out[TENANT + r]
        seat = out[COUNT + tenant]
        out[COUNT + tenant] = seat + 1
        out[MEMBERS + seat] = out[POS + r]
        out[VALID + seat] = 1
        return 0

    lax.fori_loop(0, reqs, second_pass, 0, unroll=4)

    def node(n, _):
        slot = place[n]
        owner = slot >> 1

        @pl.when((owner & (PEERS - 1)) == my_x * NY + my_y)
        def _():
            out[LENS + (((owner // PEERS) ^ my_z) << 1) + (slot & 1)] = length[n]

        return 0

    lax.fori_loop(0, place.shape[0], node, 0, unroll=4)


def make_tables(coords, leaf_of, parent, place, length, root_len):
    smem = pl.BlockSpec(memory_space=pltpu.SMEM)
    return pl.pallas_call(
        table_kernel,
        out_shape=jax.ShapeDtypeStruct((TABLE,), I32),
        in_specs=[smem] * 6,
        out_specs=smem,
        cost_estimate=pl.CostEstimate(flops=1 << 20, bytes_accessed=1 << 12, transcendentals=0),
    )(coords, leaf_of, parent, place, length, root_len)


def query_kernel(tab, half_ref, near_ref, other_ref, w_ref, after_ref, q_ref, out_ref):
    del after_ref
    reqs, suf, cols = q_ref.shape
    out_ref[...] = jnp.zeros_like(out_ref)
    weights = w_ref[...]
    at = 0
    for ref in (half_ref, near_ref, other_ref):
        rows = ref[...].reshape(-1, ref.shape[-1])
        q = dot_nn(rows, weights).astype(BF16).astype(F32) * HD**-0.5
        count = rows.shape[0] // suf
        q_ref[at : at + count] = q.astype(BF16).reshape(count, suf, cols)
        at += count

    def body(r, _):
        tile = q_ref[tab[POS + r]]
        out_ref[tab[DST_B + r]] = tile
        out_ref[tab[DST_L + r]] = tile
        return 0

    lax.fori_loop(0, reqs, body, 0, unroll=2)


def query_and_route(tab, half, near, other, w, suf, after):
    reqs = (half.size + near.size + other.size) // (suf * half.shape[-1])
    vmem = pl.BlockSpec(memory_space=pltpu.VMEM)
    return pl.pallas_call(
        query_kernel,
        out_shape=(
            jax.ShapeDtypeStruct((reqs, suf, LANES), BF16),
            jax.ShapeDtypeStruct((PEERS * SLOTS, suf, LANES), BF16),
        ),
        in_specs=[pl.BlockSpec(memory_space=pltpu.SMEM)]
        + [vmem] * 4
        + [pl.BlockSpec(memory_space=pl.ANY)],
        out_specs=(vmem, vmem),
        compiler_params=pltpu.CompilerParams(vmem_limit_bytes=24 << 20),
        cost_estimate=pl.CostEstimate(flops=1 << 28, bytes_accessed=4 << 20, transcendentals=0),
    )(tab, half, near, other, w, after)


def pack_kernel(up_ref, down_ref, bias_ref, after_ref, out_ref):
    del after_ref
    width = up_ref.shape[0]
    units = out_ref.shape[2]
    for j in range(2):
        own = slice(j * units, (j + 1) * units)
        out_ref[j, :width] = up_ref[:, own]
        for i in range(width // units):
            out_ref[j, width + i * units : width + (i + 1) * units] = down_ref[
                own, i * units : (i + 1) * units
            ]
        bias = jnp.broadcast_to(bias_ref[:, own].astype(F32), (16, units))
        out_ref[j, 2 * width :] = bias.astype(BF16)


def pack_weights(up, down, bias, after):
    width, units = up.shape
    vmem = pl.BlockSpec(memory_space=pltpu.VMEM)
    return pl.pallas_call(
        pack_kernel,
        out_shape=jax.ShapeDtypeStruct((2, 2 * width + 16, units // 2), BF16),
        in_specs=[vmem] * 3 + [pl.BlockSpec(memory_space=pl.ANY)],
        out_specs=vmem,
        compiler_params=pltpu.CompilerParams(vmem_limit_bytes=16 << 20),
        cost_estimate=pl.CostEstimate(flops=0, bytes_accessed=4 << 20, transcendentals=0),
    )(up, down, bias.reshape(1, units), after)


def node_kernel(tab, q_ref, cache_ref, after_ref, out_ref):
    del after_ref
    peers, slots, suf, _ = q_ref.shape
    group = 4
    rows = group * suf
    node_max = cache_ref.shape[3]
    out_ref[:, 2 * SLOTS] = jnp.zeros((peers, HALF, LANES), BF16)

    def one_slot(slot, _):
        keys = both_heads(cache_ref[slot // 2, 0, slot % 2])
        values = cache_ref[slot // 2, 1, slot % 2]
        values = jnp.concatenate([both_heads(values), both_heads(jnp.ones_like(values))], axis=1)
        keep = lax.broadcasted_iota(I32, (1, node_max), 1) < tab[LENS + slot]
        lane = lax.broadcasted_iota(I32, (group, HALF, LANES), 2)
        piece = lane % (HD // 2) - 3 * slot
        for g in range(peers // group):
            part = slice(g * group, (g + 1) * group)
            q = q_ref[part, slot].reshape(rows, LANES)
            scores = dot_nt(q, keys)
            weights, peaks = [], []
            for h in range(2):
                own = jnp.where(keep, scores[:, h * node_max : (h + 1) * node_max], NEG)
                peak = jnp.max(own, axis=1, keepdims=True)
                weights.append(jnp.exp(own - peak).astype(BF16))
                peaks.append(peak)
            mixed = dot_nn(jnp.concatenate(weights, axis=1), values)
            total = mixed[:, LANES:]
            mass = by_head(jnp.concatenate(peaks, axis=0)) + jnp.log(total)
            out = (mixed[:, :LANES] / total).astype(BF16).reshape(group, 2, HALF, LANES)
            out_ref[part, 2 * slot] = out[:, 0]
            out_ref[part, 2 * slot + 1] = out[:, 1]
            mass = mass.reshape(group, 2, HALF, LANES)
            mass = jnp.where(lane % HD < HD // 2, mass[:, 0], mass[:, 1])
            high = mass.astype(BF16).astype(F32)
            rest = mass - high
            mid = rest.astype(BF16).astype(F32)
            sent = jnp.where(piece == 0, high, jnp.where(piece == 1, mid, rest - mid))
            held = out_ref[part, 2 * SLOTS].astype(F32)
            held = jnp.where((piece >= 0) & (piece < 3), sent, held)
            out_ref[part, 2 * SLOTS] = held.astype(BF16)
        return 0

    lax.fori_loop(0, slots, one_slot, 0)


def node_attention(tab, queries, caches, after):
    peers, slots, suf, _ = queries.shape
    vmem = pl.BlockSpec(memory_space=pltpu.VMEM)
    return pl.pallas_call(
        node_kernel,
        out_shape=jax.ShapeDtypeStruct((peers, 2 * slots + 1, HALF, LANES), BF16),
        in_specs=[
            pl.BlockSpec(memory_space=pltpu.SMEM),
            vmem,
            vmem,
            pl.BlockSpec(memory_space=pl.ANY),
        ],
        out_specs=vmem,
        compiler_params=pltpu.CompilerParams(vmem_limit_bytes=24 << 20),
        cost_estimate=pl.CostEstimate(
            flops=2 << 30, bytes_accessed=4 << 20, transcendentals=4 << 20
        ),
    )(tab, queries, caches, after)


def root_kernel(tab, q_ref, k_ref, v_ref, root_ref, out_ref, mass_ref):
    suf = q_ref.shape[1]
    rows = CHUNK * suf
    per = root_ref.shape[5]
    root_rows = NY * NZ * NX * per

    def body(c, _):
        tenant = tab[CHUNK_TENANT + c]
        where_ = [tab[MEMBERS + c * CHUNK + j] for j in range(CHUNK)]
        q = both_heads(jnp.concatenate([q_ref[w] for w in where_], axis=0))
        own_k = jnp.concatenate([k_ref[w] for w in where_], axis=0)
        own_v = jnp.concatenate([v_ref[w] for w in where_], axis=0)
        keys = root_ref[:, :, :, 0, tenant].reshape(root_rows, LANES)
        values = root_ref[:, :, :, 1, tenant].reshape(root_rows, LANES)
        n = lax.broadcasted_iota(I32, (1, root_rows), 1)
        row = n % per
        z = ((n // per) % NZ) ^ tab[PLACE]
        x = ((n // (per * NZ)) % NX) ^ tab[PLACE + 1]
        y = n // (per * NZ * NX)
        place = ((z * NX + x) * NY + y) * per + row
        scores = jnp.where(place < tab[ROOT_LEN + tenant], dot_nt(q, keys), NEG)
        own_row = (lax.broadcasted_iota(I32, (2 * rows, rows), 0) % rows) // suf
        own_col = lax.broadcasted_iota(I32, (2 * rows, rows), 1) // suf
        own = jnp.where(own_row == own_col, dot_nt(q, own_k), NEG)
        peak = jnp.maximum(
            jnp.max(scores, axis=1, keepdims=True), jnp.max(own, axis=1, keepdims=True)
        )
        weights = jnp.exp(scores - peak)
        own_weights = jnp.exp(own - peak)
        total = jnp.sum(weights, axis=1, keepdims=True) + jnp.sum(
            own_weights, axis=1, keepdims=True
        )
        mixed = dot_nn(weights.astype(BF16), values) + dot_nn(own_weights.astype(BF16), own_v)
        out = by_head(mixed) / by_head(total)
        mass = by_head(peak + jnp.log(total))
        for j in range(CHUNK):

            @pl.when(tab[VALID + c * CHUNK + j] > 0)
            def _(j=j):
                out_ref[where_[j]] = out[j * suf : (j + 1) * suf]
                mass_ref[where_[j]] = mass[j * suf : (j + 1) * suf]

        return 0

    lax.fori_loop(0, tab[USED], body, 0)


def root_attention(tab, q, k, v, roots):
    reqs, suf, _ = q.shape
    shape = jax.ShapeDtypeStruct((reqs, suf, LANES), F32)
    vmem = pl.BlockSpec(memory_space=pltpu.VMEM)
    return pl.pallas_call(
        root_kernel,
        out_shape=(shape, shape),
        in_specs=[pl.BlockSpec(memory_space=pltpu.SMEM)] + [vmem] * 4,
        out_specs=(vmem, vmem),
        compiler_params=pltpu.CompilerParams(vmem_limit_bytes=40 << 20),
        cost_estimate=pl.CostEstimate(
            flops=4 << 30, bytes_accessed=4 << 20, transcendentals=4 << 20
        ),
    )(tab, q, k, v, roots)


def merge_kernel(tab, back_ref, out_ref, mass_ref, send_ref, node_mass):
    reqs, suf, _ = out_ref.shape
    per_block = reqs // N_BLK
    src = lax.broadcasted_iota(I32, (LANES, LANES), 0)
    dst = lax.broadcasted_iota(I32, (LANES, LANES), 1)
    packed = back_ref[:, 2 * SLOTS].reshape(PEERS * HALF, LANES)
    for s in range(SLOTS):
        for g in range(2):
            hit = (src // HD == dst // HD) & ((src % HD) // (HD // 2) == g)
            hit = hit & ((src % (HD // 2)) // 3 == s)
            pick = jnp.where(hit, 1.0, 0.0).astype(BF16)
            node_mass[:, s, g] = dot_nn(packed, pick).reshape(PEERS, HALF, LANES)

    def body(r, _):
        here = tab[POS + r]
        outs = [out_ref[here]]
        masses = [mass_ref[here]]
        for first in (DST_B, DST_L):
            peer = tab[first + r] // SLOTS
            slot = tab[first + r] % SLOTS
            outs.append(back_ref[peer, pl.ds(2 * slot, 2)].astype(F32).reshape(suf, LANES))
            masses.append(node_mass[peer, slot].reshape(suf, LANES))
        top = jnp.maximum(jnp.maximum(masses[0], masses[1]), masses[2])
        parts = [jnp.exp(m - top) for m in masses]
        total = parts[0] + parts[1] + parts[2]
        attn = (parts[0] * outs[0] + parts[1] * outs[1] + parts[2] * outs[2]) / total
        attn = attn.astype(BF16)
        block = r // per_block
        send_ref[block, 0, r % per_block] = attn
        send_ref[(block + N_BLK // 2) % N_BLK, 1, r % per_block] = attn
        return 0

    lax.fori_loop(0, reqs, body, 0, unroll=2)


def merge(tab, back, out, mass):
    reqs, suf, _ = out.shape
    vmem = pl.BlockSpec(memory_space=pltpu.VMEM)
    return pl.pallas_call(
        merge_kernel,
        out_shape=jax.ShapeDtypeStruct((N_BLK, 2, reqs // N_BLK, suf, LANES), BF16),
        in_specs=[pl.BlockSpec(memory_space=pltpu.SMEM)] + [vmem] * 3,
        out_specs=vmem,
        scratch_shapes=[pltpu.VMEM((PEERS, SLOTS, 2, HALF, LANES), F32)],
        compiler_params=pltpu.CompilerParams(vmem_limit_bytes=30 << 20),
        cost_estimate=pl.CostEstimate(
            flops=1 << 27, bytes_accessed=4 << 20, transcendentals=1 << 20
        ),
    )(tab, back, out, mass)


def after_kernel(*refs):
    del refs


def after(arrays, value):
    keep = pl.BlockSpec(memory_space=pl.ANY)
    return list(
        pl.pallas_call(
            after_kernel,
            out_shape=tuple(jax.ShapeDtypeStruct(a.shape, a.dtype) for a in arrays),
            in_specs=[keep] * (len(arrays) + 1),
            out_specs=(keep,) * len(arrays),
            input_output_aliases={i: i for i in range(len(arrays))},
        )(*arrays, value)
    )


def rows_norm(values, gain, shift):
    center = values - jnp.mean(values, axis=1, keepdims=True)
    spread = jnp.mean(center * center, axis=1, keepdims=True)
    return center * lax.rsqrt(spread + EPS) * gain + shift


def feed_kernel(attn_ref, w_out_ref, tok_a, tok_b, vec_ref, w0, w1, w2, w3, w4, w5, norm_ref, own_ref, far_ref):
    rows = tok_a.shape[0]
    width = tok_a.shape[1]
    attn = jnp.concatenate([attn_ref[h] for h in range(N_BLK)], axis=1)
    tok = jnp.concatenate([tok_a[...], tok_b[...]], axis=0).astype(F32)
    vec = vec_ref[...].astype(F32)
    mixed = tok + dot_nn(attn, w_out_ref[...]) + vec[0:1]
    norm = rows_norm(mixed, vec[1:2], vec[2:3]).astype(BF16)
    norm_ref[...] = norm[:rows]
    total = jnp.zeros((2 * rows, width), F32)
    units = w0.shape[-1]
    for w in [ref.at[i] for ref in (w0, w1) for i in range(2)] + [w2, w3, w4, w5]:
        bias = w[width + units * (width // units) :].astype(F32)[0:1]
        inner = dot_nn(norm, w[:width]) + bias
        hidden = (0.5 * inner * (1.0 + lax.erf(inner * (0.5**0.5)))).astype(BF16)
        down = [
            dot_nn(hidden, w[width + i * units : width + (i + 1) * units])
            for i in range(width // units)
        ]
        total = total + jnp.concatenate(down, axis=1)
    own_ref[...] = total[:rows]
    far_ref[...] = total[rows:].astype(BF16)


def feed_forward(attn, w_out, tok_a, tok_b, vectors, packs):
    rows, width = tok_a.shape
    vmem = pl.BlockSpec(memory_space=pltpu.VMEM)
    return pl.pallas_call(
        feed_kernel,
        out_shape=(
            jax.ShapeDtypeStruct((rows, width), BF16),
            jax.ShapeDtypeStruct((rows, width), F32),
            jax.ShapeDtypeStruct((rows, width), BF16),
        ),
        in_specs=[vmem] * (5 + len(packs)),
        out_specs=(vmem, vmem, vmem),
        compiler_params=pltpu.CompilerParams(vmem_limit_bytes=48 << 20),
        cost_estimate=pl.CostEstimate(
            flops=3 << 30, bytes_accessed=12 << 20, transcendentals=1 << 20
        ),
    )(attn, w_out, tok_a, tok_b, vectors, *packs)


def on_device(
    tokens,
    w_qkv,
    w_out,
    b_out,
    gain1,
    shift1,
    w_up,
    b_up,
    w_down,
    b_down,
    gain2,
    shift2,
    root_cache,
    node_cache,
    root_len,
    node_len,
    node_parent,
    node_place,
    req_leaf,
):
    req_dev, suf, width = tokens.shape
    cols = w_qkv.shape[2]
    own_rows = req_dev * suf
    reqs = req_leaf.shape[0]
    node_max = node_cache.shape[2]
    tenants = root_cache.shape[1]
    root_per = root_cache.shape[2]
    blk = lax.axis_index("blk")
    owner = lax.axis_index("owner")
    my_z = owner // (NX * NY)
    my_x = (owner // NY) % NX
    my_y = owner % NY
    swap = xor_pairs(N_BLK, 1)
    n_own = N_BLK // 2

    def zero_after(value):
        flat = value.reshape(-1, value.shape[-1])
        return jnp.minimum(jnp.abs(flat[:1, :1]), 0)

    coords = jnp.stack([my_z, my_x, my_y, blk]).astype(I32)
    tab = make_tables(coords, req_leaf, node_parent, node_place, node_len, root_len)

    tok = tokens.reshape(own_rows, width)
    near = lax.ppermute(tok, "blk", swap)
    half = [lax.ppermute(tok, "blk", xor_pairs(N_BLK, 2 * k)) for k in range(1, n_own)]
    tok_far, last_come = half[1], half[2]

    n_owner = NX * NY * NZ
    roots = root_cache.reshape(-1, LANES)
    roots = jnp.stack([roots, lax.ppermute(roots, "owner", xor_pairs(n_owner, NX * NY))])
    roots = jnp.stack(
        [roots] + [lax.ppermute(roots, "owner", xor_pairs(n_owner, k * NY)) for k in range(1, NX)]
    )
    roots = roots + jnp.minimum(jnp.abs(tab[:1]), 0).astype(BF16)
    for came in half + [near]:
        roots = roots + zero_after(came)
    y_groups = [[g * NY + y for y in range(NY)] for g in range(NZ * NX)]
    roots = lax.all_gather(roots, "owner", axis=0, tiled=False, axis_index_groups=y_groups)
    groups = [[z * PEERS + p for p in range(PEERS)] for z in range(NZ)]
    other = lax.ppermute(jnp.stack(half), "blk", swap)
    half = jnp.stack([tok] + half)
    roots = roots.reshape(NY, NX, NZ, 2, tenants, root_per, LANES)

    node_rows = node_cache.reshape(-1, LANES) + zero_after(last_come)
    node_far = lax.ppermute(node_rows, "owner", xor_pairs(n_owner, NX * NY))
    caches = jnp.stack([node_rows, node_far]).reshape(NZ, 2, 2, node_max, LANES)

    w_out_all = lax.all_gather(w_out + zero_after(last_come), "blk", axis=0, tiled=True)
    packs = pack_weights(w_up, w_down, b_up, last_come)
    pack_side = lax.ppermute(packs, "blk", swap)

    q, outgoing = query_and_route(tab, half, near, other, w_qkv[:, 0], suf, last_come)
    outgoing = outgoing.reshape(PEERS, SLOTS, suf, cols)

    def project(which):
        w = w_qkv[:, which]
        out = jnp.concatenate(
            [
                jnp.dot(part.reshape(-1, width), w, preferred_element_type=F32)
                for part in (half, near, other)
            ]
        )
        return out.astype(BF16).reshape(reqs, suf, cols)

    incoming = lax.all_to_all(
        outgoing, "owner", split_axis=0, concat_axis=0, axis_index_groups=groups, tiled=True
    )
    k_new = project(1)
    v_new = project(2)
    order = jnp.arange(N_BLK, dtype=I32) ^ blk
    order = (order % 2) * n_own + order // 2
    new_caches = jnp.stack([k_new, v_new]).reshape(2, N_BLK, req_dev, suf, cols)
    new_caches = jnp.take(new_caches, order, axis=1).reshape(2, reqs, suf, cols)

    answers = node_attention(tab, incoming, caches, packs)
    z_chips = NZ * n_own

    def to_neighbour(step):
        pairs = []
        for dev in range(n_owner * N_BLK):
            b, own = dev // n_owner, dev % n_owner
            z = (own // PEERS * n_own + b // 2 + step) % z_chips
            pairs.append((dev, (z % n_own * 2 + b % 2) * n_owner + z // n_own * PEERS + own % PEERS))
        part = ((blk // 2 + step + n_own) % n_own) // (n_own // 2)
        sent = lax.dynamic_index_in_dim(packs, part, 0, keepdims=False) + zero_after(answers)
        return lax.ppermute(sent, ("blk", "owner"), pairs)

    pack_next = [to_neighbour(1), to_neighbour(-1)]
    back = lax.all_to_all(
        answers, "owner", split_axis=0, concat_axis=0, axis_index_groups=groups, tiled=True
    )
    out, mass = root_attention(tab, q, k_new, v_new, roots)
    send = merge(tab, back, out, mass)
    pack_next = after(pack_next, mass)
    pack_last = [lax.ppermute(part, "blk", swap) for part in pack_next]
    parts = [packs, pack_side] + pack_next + pack_last
    attn = lax.all_to_all(
        send.reshape(N_BLK, 2 * own_rows, cols), "blk", split_axis=0, concat_axis=0, tiled=True
    )
    vectors = jnp.stack([b_out, gain1, shift1])
    own_norm, down, down_far = feed_forward(attn, w_out_all, tok, tok_far, vectors, parts)
    total = down + lax.ppermute(down_far, "blk", xor_pairs(N_BLK, N_BLK // 2)).astype(F32)
    result = layer_norm(
        own_norm.astype(F32) + total + b_down.astype(F32), gain2, shift2
    ).astype(BF16)
    return (result.reshape(req_dev, suf, width), new_caches)


def solution(mesh):
    in_specs = (
        P(("owner", "blk"), None, None),
        P(None, None, "blk"),
        P("blk", None),
        P(),
        P(),
        P(),
        P(None, "blk"),
        P("blk"),
        P("blk", None),
        P(),
        P(),
        P(),
        P(None, None, "owner", "blk"),
        P(None, "owner", None, "blk"),
        P(),
        P(),
        P(),
        P(),
        P("owner"),
    )
    out_specs = (P(("owner", "blk"), None, None), P(None, "owner", None, "blk"))
    return jax.shard_map(
        on_device, mesh=mesh, in_specs=in_specs, out_specs=out_specs, check_vma=False
    )
```

```python
import functools

import jax
import jax.numpy as jnp
from jax import lax
from jax.experimental import pallas as pl
from jax.experimental.pallas import tpu as pltpu
from jax.sharding import PartitionSpec as P

F32 = jnp.float32
BF16 = jnp.bfloat16
I32 = jnp.int32

HD = 64
LANES = 128
N_BLK = 8
NX, NY, NZ = 4, 8, 2
PEERS = NX * NY
SLOTS = 2 * NZ
HALF = 16
CHUNK = 4
NEG = -1e30
EPS = 1e-05


def layer_norm(values, gain, shift):
    center = values - jnp.mean(values, axis=-1, keepdims=True)
    spread = jnp.mean(center * center, axis=-1, keepdims=True)
    return center * lax.rsqrt(spread + EPS) * gain.astype(F32) + shift.astype(F32)


def xor_pairs(count, bits):
    return [(i, i ^ bits) for i in range(count)]


def dot_nt(a, b):
    return lax.dot_general(a, b, (((1,), (1,)), ((), ())), preferred_element_type=F32)


def dot_nn(a, b):
    return lax.dot_general(a, b, (((1,), (0,)), ((), ())), preferred_element_type=F32)


def both_heads(q):
    lane = lax.broadcasted_iota(I32, q.shape, 1)
    zero = jnp.zeros_like(q)
    return jnp.concatenate([jnp.where(lane < HD, q, zero), jnp.where(lane < HD, zero, q)], axis=0)


def by_head(stacked):
    rows = stacked.shape[0] // 2
    lane = lax.broadcasted_iota(I32, (rows, LANES), 1)
    first = jnp.broadcast_to(stacked[:rows], (rows, LANES))
    second = jnp.broadcast_to(stacked[rows:], (rows, LANES))
    return jnp.where(lane < HD, first, second)


DST_B, DST_L, POS, LENS, USED, ROOT_LEN, PLACE, TENANT, MEMBERS, VALID, COUNT, CHUNK_TENANT, TABLE = (
    0, 32, 64, 96, 100, 104, 112, 128, 160, 208, 256, 264, 288,
)


def table_kernel(coords, leaf_of, parent, place, length, root_len, out):
    my_z, my_x, my_y, blk = (coords[i] for i in range(4))
    reqs = leaf_of.shape[0]
    req_dev = reqs // N_BLK
    tenants = root_len.shape[0]
    seats = (reqs // CHUNK + tenants - 1) * CHUNK

    def slot_index(slot):
        owner = slot >> 1
        return (owner & (PEERS - 1)) * SLOTS + (((owner // PEERS) ^ my_z) << 1) + (slot & 1)

    for t in range(tenants):
        out[COUNT + t] = 0
        out[ROOT_LEN + t] = root_len[t]
    out[PLACE] = my_z
    out[PLACE + 1] = my_x
    out[PLACE + 2] = blk

    def first_pass(r, _):
        leaf = leaf_of[r]
        branch = parent[leaf]
        tenant = parent[branch]
        out[DST_B + r] = slot_index(place[branch])
        out[DST_L + r] = slot_index(place[leaf])
        rel = (r // req_dev) ^ blk
        out[POS + r] = ((rel & 1) * (N_BLK // 2) + (rel >> 1)) * req_dev + (r & (req_dev - 1))
        out[TENANT + r] = tenant
        out[COUNT + tenant] = out[COUNT + tenant] + 1
        return 0

    lax.fori_loop(0, reqs, first_pass, 0, unroll=4)

    def clear(i, _):
        out[MEMBERS + i] = 0
        out[VALID + i] = 0
        return 0

    lax.fori_loop(0, seats, clear, 0, unroll=4)
    end = 0
    for t in range(tenants):
        chunks = (out[COUNT + t] + CHUNK - 1) // CHUNK

        def name(c, _, t=t):
            out[CHUNK_TENANT + c] = t
            return 0

        lax.fori_loop(end, end + chunks, name, 0)
        out[COUNT + t] = end * CHUNK
        end = end + chunks
    out[USED] = end

    def second_pass(r, _):
        tenant = out[TENANT + r]
        seat = out[COUNT + tenant]
        out[COUNT + tenant] = seat + 1
        out[MEMBERS + seat] = out[POS + r]
        out[VALID + seat] = 1
        return 0

    lax.fori_loop(0, reqs, second_pass, 0, unroll=4)

    def node(n, _):
        slot = place[n]
        owner = slot >> 1

        @pl.when((owner & (PEERS - 1)) == my_x * NY + my_y)
        def _():
            out[LENS + (((owner // PEERS) ^ my_z) << 1) + (slot & 1)] = length[n]

        return 0

    lax.fori_loop(0, place.shape[0], node, 0, unroll=4)


def make_tables(coords, leaf_of, parent, place, length, root_len):
    smem = pl.BlockSpec(memory_space=pltpu.SMEM)
    return pl.pallas_call(
        table_kernel,
        out_shape=jax.ShapeDtypeStruct((TABLE,), I32),
        in_specs=[smem] * 6,
        out_specs=smem,
        cost_estimate=pl.CostEstimate(flops=1 << 20, bytes_accessed=1 << 12, transcendentals=0),
    )(coords, leaf_of, parent, place, length, root_len)


def query_kernel(tab, half_ref, near_ref, other_ref, w_ref, after_ref, q_ref, out_ref):
    del after_ref
    reqs, suf, cols = q_ref.shape
    out_ref[...] = jnp.zeros_like(out_ref)
    weights = w_ref[...]
    at = 0
    for ref in (half_ref, near_ref, other_ref):
        rows = ref[...].reshape(-1, ref.shape[-1])
        q = dot_nn(rows, weights).astype(BF16).astype(F32) * HD**-0.5
        count = rows.shape[0] // suf
        q_ref[at : at + count] = q.astype(BF16).reshape(count, suf, cols)
        at += count

    def body(r, _):
        tile = q_ref[tab[POS + r]]
        out_ref[tab[DST_B + r]] = tile
        out_ref[tab[DST_L + r]] = tile
        return 0

    lax.fori_loop(0, reqs, body, 0, unroll=2)


def query_and_route(tab, half, near, other, w, suf, after):
    reqs = (half.size + near.size + other.size) // (suf * half.shape[-1])
    vmem = pl.BlockSpec(memory_space=pltpu.VMEM)
    return pl.pallas_call(
        query_kernel,
        out_shape=(
            jax.ShapeDtypeStruct((reqs, suf, LANES), BF16),
            jax.ShapeDtypeStruct((PEERS * SLOTS, suf, LANES), BF16),
        ),
        in_specs=[pl.BlockSpec(memory_space=pltpu.SMEM)]
        + [vmem] * 4
        + [pl.BlockSpec(memory_space=pl.ANY)],
        out_specs=(vmem, vmem),
        compiler_params=pltpu.CompilerParams(vmem_limit_bytes=24 << 20),
        cost_estimate=pl.CostEstimate(flops=1 << 28, bytes_accessed=4 << 20, transcendentals=0),
    )(tab, half, near, other, w, after)


def pack_kernel(up_ref, down_ref, bias_ref, after_ref, out_ref):
    del after_ref
    width = up_ref.shape[0]
    units = out_ref.shape[2]
    for j in range(2):
        own = slice(j * units, (j + 1) * units)
        out_ref[j, :width] = up_ref[:, own]
        for i in range(width // units):
            out_ref[j, width + i * units : width + (i + 1) * units] = down_ref[
                own, i * units : (i + 1) * units
            ]
        bias = jnp.broadcast_to(bias_ref[:, own].astype(F32), (16, units))
        out_ref[j, 2 * width :] = bias.astype(BF16)


def pack_weights(up, down, bias, after):
    width, units = up.shape
    vmem = pl.BlockSpec(memory_space=pltpu.VMEM)
    return pl.pallas_call(
        pack_kernel,
        out_shape=jax.ShapeDtypeStruct((2, 2 * width + 16, units // 2), BF16),
        in_specs=[vmem] * 3 + [pl.BlockSpec(memory_space=pl.ANY)],
        out_specs=vmem,
        compiler_params=pltpu.CompilerParams(vmem_limit_bytes=16 << 20),
        cost_estimate=pl.CostEstimate(flops=0, bytes_accessed=4 << 20, transcendentals=0),
    )(up, down, bias.reshape(1, units), after)


def node_kernel(tab, q_ref, cache_ref, after_ref, out_ref):
    del after_ref
    peers, slots, suf, _ = q_ref.shape
    group = 4
    rows = group * suf
    node_max = cache_ref.shape[3]
    out_ref[:, 2 * SLOTS] = jnp.zeros((peers, HALF, LANES), BF16)

    def one_slot(slot, _):
        keys = both_heads(cache_ref[slot // 2, 0, slot % 2])
        values = cache_ref[slot // 2, 1, slot % 2]
        values = jnp.concatenate([both_heads(values), both_heads(jnp.ones_like(values))], axis=1)
        keep = lax.broadcasted_iota(I32, (1, node_max), 1) < tab[LENS + slot]
        lane = lax.broadcasted_iota(I32, (group, HALF, LANES), 2)
        piece = lane % (HD // 2) - 3 * slot
        for g in range(peers // group):
            part = slice(g * group, (g + 1) * group)
            q = q_ref[part, slot].reshape(rows, LANES)
            scores = dot_nt(q, keys)
            weights, peaks = [], []
            for h in range(2):
                own = jnp.where(keep, scores[:, h * node_max : (h + 1) * node_max], NEG)
                peak = jnp.max(own, axis=1, keepdims=True)
                weights.append(jnp.exp(own - peak).astype(BF16))
                peaks.append(peak)
            mixed = dot_nn(jnp.concatenate(weights, axis=1), values)
            total = mixed[:, LANES:]
            mass = by_head(jnp.concatenate(peaks, axis=0)) + jnp.log(total)
            out = (mixed[:, :LANES] / total).astype(BF16).reshape(group, 2, HALF, LANES)
            out_ref[part, 2 * slot] = out[:, 0]
            out_ref[part, 2 * slot + 1] = out[:, 1]
            mass = mass.reshape(group, 2, HALF, LANES)
            mass = jnp.where(lane % HD < HD // 2, mass[:, 0], mass[:, 1])
            high = mass.astype(BF16).astype(F32)
            rest = mass - high
            mid = rest.astype(BF16).astype(F32)
            sent = jnp.where(piece == 0, high, jnp.where(piece == 1, mid, rest - mid))
            held = out_ref[part, 2 * SLOTS].astype(F32)
            held = jnp.where((piece >= 0) & (piece < 3), sent, held)
            out_ref[part, 2 * SLOTS] = held.astype(BF16)
        return 0

    lax.fori_loop(0, slots, one_slot, 0)


def node_attention(tab, queries, caches, after):
    peers, slots, suf, _ = queries.shape
    vmem = pl.BlockSpec(memory_space=pltpu.VMEM)
    return pl.pallas_call(
        node_kernel,
        out_shape=jax.ShapeDtypeStruct((peers, 2 * slots + 1, HALF, LANES), BF16),
        in_specs=[
            pl.BlockSpec(memory_space=pltpu.SMEM),
            vmem,
            vmem,
            pl.BlockSpec(memory_space=pl.ANY),
        ],
        out_specs=vmem,
        compiler_params=pltpu.CompilerParams(vmem_limit_bytes=24 << 20),
        cost_estimate=pl.CostEstimate(
            flops=2 << 30, bytes_accessed=4 << 20, transcendentals=4 << 20
        ),
    )(tab, queries, caches, after)


def root_kernel(tab, q_ref, k_ref, v_ref, root_ref, out_ref, mass_ref):
    suf = q_ref.shape[1]
    rows = CHUNK * suf
    per = root_ref.shape[5]
    root_rows = NY * NZ * NX * per

    def body(c, _):
        tenant = tab[CHUNK_TENANT + c]
        where_ = [tab[MEMBERS + c * CHUNK + j] for j in range(CHUNK)]
        q = both_heads(jnp.concatenate([q_ref[w] for w in where_], axis=0))
        own_k = jnp.concatenate([k_ref[w] for w in where_], axis=0)
        own_v = jnp.concatenate([v_ref[w] for w in where_], axis=0)
        keys = root_ref[:, :, :, 0, tenant].reshape(root_rows, LANES)
        values = root_ref[:, :, :, 1, tenant].reshape(root_rows, LANES)
        n = lax.broadcasted_iota(I32, (1, root_rows), 1)
        row = n % per
        z = ((n // per) % NZ) ^ tab[PLACE]
        y = (n // (per * NZ)) % NY
        x = n // (per * NZ * NY)
        place = ((z * NX + x) * NY + y) * per + row
        scores = jnp.where(place < tab[ROOT_LEN + tenant], dot_nt(q, keys), NEG)
        own_row = (lax.broadcasted_iota(I32, (2 * rows, rows), 0) % rows) // suf
        own_col = lax.broadcasted_iota(I32, (2 * rows, rows), 1) // suf
        own = jnp.where(own_row == own_col, dot_nt(q, own_k), NEG)
        peak = jnp.maximum(
            jnp.max(scores, axis=1, keepdims=True), jnp.max(own, axis=1, keepdims=True)
        )
        weights = jnp.exp(scores - peak)
        own_weights = jnp.exp(own - peak)
        total = jnp.sum(weights, axis=1, keepdims=True) + jnp.sum(
            own_weights, axis=1, keepdims=True
        )
        mixed = dot_nn(weights.astype(BF16), values) + dot_nn(own_weights.astype(BF16), own_v)
        out = by_head(mixed) / by_head(total)
        mass = by_head(peak + jnp.log(total))
        for j in range(CHUNK):

            @pl.when(tab[VALID + c * CHUNK + j] > 0)
            def _(j=j):
                out_ref[where_[j]] = out[j * suf : (j + 1) * suf]
                mass_ref[where_[j]] = mass[j * suf : (j + 1) * suf]

        return 0

    lax.fori_loop(0, tab[USED], body, 0)


def root_attention(tab, q, k, v, roots):
    reqs, suf, _ = q.shape
    shape = jax.ShapeDtypeStruct((reqs, suf, LANES), F32)
    vmem = pl.BlockSpec(memory_space=pltpu.VMEM)
    return pl.pallas_call(
        root_kernel,
        out_shape=(shape, shape),
        in_specs=[pl.BlockSpec(memory_space=pltpu.SMEM)] + [vmem] * 4,
        out_specs=(vmem, vmem),
        compiler_params=pltpu.CompilerParams(vmem_limit_bytes=40 << 20),
        cost_estimate=pl.CostEstimate(
            flops=4 << 30, bytes_accessed=4 << 20, transcendentals=4 << 20
        ),
    )(tab, q, k, v, roots)


def merge_kernel(tab, back_ref, out_ref, mass_ref, send_ref, node_mass):
    reqs, suf, _ = out_ref.shape
    per_block = reqs // N_BLK
    src = lax.broadcasted_iota(I32, (LANES, LANES), 0)
    dst = lax.broadcasted_iota(I32, (LANES, LANES), 1)
    packed = back_ref[:, 2 * SLOTS].reshape(PEERS * HALF, LANES)
    for s in range(SLOTS):
        for g in range(2):
            hit = (src // HD == dst // HD) & ((src % HD) // (HD // 2) == g)
            hit = hit & ((src % (HD // 2)) // 3 == s)
            pick = jnp.where(hit, 1.0, 0.0).astype(BF16)
            node_mass[:, s, g] = dot_nn(packed, pick).reshape(PEERS, HALF, LANES)

    def body(r, _):
        here = tab[POS + r]
        outs = [out_ref[here]]
        masses = [mass_ref[here]]
        for first in (DST_B, DST_L):
            peer = tab[first + r] // SLOTS
            slot = tab[first + r] % SLOTS
            outs.append(back_ref[peer, pl.ds(2 * slot, 2)].astype(F32).reshape(suf, LANES))
            masses.append(node_mass[peer, slot].reshape(suf, LANES))
        top = jnp.maximum(jnp.maximum(masses[0], masses[1]), masses[2])
        parts = [jnp.exp(m - top) for m in masses]
        total = parts[0] + parts[1] + parts[2]
        attn = (parts[0] * outs[0] + parts[1] * outs[1] + parts[2] * outs[2]) / total
        attn = attn.astype(BF16)
        block = r // per_block
        send_ref[block, 0, r % per_block] = attn
        send_ref[(block + N_BLK // 2) % N_BLK, 1, r % per_block] = attn
        return 0

    lax.fori_loop(0, reqs, body, 0, unroll=2)


def merge(tab, back, out, mass):
    reqs, suf, _ = out.shape
    vmem = pl.BlockSpec(memory_space=pltpu.VMEM)
    return pl.pallas_call(
        merge_kernel,
        out_shape=jax.ShapeDtypeStruct((N_BLK, 2, reqs // N_BLK, suf, LANES), BF16),
        in_specs=[pl.BlockSpec(memory_space=pltpu.SMEM)] + [vmem] * 3,
        out_specs=vmem,
        scratch_shapes=[pltpu.VMEM((PEERS, SLOTS, 2, HALF, LANES), F32)],
        compiler_params=pltpu.CompilerParams(vmem_limit_bytes=16 << 20),
        cost_estimate=pl.CostEstimate(
            flops=1 << 27, bytes_accessed=4 << 20, transcendentals=1 << 20
        ),
    )(tab, back, out, mass)


def after_kernel(*refs):
    del refs


def after(arrays, value):
    keep = pl.BlockSpec(memory_space=pl.ANY)
    return list(
        pl.pallas_call(
            after_kernel,
            out_shape=tuple(jax.ShapeDtypeStruct(a.shape, a.dtype) for a in arrays),
            in_specs=[keep] * (len(arrays) + 1),
            out_specs=(keep,) * len(arrays),
            input_output_aliases={i: i for i in range(len(arrays))},
        )(*arrays, value)
    )


def rows_norm(values, gain, shift):
    center = values - jnp.mean(values, axis=1, keepdims=True)
    spread = jnp.mean(center * center, axis=1, keepdims=True)
    return center * lax.rsqrt(spread + EPS) * gain + shift


def feed_kernel(
    tab, attn_ref, half_ref, other_ref, tok_a, tok_b, vec_ref, w0, w1, w2, w3, w4, w5, norm_ref, own_ref, far_ref
):
    rows, width = tok_a.shape
    blk = tab[PLACE + 2]
    proj = jnp.zeros((2 * rows, width), F32)
    for core, ref in enumerate((half_ref, other_ref)):
        parts = [attn_ref[blk ^ (2 * k + core)] for k in range(N_BLK // 2)]
        proj = proj + dot_nn(jnp.concatenate(parts, axis=1), ref[...].reshape(-1, width))
    tok = jnp.concatenate([tok_a[...], tok_b[...]], axis=0).astype(F32)
    vec = vec_ref[...].astype(F32)
    mixed = tok + proj + vec[0:1]
    norm = rows_norm(mixed, vec[1:2], vec[2:3]).astype(BF16)
    norm_ref[...] = norm[:rows]
    total = jnp.zeros((2 * rows, width), F32)
    units = w0.shape[-1]
    for w in [ref.at[i] for ref in (w0, w1) for i in range(2)] + [w2, w3, w4, w5]:
        bias = w[width + units * (width // units) :].astype(F32)[0:1]
        inner = dot_nn(norm, w[:width]) + bias
        hidden = (0.5 * inner * (1.0 + lax.erf(inner * (0.5**0.5)))).astype(BF16)
        down = [
            dot_nn(hidden, w[width + i * units : width + (i + 1) * units])
            for i in range(width // units)
        ]
        total = total + jnp.concatenate(down, axis=1)
    own_ref[...] = total[:rows]
    far_ref[...] = total[rows:].astype(BF16)


def feed_forward(tab, attn, out_half, out_other, tok_a, tok_b, vectors, packs):
    rows, width = tok_a.shape
    vmem = pl.BlockSpec(memory_space=pltpu.VMEM)
    return pl.pallas_call(
        feed_kernel,
        out_shape=(
            jax.ShapeDtypeStruct((rows, width), BF16),
            jax.ShapeDtypeStruct((rows, width), F32),
            jax.ShapeDtypeStruct((rows, width), BF16),
        ),
        in_specs=[pl.BlockSpec(memory_space=pltpu.SMEM)] + [vmem] * (6 + len(packs)),
        out_specs=(vmem, vmem, vmem),
        compiler_params=pltpu.CompilerParams(vmem_limit_bytes=48 << 20),
        cost_estimate=pl.CostEstimate(
            flops=3 << 30, bytes_accessed=12 << 20, transcendentals=1 << 20
        ),
    )(tab, attn, out_half, out_other, tok_a, tok_b, vectors, *packs)


def on_device(
    tokens,
    w_qkv,
    w_out,
    b_out,
    gain1,
    shift1,
    w_up,
    b_up,
    w_down,
    b_down,
    gain2,
    shift2,
    root_cache,
    node_cache,
    root_len,
    node_len,
    node_parent,
    node_place,
    req_leaf,
):
    req_dev, suf, width = tokens.shape
    cols = w_qkv.shape[2]
    own_rows = req_dev * suf
    reqs = req_leaf.shape[0]
    node_max = node_cache.shape[2]
    tenants = root_cache.shape[1]
    root_per = root_cache.shape[2]
    blk = lax.axis_index("blk")
    owner = lax.axis_index("owner")
    my_z = owner // (NX * NY)
    my_x = (owner // NY) % NX
    my_y = owner % NY
    swap = xor_pairs(N_BLK, 1)
    n_own = N_BLK // 2

    def zero_after(value):
        flat = value.reshape(-1, value.shape[-1])
        return jnp.minimum(jnp.abs(flat[:1, :1]), 0)

    coords = jnp.stack([my_z, my_x, my_y, blk]).astype(I32)
    tab = make_tables(coords, req_leaf, node_parent, node_place, node_len, root_len)

    tok = tokens.reshape(own_rows, width)
    near = lax.ppermute(tok, "blk", swap)
    half = [lax.ppermute(tok, "blk", xor_pairs(N_BLK, 2 * k)) for k in range(1, n_own)]
    tok_far, last_come = half[1], half[2]

    n_owner = NX * NY * NZ
    roots = root_cache.reshape(-1, LANES)
    roots = jnp.stack([roots, lax.ppermute(roots, "owner", xor_pairs(n_owner, NX * NY))])
    groups = [[z * PEERS + p for p in range(PEERS)] for z in range(NZ)]
    roots = roots + jnp.minimum(jnp.abs(tab[:1]), 0).astype(BF16)
    for came in half + [near]:
        roots = roots + zero_after(came)
    roots = lax.all_gather(roots, "owner", axis=0, tiled=False, axis_index_groups=groups)
    other = lax.ppermute(jnp.stack(half), "blk", swap)
    half = jnp.stack([tok] + half)
    roots = roots.reshape(NX, NY, NZ, 2, tenants, root_per, LANES)

    node_rows = node_cache.reshape(-1, LANES) + zero_after(last_come)
    node_far = lax.ppermute(node_rows, "owner", xor_pairs(n_owner, NX * NY))
    caches = jnp.stack([node_rows, node_far]).reshape(NZ, 2, 2, node_max, LANES)

    packs = pack_weights(w_up, w_down, b_up, last_come)
    pack_side = lax.ppermute(packs, "blk", swap)

    q, outgoing = query_and_route(tab, half, near, other, w_qkv[:, 0], suf, last_come)
    outgoing = outgoing.reshape(PEERS, SLOTS, suf, cols)

    def project(which):
        w = w_qkv[:, which]
        out = jnp.concatenate(
            [
                jnp.dot(part.reshape(-1, width), w, preferred_element_type=F32)
                for part in (half, near, other)
            ]
        )
        return out.astype(BF16).reshape(reqs, suf, cols)

    incoming = lax.all_to_all(
        outgoing, "owner", split_axis=0, concat_axis=0, axis_index_groups=groups, tiled=True
    )
    k_new = project(1)
    v_new = project(2)
    order = jnp.arange(N_BLK, dtype=I32) ^ blk
    order = (order % 2) * n_own + order // 2
    new_caches = jnp.stack([k_new, v_new]).reshape(2, N_BLK, req_dev, suf, cols)
    new_caches = jnp.take(new_caches, order, axis=1).reshape(2, reqs, suf, cols)

    answers = node_attention(tab, incoming, caches, packs)
    z_chips = NZ * n_own

    def to_neighbour(step):
        pairs = []
        for dev in range(n_owner * N_BLK):
            b, own = dev // n_owner, dev % n_owner
            z = (own // PEERS * n_own + b // 2 + step) % z_chips
            pairs.append((dev, (z % n_own * 2 + b % 2) * n_owner + z // n_own * PEERS + own % PEERS))
        part = ((blk // 2 + step + n_own) % n_own) // (n_own // 2)
        sent = lax.dynamic_index_in_dim(packs, part, 0, keepdims=False) + zero_after(answers)
        return lax.ppermute(sent, ("blk", "owner"), pairs)

    pack_next = [to_neighbour(1), to_neighbour(-1)]
    w_out_sent = w_out + zero_after(answers.reshape(-1, LANES))
    out_half = [
        lax.ppermute(w_out_sent, "blk", xor_pairs(N_BLK, 2 * k)) for k in range(1, n_own)
    ]
    back = lax.all_to_all(
        answers, "owner", split_axis=0, concat_axis=0, axis_index_groups=groups, tiled=True
    )
    out, mass = root_attention(tab, q, k_new, v_new, roots)
    send = merge(tab, back, out, mass)
    out_half = jnp.stack([w_out] + out_half)
    out_other = lax.ppermute(out_half, "blk", swap)
    pack_next = after(pack_next, mass)
    pack_last = [lax.ppermute(part, "blk", swap) for part in pack_next]
    parts = [packs, pack_side] + pack_next + pack_last
    attn = lax.all_to_all(
        send.reshape(N_BLK, 2 * own_rows, cols), "blk", split_axis=0, concat_axis=0, tiled=True
    )
    vectors = jnp.stack([b_out, gain1, shift1])
    own_norm, down, down_far = feed_forward(tab, attn, out_half, out_other, tok, tok_far, vectors, parts)
    total = down + lax.ppermute(down_far, "blk", xor_pairs(N_BLK, N_BLK // 2)).astype(F32)
    result = layer_norm(
        own_norm.astype(F32) + total + b_down.astype(F32), gain2, shift2
    ).astype(BF16)
    return (result.reshape(req_dev, suf, width), new_caches)


def solution(mesh):
    in_specs = (
        P(("owner", "blk"), None, None),
        P(None, None, "blk"),
        P("blk", None),
        P(),
        P(),
        P(),
        P(None, "blk"),
        P("blk"),
        P("blk", None),
        P(),
        P(),
        P(),
        P(None, None, "owner", "blk"),
        P(None, "owner", None, "blk"),
        P(),
        P(),
        P(),
        P(),
        P("owner"),
    )
    out_specs = (P(("owner", "blk"), None, None), P(None, "owner", None, "blk"))
    return jax.shard_map(
        on_device, mesh=mesh, in_specs=in_specs, out_specs=out_specs, check_vma=False
    )
```

```python
import functools

import jax
import jax.numpy as jnp
from jax import lax
from jax.experimental import pallas as pl
from jax.experimental.pallas import tpu as pltpu
from jax.sharding import PartitionSpec as P

F32 = jnp.float32
BF16 = jnp.bfloat16
I32 = jnp.int32

HD = 64
LANES = 128
N_BLK = 8
NX, NY, NZ = 4, 8, 2
PEERS = NX * NY
SLOTS = 2 * NZ
HALF = 16
CHUNK = 4
NEG = -1e30
EPS = 1e-05


def layer_norm(values, gain, shift):
    center = values - jnp.mean(values, axis=-1, keepdims=True)
    spread = jnp.mean(center * center, axis=-1, keepdims=True)
    return center * lax.rsqrt(spread + EPS) * gain.astype(F32) + shift.astype(F32)


def xor_pairs(count, bits):
    return [(i, i ^ bits) for i in range(count)]


def dot_nt(a, b):
    return lax.dot_general(a, b, (((1,), (1,)), ((), ())), preferred_element_type=F32)


def dot_nn(a, b):
    return lax.dot_general(a, b, (((1,), (0,)), ((), ())), preferred_element_type=F32)


def both_heads(q):
    lane = lax.broadcasted_iota(I32, q.shape, 1)
    zero = jnp.zeros_like(q)
    return jnp.concatenate([jnp.where(lane < HD, q, zero), jnp.where(lane < HD, zero, q)], axis=0)


def by_head(stacked):
    rows = stacked.shape[0] // 2
    lane = lax.broadcasted_iota(I32, (rows, LANES), 1)
    first = jnp.broadcast_to(stacked[:rows], (rows, LANES))
    second = jnp.broadcast_to(stacked[rows:], (rows, LANES))
    return jnp.where(lane < HD, first, second)


DST_B, DST_L, POS, LENS, USED, ROOT_LEN, PLACE, TENANT, MEMBERS, VALID, COUNT, CHUNK_TENANT, TABLE = (
    0, 32, 64, 96, 100, 104, 112, 128, 160, 208, 256, 264, 288,
)


def table_kernel(coords, leaf_of, parent, place, length, root_len, out):
    my_z, my_x, my_y, blk = (coords[i] for i in range(4))
    reqs = leaf_of.shape[0]
    req_dev = reqs // N_BLK
    tenants = root_len.shape[0]
    seats = (reqs // CHUNK + tenants - 1) * CHUNK

    def slot_index(slot):
        owner = slot >> 1
        return (owner & (PEERS - 1)) * SLOTS + (((owner // PEERS) ^ my_z) << 1) + (slot & 1)

    for t in range(tenants):
        out[COUNT + t] = 0
        out[ROOT_LEN + t] = root_len[t]
    out[PLACE] = my_z
    out[PLACE + 1] = my_x
    out[PLACE + 2] = blk

    def first_pass(r, _):
        leaf = leaf_of[r]
        branch = parent[leaf]
        tenant = parent[branch]
        out[DST_B + r] = slot_index(place[branch])
        out[DST_L + r] = slot_index(place[leaf])
        rel = (r // req_dev) ^ blk
        out[POS + r] = ((rel & 1) * (N_BLK // 2) + (rel >> 1)) * req_dev + (r & (req_dev - 1))
        out[TENANT + r] = tenant
        out[COUNT + tenant] = out[COUNT + tenant] + 1
        return 0

    lax.fori_loop(0, reqs, first_pass, 0, unroll=4)

    def clear(i, _):
        out[MEMBERS + i] = 0
        out[VALID + i] = 0
        return 0

    lax.fori_loop(0, seats, clear, 0, unroll=4)
    end = 0
    for t in range(tenants):
        chunks = (out[COUNT + t] + CHUNK - 1) // CHUNK

        def name(c, _, t=t):
            out[CHUNK_TENANT + c] = t
            return 0

        lax.fori_loop(end, end + chunks, name, 0)
        out[COUNT + t] = end * CHUNK
        end = end + chunks
    out[USED] = end

    def second_pass(r, _):
        tenant = out[TENANT + r]
        seat = out[COUNT + tenant]
        out[COUNT + tenant] = seat + 1
        out[MEMBERS + seat] = out[POS + r]
        out[VALID + seat] = 1
        return 0

    lax.fori_loop(0, reqs, second_pass, 0, unroll=4)

    def node(n, _):
        slot = place[n]
        owner = slot >> 1

        @pl.when((owner & (PEERS - 1)) == my_x * NY + my_y)
        def _():
            out[LENS + (((owner // PEERS) ^ my_z) << 1) + (slot & 1)] = length[n]

        return 0

    lax.fori_loop(0, place.shape[0], node, 0, unroll=4)


def make_tables(coords, leaf_of, parent, place, length, root_len):
    smem = pl.BlockSpec(memory_space=pltpu.SMEM)
    return pl.pallas_call(
        table_kernel,
        out_shape=jax.ShapeDtypeStruct((TABLE,), I32),
        in_specs=[smem] * 6,
        out_specs=smem,
        cost_estimate=pl.CostEstimate(flops=1 << 20, bytes_accessed=1 << 12, transcendentals=0),
    )(coords, leaf_of, parent, place, length, root_len)


def query_kernel(tab, half_ref, near_ref, other_ref, w_ref, after_ref, q_ref, out_ref):
    del after_ref
    reqs, suf, cols = q_ref.shape
    out_ref[...] = jnp.zeros_like(out_ref)
    weights = w_ref[...]
    at = 0
    for ref in (half_ref, near_ref, other_ref):
        rows = ref[...].reshape(-1, ref.shape[-1])
        q = dot_nn(rows, weights).astype(BF16).astype(F32) * HD**-0.5
        count = rows.shape[0] // suf
        q_ref[at : at + count] = q.astype(BF16).reshape(count, suf, cols)
        at += count

    def body(r, _):
        tile = q_ref[tab[POS + r]]
        out_ref[tab[DST_B + r]] = tile
        out_ref[tab[DST_L + r]] = tile
        return 0

    lax.fori_loop(0, reqs, body, 0, unroll=2)


def query_and_route(tab, half, near, other, w, suf, after):
    reqs = (half.size + near.size + other.size) // (suf * half.shape[-1])
    vmem = pl.BlockSpec(memory_space=pltpu.VMEM)
    return pl.pallas_call(
        query_kernel,
        out_shape=(
            jax.ShapeDtypeStruct((reqs, suf, LANES), BF16),
            jax.ShapeDtypeStruct((PEERS * SLOTS, suf, LANES), BF16),
        ),
        in_specs=[pl.BlockSpec(memory_space=pltpu.SMEM)]
        + [vmem] * 4
        + [pl.BlockSpec(memory_space=pl.ANY)],
        out_specs=(vmem, vmem),
        compiler_params=pltpu.CompilerParams(vmem_limit_bytes=24 << 20),
        cost_estimate=pl.CostEstimate(flops=1 << 28, bytes_accessed=4 << 20, transcendentals=0),
    )(tab, half, near, other, w, after)


def pack_kernel(up_ref, down_ref, bias_ref, after_ref, out_ref):
    del after_ref
    width = up_ref.shape[0]
    units = out_ref.shape[2]
    for j in range(2):
        own = slice(j * units, (j + 1) * units)
        out_ref[j, :width] = up_ref[:, own]
        for i in range(width // units):
            out_ref[j, width + i * units : width + (i + 1) * units] = down_ref[
                own, i * units : (i + 1) * units
            ]
        bias = jnp.broadcast_to(bias_ref[:, own].astype(F32), (16, units))
        out_ref[j, 2 * width :] = bias.astype(BF16)


def pack_weights(up, down, bias, after):
    width, units = up.shape
    vmem = pl.BlockSpec(memory_space=pltpu.VMEM)
    return pl.pallas_call(
        pack_kernel,
        out_shape=jax.ShapeDtypeStruct((2, 2 * width + 16, units // 2), BF16),
        in_specs=[vmem] * 3 + [pl.BlockSpec(memory_space=pl.ANY)],
        out_specs=vmem,
        compiler_params=pltpu.CompilerParams(vmem_limit_bytes=16 << 20),
        cost_estimate=pl.CostEstimate(flops=0, bytes_accessed=4 << 20, transcendentals=0),
    )(up, down, bias.reshape(1, units), after)


def node_kernel(tab, q_ref, cache_ref, after_ref, out_ref):
    del after_ref
    peers, slots, suf, _ = q_ref.shape
    group = 4
    rows = group * suf
    node_max = cache_ref.shape[3]
    out_ref[:, 2 * SLOTS] = jnp.zeros((peers, HALF, LANES), BF16)

    def one_slot(slot, _):
        keys = both_heads(cache_ref[slot // 2, 0, slot % 2])
        values = cache_ref[slot // 2, 1, slot % 2]
        values = jnp.concatenate([both_heads(values), both_heads(jnp.ones_like(values))], axis=1)
        keep = lax.broadcasted_iota(I32, (1, node_max), 1) < tab[LENS + slot]
        lane = lax.broadcasted_iota(I32, (group, HALF, LANES), 2)
        piece = lane % (HD // 2) - 3 * slot
        for g in range(peers // group):
            part = slice(g * group, (g + 1) * group)
            q = q_ref[part, slot].reshape(rows, LANES)
            scores = dot_nt(q, keys)
            weights, peaks = [], []
            for h in range(2):
                own = jnp.where(keep, scores[:, h * node_max : (h + 1) * node_max], NEG)
                peak = jnp.max(own, axis=1, keepdims=True)
                weights.append(jnp.exp(own - peak).astype(BF16))
                peaks.append(peak)
            mixed = dot_nn(jnp.concatenate(weights, axis=1), values)
            total = mixed[:, LANES:]
            mass = by_head(jnp.concatenate(peaks, axis=0)) + jnp.log(total)
            out = (mixed[:, :LANES] / total).astype(BF16).reshape(group, 2, HALF, LANES)
            out_ref[part, 2 * slot] = out[:, 0]
            out_ref[part, 2 * slot + 1] = out[:, 1]
            mass = mass.reshape(group, 2, HALF, LANES)
            mass = jnp.where(lane % HD < HD // 2, mass[:, 0], mass[:, 1])
            high = mass.astype(BF16).astype(F32)
            rest = mass - high
            mid = rest.astype(BF16).astype(F32)
            sent = jnp.where(piece == 0, high, jnp.where(piece == 1, mid, rest - mid))
            held = out_ref[part, 2 * SLOTS].astype(F32)
            held = jnp.where((piece >= 0) & (piece < 3), sent, held)
            out_ref[part, 2 * SLOTS] = held.astype(BF16)
        return 0

    lax.fori_loop(0, slots, one_slot, 0)


def node_attention(tab, queries, caches, after):
    peers, slots, suf, _ = queries.shape
    vmem = pl.BlockSpec(memory_space=pltpu.VMEM)
    return pl.pallas_call(
        node_kernel,
        out_shape=jax.ShapeDtypeStruct((peers, 2 * slots + 1, HALF, LANES), BF16),
        in_specs=[
            pl.BlockSpec(memory_space=pltpu.SMEM),
            vmem,
            vmem,
            pl.BlockSpec(memory_space=pl.ANY),
        ],
        out_specs=vmem,
        compiler_params=pltpu.CompilerParams(vmem_limit_bytes=24 << 20),
        cost_estimate=pl.CostEstimate(
            flops=2 << 30, bytes_accessed=4 << 20, transcendentals=4 << 20
        ),
    )(tab, queries, caches, after)


def root_kernel(tab, q_ref, k_ref, v_ref, root_ref, out_ref, mass_ref):
    suf = q_ref.shape[1]
    rows = CHUNK * suf
    per = root_ref.shape[5]
    root_rows = NY * NZ * NX * per

    def body(c, _):
        tenant = tab[CHUNK_TENANT + c]
        where_ = [tab[MEMBERS + c * CHUNK + j] for j in range(CHUNK)]
        q = both_heads(jnp.concatenate([q_ref[w] for w in where_], axis=0))
        own_k = jnp.concatenate([k_ref[w] for w in where_], axis=0)
        own_v = jnp.concatenate([v_ref[w] for w in where_], axis=0)
        keys = root_ref[:, :, :, 0, tenant].reshape(root_rows, LANES)
        values = root_ref[:, :, :, 1, tenant].reshape(root_rows, LANES)
        n = lax.broadcasted_iota(I32, (1, root_rows), 1)
        row = n % per
        z = ((n // per) % NZ) ^ tab[PLACE]
        y = (n // (per * NZ)) % NY
        x = n // (per * NZ * NY)
        place = ((z * NX + x) * NY + y) * per + row
        scores = jnp.where(place < tab[ROOT_LEN + tenant], dot_nt(q, keys), NEG)
        own_row = (lax.broadcasted_iota(I32, (2 * rows, rows), 0) % rows) // suf
        own_col = lax.broadcasted_iota(I32, (2 * rows, rows), 1) // suf
        own = jnp.where(own_row == own_col, dot_nt(q, own_k), NEG)
        peak = jnp.maximum(
            jnp.max(scores, axis=1, keepdims=True), jnp.max(own, axis=1, keepdims=True)
        )
        weights = jnp.exp(scores - peak)
        own_weights = jnp.exp(own - peak)
        total = jnp.sum(weights, axis=1, keepdims=True) + jnp.sum(
            own_weights, axis=1, keepdims=True
        )
        mixed = dot_nn(weights.astype(BF16), values) + dot_nn(own_weights.astype(BF16), own_v)
        out = by_head(mixed) / by_head(total)
        mass = by_head(peak + jnp.log(total))
        for j in range(CHUNK):

            @pl.when(tab[VALID + c * CHUNK + j] > 0)
            def _(j=j):
                out_ref[where_[j]] = out[j * suf : (j + 1) * suf]
                mass_ref[where_[j]] = mass[j * suf : (j + 1) * suf]

        return 0

    lax.fori_loop(0, tab[USED], body, 0)


def root_attention(tab, q, k, v, roots):
    reqs, suf, _ = q.shape
    shape = jax.ShapeDtypeStruct((reqs, suf, LANES), F32)
    vmem = pl.BlockSpec(memory_space=pltpu.VMEM)
    return pl.pallas_call(
        root_kernel,
        out_shape=(shape, shape),
        in_specs=[pl.BlockSpec(memory_space=pltpu.SMEM)] + [vmem] * 4,
        out_specs=(vmem, vmem),
        compiler_params=pltpu.CompilerParams(vmem_limit_bytes=40 << 20),
        cost_estimate=pl.CostEstimate(
            flops=4 << 30, bytes_accessed=4 << 20, transcendentals=4 << 20
        ),
    )(tab, q, k, v, roots)


def merge_kernel(tab, back_ref, out_ref, mass_ref, send_ref, node_mass):
    reqs, suf, _ = out_ref.shape
    per_block = reqs // N_BLK
    src = lax.broadcasted_iota(I32, (LANES, LANES), 0)
    dst = lax.broadcasted_iota(I32, (LANES, LANES), 1)
    packed = back_ref[:, 2 * SLOTS].reshape(PEERS * HALF, LANES)
    for s in range(SLOTS):
        for g in range(2):
            hit = (src // HD == dst // HD) & ((src % HD) // (HD // 2) == g)
            hit = hit & ((src % (HD // 2)) // 3 == s)
            pick = jnp.where(hit, 1.0, 0.0).astype(BF16)
            node_mass[:, s, g] = dot_nn(packed, pick).reshape(PEERS, HALF, LANES)

    def body(r, _):
        here = tab[POS + r]
        outs = [out_ref[here]]
        masses = [mass_ref[here]]
        for first in (DST_B, DST_L):
            peer = tab[first + r] // SLOTS
            slot = tab[first + r] % SLOTS
            outs.append(back_ref[peer, pl.ds(2 * slot, 2)].astype(F32).reshape(suf, LANES))
            masses.append(node_mass[peer, slot].reshape(suf, LANES))
        top = jnp.maximum(jnp.maximum(masses[0], masses[1]), masses[2])
        parts = [jnp.exp(m - top) for m in masses]
        total = parts[0] + parts[1] + parts[2]
        attn = (parts[0] * outs[0] + parts[1] * outs[1] + parts[2] * outs[2]) / total
        attn = attn.astype(BF16)
        block = r // per_block
        send_ref[block, 0, r % per_block] = attn
        send_ref[(block + N_BLK // 2) % N_BLK, 1, r % per_block] = attn
        return 0

    lax.fori_loop(0, reqs, body, 0, unroll=2)


def merge(tab, back, out, mass):
    reqs, suf, _ = out.shape
    vmem = pl.BlockSpec(memory_space=pltpu.VMEM)
    return pl.pallas_call(
        merge_kernel,
        out_shape=jax.ShapeDtypeStruct((N_BLK, 2, reqs // N_BLK, suf, LANES), BF16),
        in_specs=[pl.BlockSpec(memory_space=pltpu.SMEM)] + [vmem] * 3,
        out_specs=vmem,
        scratch_shapes=[pltpu.VMEM((PEERS, SLOTS, 2, HALF, LANES), F32)],
        compiler_params=pltpu.CompilerParams(vmem_limit_bytes=16 << 20),
        cost_estimate=pl.CostEstimate(
            flops=1 << 27, bytes_accessed=4 << 20, transcendentals=1 << 20
        ),
    )(tab, back, out, mass)


def after_kernel(*refs):
    del refs


def after(arrays, value):
    keep = pl.BlockSpec(memory_space=pl.ANY)
    return list(
        pl.pallas_call(
            after_kernel,
            out_shape=tuple(jax.ShapeDtypeStruct(a.shape, a.dtype) for a in arrays),
            in_specs=[keep] * (len(arrays) + 1),
            out_specs=(keep,) * len(arrays),
            input_output_aliases={i: i for i in range(len(arrays))},
        )(*arrays, value)
    )


def rows_norm(values, gain, shift):
    center = values - jnp.mean(values, axis=1, keepdims=True)
    spread = jnp.mean(center * center, axis=1, keepdims=True)
    return center * lax.rsqrt(spread + EPS) * gain + shift


def feed_kernel(
    tab, attn_ref, half_ref, other_ref, tok_a, tok_b, vec_ref, w0, w1, w2, w3, w4, w5, norm_ref, own_ref, far_ref
):
    rows, width = tok_a.shape
    blk = tab[PLACE + 2]
    proj = jnp.zeros((2 * rows, width), F32)
    for core, ref in enumerate((half_ref, other_ref)):
        parts = [attn_ref[blk ^ (2 * k + core)] for k in range(N_BLK // 2)]
        proj = proj + dot_nn(jnp.concatenate(parts, axis=1), ref[...].reshape(-1, width))
    tok = jnp.concatenate([tok_a[...], tok_b[...]], axis=0).astype(F32)
    vec = vec_ref[...].astype(F32)
    mixed = tok + proj + vec[0:1]
    norm = rows_norm(mixed, vec[1:2], vec[2:3]).astype(BF16)
    norm_ref[...] = norm[:rows]
    total = jnp.zeros((2 * rows, width), F32)
    units = w0.shape[-1]
    for w in [ref.at[i] for ref in (w0, w1) for i in range(2)] + [w2, w3, w4, w5]:
        bias = w[width + units * (width // units) :].astype(F32)[0:1]
        inner = dot_nn(norm, w[:width]) + bias
        hidden = (0.5 * inner * (1.0 + lax.erf(inner * (0.5**0.5)))).astype(BF16)
        down = [
            dot_nn(hidden, w[width + i * units : width + (i + 1) * units])
            for i in range(width // units)
        ]
        total = total + jnp.concatenate(down, axis=1)
    own_ref[...] = total[:rows]
    far_ref[...] = total[rows:].astype(BF16)


def feed_forward(tab, attn, out_half, out_other, tok_a, tok_b, vectors, packs):
    rows, width = tok_a.shape
    vmem = pl.BlockSpec(memory_space=pltpu.VMEM)
    return pl.pallas_call(
        feed_kernel,
        out_shape=(
            jax.ShapeDtypeStruct((rows, width), BF16),
            jax.ShapeDtypeStruct((rows, width), F32),
            jax.ShapeDtypeStruct((rows, width), BF16),
        ),
        in_specs=[pl.BlockSpec(memory_space=pltpu.SMEM)] + [vmem] * (6 + len(packs)),
        out_specs=(vmem, vmem, vmem),
        compiler_params=pltpu.CompilerParams(vmem_limit_bytes=48 << 20),
        cost_estimate=pl.CostEstimate(
            flops=3 << 30, bytes_accessed=12 << 20, transcendentals=1 << 20
        ),
    )(tab, attn, out_half, out_other, tok_a, tok_b, vectors, *packs)


def on_device(
    tokens,
    w_qkv,
    w_out,
    b_out,
    gain1,
    shift1,
    w_up,
    b_up,
    w_down,
    b_down,
    gain2,
    shift2,
    root_cache,
    node_cache,
    root_len,
    node_len,
    node_parent,
    node_place,
    req_leaf,
):
    req_dev, suf, width = tokens.shape
    cols = w_qkv.shape[2]
    own_rows = req_dev * suf
    reqs = req_leaf.shape[0]
    node_max = node_cache.shape[2]
    tenants = root_cache.shape[1]
    root_per = root_cache.shape[2]
    blk = lax.axis_index("blk")
    owner = lax.axis_index("owner")
    my_z = owner // (NX * NY)
    my_x = (owner // NY) % NX
    my_y = owner % NY
    swap = xor_pairs(N_BLK, 1)
    n_own = N_BLK // 2

    def zero_after(value):
        flat = value.reshape(-1, value.shape[-1])
        return jnp.minimum(jnp.abs(flat[:1, :1]), 0)

    coords = jnp.stack([my_z, my_x, my_y, blk]).astype(I32)
    tab = make_tables(coords, req_leaf, node_parent, node_place, node_len, root_len)

    tok = tokens.reshape(own_rows, width)
    near = lax.ppermute(tok, "blk", swap)
    half = [lax.ppermute(tok, "blk", xor_pairs(N_BLK, 2 * k)) for k in range(1, n_own)]
    tok_far, last_come = half[1], half[2]

    n_owner = NX * NY * NZ
    roots = root_cache.reshape(-1, LANES)
    roots = jnp.stack([roots, lax.ppermute(roots, "owner", xor_pairs(n_owner, NX * NY))])
    groups = [[z * PEERS + p for p in range(PEERS)] for z in range(NZ)]
    roots = roots + jnp.minimum(jnp.abs(tab[:1]), 0).astype(BF16)
    for came in half + [near]:
        roots = roots + zero_after(came)
    planned = zero_after(roots)
    roots = lax.all_gather(roots, "owner", axis=0, tiled=False, axis_index_groups=groups)
    other = lax.ppermute(jnp.stack(half) + planned, "blk", swap)
    half = jnp.stack([tok] + half)
    roots = roots.reshape(NX, NY, NZ, 2, tenants, root_per, LANES)

    node_rows = node_cache.reshape(-1, LANES) + zero_after(last_come)
    node_far = lax.ppermute(node_rows, "owner", xor_pairs(n_owner, NX * NY))
    caches = jnp.stack([node_rows, node_far]).reshape(NZ, 2, 2, node_max, LANES)

    packs = pack_weights(w_up, w_down, b_up, last_come)
    pack_side = lax.ppermute(packs, "blk", swap)

    q, outgoing = query_and_route(tab, half, near, other, w_qkv[:, 0], suf, last_come)
    outgoing = outgoing.reshape(PEERS, SLOTS, suf, cols)

    def project(which):
        w = w_qkv[:, which]
        out = jnp.concatenate(
            [
                jnp.dot(part.reshape(-1, width), w, preferred_element_type=F32)
                for part in (half, near, other)
            ]
        )
        return out.astype(BF16).reshape(reqs, suf, cols)

    incoming = lax.all_to_all(
        outgoing, "owner", split_axis=0, concat_axis=0, axis_index_groups=groups, tiled=True
    )
    k_new = project(1)
    v_new = project(2)
    order = jnp.arange(N_BLK, dtype=I32) ^ blk
    order = (order % 2) * n_own + order // 2
    new_caches = jnp.stack([k_new, v_new]).reshape(2, N_BLK, req_dev, suf, cols)
    new_caches = jnp.take(new_caches, order, axis=1).reshape(2, reqs, suf, cols)

    answers = node_attention(tab, incoming, caches, packs)
    z_chips = NZ * n_own

    def to_neighbour(step):
        pairs = []
        for dev in range(n_owner * N_BLK):
            b, own = dev // n_owner, dev % n_owner
            z = (own // PEERS * n_own + b // 2 + step) % z_chips
            pairs.append((dev, (z % n_own * 2 + b % 2) * n_owner + z // n_own * PEERS + own % PEERS))
        part = ((blk // 2 + step + n_own) % n_own) // (n_own // 2)
        sent = lax.dynamic_index_in_dim(packs, part, 0, keepdims=False) + zero_after(answers)
        return lax.ppermute(sent, ("blk", "owner"), pairs)

    pack_next = [to_neighbour(1), to_neighbour(-1)]
    w_out_sent = w_out + zero_after(answers.reshape(-1, LANES))
    out_half = [
        lax.ppermute(w_out_sent, "blk", xor_pairs(N_BLK, 2 * k)) for k in range(1, n_own)
    ]
    back = lax.all_to_all(
        answers, "owner", split_axis=0, concat_axis=0, axis_index_groups=groups, tiled=True
    )
    out, mass = root_attention(tab, q, k_new, v_new, roots)
    send = merge(tab, back, out, mass)
    out_half = jnp.stack([w_out] + out_half)
    out_other = lax.ppermute(out_half, "blk", swap)
    pack_next = after(pack_next, mass)
    pack_last = [lax.ppermute(part, "blk", swap) for part in pack_next]
    parts = [packs, pack_side] + pack_next + pack_last
    attn = lax.all_to_all(
        send.reshape(N_BLK, 2 * own_rows, cols), "blk", split_axis=0, concat_axis=0, tiled=True
    )
    vectors = jnp.stack([b_out, gain1, shift1])
    own_norm, down, down_far = feed_forward(tab, attn, out_half, out_other, tok, tok_far, vectors, parts)
    total = down + lax.ppermute(down_far, "blk", xor_pairs(N_BLK, N_BLK // 2)).astype(F32)
    result = layer_norm(
        own_norm.astype(F32) + total + b_down.astype(F32), gain2, shift2
    ).astype(BF16)
    return (result.reshape(req_dev, suf, width), new_caches)


def solution(mesh):
    in_specs = (
        P(("owner", "blk"), None, None),
        P(None, None, "blk"),
        P("blk", None),
        P(),
        P(),
        P(),
        P(None, "blk"),
        P("blk"),
        P("blk", None),
        P(),
        P(),
        P(),
        P(None, None, "owner", "blk"),
        P(None, "owner", None, "blk"),
        P(),
        P(),
        P(),
        P(),
        P("owner"),
    )
    out_specs = (P(("owner", "blk"), None, None), P(None, "owner", None, "blk"))
    return jax.shard_map(
        on_device, mesh=mesh, in_specs=in_specs, out_specs=out_specs, check_vma=False
    )
```
